32 devices in a mesh: img: 2 (over core), ch: 16 (over z, y, x).
Axes of the slice: x: 2, y: 2, z: 4, core: 2. Of those that a mesh axis runs over, the one named last changes fastest.
Arguments:
- features: bfloat16 [384, 16384], P('ch', 'img'), may hold values from -6 to 6
- cotangent: bfloat16 [384, 16384], P('ch', 'img'), may hold values from -6 to 6
- heights: int32 [16], P('img'), may hold values from 16 to 32, as said below
- widths: int32 [16], P('img'), may hold values from 16 to 32, as said below
- step_height: float32 [384], P('ch'), may hold values from -3 to 0
- rate_height: float32 [384, 64], P('ch'), may hold values from 0.05 to 2
- readout_height: float32 [384, 64], P('ch'), may hold values from -0.125 to 0.125
- step_width: float32 [384], P('ch'), may hold values from -3 to 0
- rate_width: float32 [384, 64], P('ch'), may hold values from 0.05 to 2
- readout_width: float32 [384, 64], P('ch'), may hold values from -0.125 to 0.125
- skip_gain: float32 [384], P('ch'), may hold values from -4 to 4
- norm_gain: bfloat16 [384], P('ch'), may hold values from 0.5 to 1.5
- norm_shift: bfloat16 [384], P('ch'), may hold values from -3 to 3
- in_weight: bfloat16 [384, 1536], P(None, 'ch'), may hold values from -0.3125 to 0.3125
- in_bias: bfloat16 [1536], P('ch'), may hold values from -3 to 3
- out_weight: bfloat16 [1536, 384], P('ch'), may hold values from -0.15625 to 0.15625
- out_bias: float32 [384], P('ch'), may hold values from -3 to 3
- layer_scale: float32 [384], P('ch'), may hold values from 0.3 to 3
Outputs:
- result: bfloat16 [384, 16384], P('ch', 'img')
- grad_features: float32 [384, 16384], P('ch', 'img')
- grad_step_height: float32 [384], P('ch')
- grad_rate_height: float32 [384, 64], P('ch')
- grad_readout_height: float32 [384, 64], P('ch')
- grad_step_width: float32 [384], P('ch')
- grad_rate_width: float32 [384, 64], P('ch')
- grad_readout_width: float32 [384, 64], P('ch')
- grad_skip_gain: float32 [384], P('ch')
- grad_norm_gain: float32 [384], P('ch')
- grad_norm_shift: float32 [384], P('ch')
- grad_in_weight: float32 [384, 1536], P(None, 'ch')
- grad_in_bias: float32 [1536], P('ch')
- grad_out_weight: float32 [1536, 384], P('ch')
- grad_out_bias: float32 [384], P('ch')
- grad_layer_scale: float32 [384], P('ch')
The draws below stay inside these ranges and needn't reach their ends.
Inputs may be any that keep to these rules, and one draw needn't show every extreme that they name: `heights`: every image is 16 to 32 cells high; in every draw some image is exactly 32 high and some image is less. `widths`: every image is 16 to 32 cells wide; in every draw some image is exactly 32 wide and some image is less.
All inputs are finite; a program needn't handle non-finite values.
Results may differ from the reference program's by a relative error of at most 0.009.
Values may be sent and summed in bfloat16 or wider, within the bound.
No kernel may reach another device: no remote copies, remote signals or barrier semaphores. Data moves between devices by JAX's collectives and lax.ppermute only.
A program may use at most 128 MiB of HBM per device.

```python
import math
from functools import partial
import jax
import jax.numpy as jnp
from jax import lax

C = 384
FF = 1536
NSTATE = 64
SIDE = 32
IMAGES = 16
PIXELS = 16384


def side_draw(key, salt):
    base = jax.random.randint(jax.random.fold_in(key, salt), (IMAGES,), SIDE // 2, SIDE + 1, dtype=jnp.int32)
    lesser = jax.random.randint(jax.random.fold_in(key, salt + 13), (), SIDE // 2, SIDE, dtype=jnp.int32)
    chosen = jax.random.randint(jax.random.fold_in(key, salt + 7), (), 0, IMAGES, dtype=jnp.int32)
    following = (chosen + 1) % IMAGES
    places = jnp.arange(IMAGES, dtype=jnp.int32)
    sides = jnp.where(places == following, lesser, base)
    return jnp.where(places == chosen, SIDE, sides).astype(jnp.int32)


def draw_heights(key, part):
    return side_draw(key, 1)


def draw_widths(key, part):
    return side_draw(key, 2)


def block_levels(key, dims, pieces, least, top_value):
    level = 1.0
    for position, blocks in pieces:
        steps = jax.random.uniform(jax.random.fold_in(jax.random.fold_in(key, 6), position), (blocks,), jnp.float32, least / len(pieces), top_value / len(pieces))
        level = level * jnp.repeat(jnp.exp(steps), dims[position] // blocks).reshape((-1,) + (1,) * (len(dims) - 1 - position))
    return level


def gaussian(rng, dims, scale, bound, cuts=(), kind=jnp.bfloat16):
    values = jax.random.normal(rng, dims, jnp.float32) * scale
    if len(cuts) > 0:
        values = block_levels(rng, dims, cuts, -0.22, 0.18) * values
    return jnp.clip(values, min=-bound, max=bound).astype(kind)


def setup_inputs(seed: int = 0) -> dict:
    streams_of = jax.random.split(jax.random.key(seed), 19)
    return {
        "features": gaussian(streams_of[0], (C, PIXELS), 1.0, 6.0, ((0, 16), (1, 2))),
        "cotangent": gaussian(streams_of[1], (C, PIXELS), 1.0, 6.0, ((0, 16), (1, 2))),
        "heights": draw_heights(jax.random.fold_in(streams_of[18], 71), 0),
        "widths": draw_widths(jax.random.fold_in(streams_of[18], 71), 0),
        "step_height": jnp.clip(-3.0 + 3.0 * jax.random.uniform(streams_of[4], (C,), jnp.float32) ** block_levels(streams_of[4], (C,), ((0, 16),), -0.2, 0.2), -3.0, 0.0),
        "rate_height": jnp.clip(jnp.exp(math.log(2.0) - 3.6888794 * jax.random.uniform(streams_of[5], (C, NSTATE), jnp.float32) ** block_levels(streams_of[5], (C, NSTATE), ((0, 16),), -0.2, 0.2)), 0.05, 2.0),
        "readout_height": gaussian(streams_of[6], (C, NSTATE), (NSTATE * SIDE) ** -0.5, 0.125, ((0, 16),), jnp.float32),
        "step_width": jnp.clip(-3.0 + 3.0 * jax.random.uniform(streams_of[7], (C,), jnp.float32) ** block_levels(streams_of[7], (C,), ((0, 16),), -0.2, 0.2), -3.0, 0.0),
        "rate_width": jnp.clip(jnp.exp(math.log(2.0) - 3.6888794 * jax.random.uniform(streams_of[8], (C, NSTATE), jnp.float32) ** block_levels(streams_of[8], (C, NSTATE), ((0, 16),), -0.2, 0.2)), 0.05, 2.0),
        "readout_width": gaussian(streams_of[9], (C, NSTATE), (NSTATE * SIDE) ** -0.5, 0.125, ((0, 16),), jnp.float32),
        "skip_gain": gaussian(streams_of[10], (C,), 1.0, 4.0, ((0, 16),), jnp.float32),
        "norm_gain": jnp.clip(1.0 + 0.1 * jax.random.normal(streams_of[11], (C,), jnp.float32), 0.5, 1.5).astype(jnp.bfloat16),
        "norm_shift": gaussian(streams_of[12], (C,), 0.5, 3.0, ((0, 16),)),
        "in_weight": gaussian(streams_of[13], (C, FF), C ** -0.5, 0.3125, ((1, 16),)),
        "in_bias": gaussian(streams_of[14], (FF,), 0.5, 3.0, ((0, 16),)),
        "out_weight": gaussian(streams_of[15], (FF, C), FF ** -0.5, 0.15625, ((0, 16),)),
        "out_bias": gaussian(streams_of[16], (C,), 0.5, 3.0, ((0, 16),), jnp.float32),
        "layer_scale": jnp.clip(jnp.exp(math.log(3.0) - 2.3025851 * jax.random.uniform(streams_of[17], (C,), jnp.float32) ** block_levels(streams_of[17], (C,), ((0, 16),), -0.2, 0.2)), 0.3, 3.0),
    }


EPS = 1e-06
HIGH = lax.Precision.HIGHEST

@jax.custom_vjp
def low(v):
    return lax.optimization_barrier(v.astype(jnp.bfloat16)).astype(jnp.float32)

@jax.custom_vjp
def low_back(v):
    return v

def low_keep(v):
    return (low(v), None)

def low_pass(kept, grad):
    return (grad,)

def back_keep(v):
    return (v, None)

def back_low(kept, grad):
    return (low(grad),)
low.defvjp(low_keep, low_pass)
low_back.defvjp(back_keep, back_low)

def slot_mask(heights, widths):
    places = jnp.arange(SIDE, dtype=jnp.int32)
    inside = (places[None, :, None] < heights[:, None, None]) & (places[None, None, :] < widths[:, None, None])
    return inside.reshape(-1).astype(jnp.float32)

def kernel_rows(step_log, rates, readout):
    places = jnp.arange(SIDE, dtype=jnp.float32)
    decays = jnp.exp(step_log)[:, None] * rates
    return jnp.einsum('cn,cnl->cl', readout, jnp.exp(-decays[:, :, None] * places), precision=HIGH)

def toeplitz(kernel):
    lagged = jnp.arange(SIDE, dtype=jnp.int32)
    select = (lagged[:, None, None] == lagged[None, :, None] - lagged[None, None, :]).astype(jnp.float32)
    return jnp.einsum('cl,lab->cab', kernel, select, precision=HIGH)

def mixer(inside, values, step_height, rate_height, readout_height, step_width, rate_width, readout_width, skip_gain):
    channels = values.shape[0]
    masked = values * inside[None, :]
    image_grid = masked.reshape(channels, -1, SIDE, SIDE)
    down_matrix = toeplitz(kernel_rows(step_height, rate_height, readout_height))
    across_matrix = toeplitz(kernel_rows(step_width, rate_width, readout_width))
    spread = jnp.einsum('cah,cihw->ciaw', down_matrix, image_grid, precision=HIGH)
    spread = jnp.einsum('ciaw,cbw->ciab', spread, across_matrix, precision=HIGH)
    return inside[None, :] * (spread.reshape(channels, -1) + skip_gain[:, None] * masked)

def normed(values, gain, shift):
    centred = values - lax.optimization_barrier(jnp.mean(values, axis=0))
    variance = lax.optimization_barrier(jnp.mean(centred * centred, axis=0))
    return centred * lax.rsqrt(variance + EPS) * gain[:, None] + shift[:, None]

def block(inside, values, step_height, rate_height, readout_height, step_width, rate_width, readout_width, skip_gain, norm_gain, norm_shift, in_weight, in_bias, out_weight, out_bias, layer_scale):
    mixed = low(mixer(inside, values, step_height, rate_height, readout_height, step_width, rate_width, readout_width, skip_gain))
    active = low(normed(mixed, norm_gain, norm_shift))
    before = low_back(jnp.dot(in_weight.T, active, precision=HIGH) + in_bias[:, None])
    hidden = low(jax.nn.gelu(before))
    summed = low_back(jnp.dot(out_weight.T, hidden, precision=HIGH))
    return values + inside[None, :] * layer_scale[:, None] * (summed + out_bias[:, None])

def reference(features, cotangent, heights, widths, step_height, rate_height, readout_height, step_width, rate_width, readout_width, skip_gain, norm_gain, norm_shift, in_weight, in_bias, out_weight, out_bias, layer_scale):
    inside = slot_mask(heights, widths)
    floats = [item.astype(jnp.float32) for item in (features, step_height, rate_height, readout_height, step_width, rate_width, readout_width, skip_gain, norm_gain, norm_shift, in_weight, in_bias, out_weight, out_bias, layer_scale)]
    output, pull = jax.vjp(partial(block, inside), *floats)
    grads = pull(cotangent.astype(jnp.float32))
    return (output.astype(jnp.bfloat16), grads[0], grads[1], grads[2], grads[3], grads[4], grads[5], grads[6], grads[7], grads[8], grads[9], grads[10], grads[11], grads[12], grads[13], grads[14])
```

```python
import math
from functools import partial

import jax
import jax.numpy as jnp
from jax import lax
from jax.experimental import pallas as pl
from jax.experimental.pallas import tpu as pltpu
from jax.sharding import PartitionSpec as P

SIDE = 32
CELLS = SIDE * SIDE
LANES = 128
PER = LANES // SIDE
TILES = CELLS // LANES
EPS = 1e-06
F32 = jnp.float32
BF16 = jnp.bfloat16
VMEM_LIMIT = 56 * 1024 * 1024


def column(row):
    n = row.shape[1]
    eye = lax.broadcasted_iota(jnp.int32, (n, n), 0) == lax.broadcasted_iota(jnp.int32, (n, n), 1)
    return jnp.sum(jnp.where(eye, jnp.broadcast_to(row, (n, n)), 0.0), axis=1, keepdims=True)


def as_row(col):
    n = col.shape[0]
    eye = lax.broadcasted_iota(jnp.int32, (n, n), 0) == lax.broadcasted_iota(jnp.int32, (n, n), 1)
    return jnp.sum(jnp.where(eye, jnp.broadcast_to(col, (n, n)), 0.0), axis=0, keepdims=True)


def image_mask(rows, height, width):
    cell = lax.broadcasted_iota(jnp.int32, (rows, CELLS), 1)
    return (cell // SIDE < height) & (cell % SIDE < width)


def lane_of(rows):
    return lax.broadcasted_iota(jnp.int32, (rows, LANES), 1)


def later(tiles, lane):
    out = [tiles]
    for step in range(1, PER):
        turned = [pltpu.roll(t, SIDE * step, 1) for t in tiles]
        out.append(
            [
                jnp.where(lane < SIDE * step, turned[k - 1] if k else 0.0, turned[k])
                for k in range(TILES)
            ]
        )
    return out


def sooner(tiles, lane):
    out = [tiles]
    for step in range(1, PER):
        turned = [pltpu.roll(t, LANES - SIDE * step, 1) for t in tiles]
        out.append(
            [
                jnp.where(
                    lane >= LANES - SIDE * step, turned[k + 1] if k < TILES - 1 else 0.0, turned[k]
                )
                for k in range(TILES)
            ]
        )
    return out


def vertical(tiles_at, taps, rows):
    out = [None] * TILES
    for lag in range(SIDE):
        tap = taps[lag, rows, :]
        for k in range(lag // PER, TILES):
            term = tap * tiles_at[lag % PER][k - lag // PER]
            out[k] = term if out[k] is None else out[k] + term
    return out


def group_of(channels):
    return 8 if channels % 8 == 0 else channels


def down_kernel(heights, widths, cot_ref, scale_ref, out_ref):
    image = pl.program_id(0)
    channels = cot_ref.shape[0]
    inside = image_mask(channels, heights[image], widths[image])
    value = jnp.where(inside, cot_ref[...].astype(F32), 0.0) * column(scale_ref[...])
    wide = out_ref.shape[2]
    for j in range(out_ref.shape[0]):
        out_ref[j] = value[:, j * wide : (j + 1) * wide].astype(BF16)


def forward_kernel(
    heights, widths, feat_ref, step_h, step_w, rate_h, rate_w, read_h, read_w, skip_ref,
    out_ref, rows_ref, taps_v, taps_h, held, done,
):
    image = pl.program_id(0)
    channels = feat_ref.shape[0]
    size = group_of(channels)

    @pl.when(image == 0)
    def _():
        lane = lane_of(channels)
        kept = jnp.zeros((channels, LANES), F32)
        decay_h = jnp.exp(column(step_h[...])) * rate_h[...]
        decay_w = jnp.exp(column(step_w[...])) * rate_w[...]
        for lag in range(SIDE):
            tap = jnp.sum(read_h[...] * jnp.exp(-decay_h * lag), axis=1, keepdims=True)
            tap = jnp.broadcast_to(tap, (channels, LANES))
            taps_v[lag] = tap
            kept = jnp.where(lane == lag, tap, kept)
            tap = jnp.sum(read_w[...] * jnp.exp(-decay_w * lag), axis=1, keepdims=True)
            tap = jnp.broadcast_to(tap, (channels, LANES))
            taps_h[lag] = jnp.where(lane % SIDE >= lag, tap, 0.0)
            kept = jnp.where(lane == SIDE + lag, tap, kept)
        kept = jnp.where(lane == 2 * SIDE, column(skip_ref[...]), kept)
        rows_ref[...] = kept

    inside = image_mask(channels, heights[image], widths[image])
    held[...] = jnp.where(inside, feat_ref[...].astype(F32), 0.0)

    def body(group, carry):
        rows = pl.ds(pl.multiple_of(group * size, size), size)
        lane = lane_of(size)
        tiles = [held[rows, k * LANES : (k + 1) * LANES] for k in range(TILES)]
        tall = vertical(later(tiles, lane), taps_v, rows)
        skip = rows_ref[rows, 2 * SIDE : 2 * SIDE + 1]
        acc = [skip * t for t in tiles]
        for lag in range(SIDE):
            tap = taps_h[lag, rows, :]
            for k in range(TILES):
                acc[k] = acc[k] + tap * (pltpu.roll(tall[k], lag, 1) if lag else tall[k])
        for k in range(TILES):
            done[rows, k * LANES : (k + 1) * LANES] = acc[k]
        return carry

    lax.fori_loop(0, channels // size, body, 0)
    value = jnp.where(inside, done[...], 0.0)
    wide = out_ref.shape[2]
    for j in range(out_ref.shape[0]):
        out_ref[j] = value[:, j * wide : (j + 1) * wide].astype(BF16)


def backward_kernel(
    heights, widths, feat_ref, cot_ref, mgrad_ref, summed_ref, rows_in, scale_ref, bias_ref,
    result_ref, gfeat_ref, small_ref, taps_v, taps_h, sums_v, sums_h, held, back, turn,
):
    image = pl.program_id(0)
    last = pl.num_programs(0) - 1
    channels = feat_ref.shape[0]
    size = group_of(channels)

    @pl.when(image == 0)
    def _():
        lane = lane_of(channels)
        for lag in range(SIDE):
            taps_v[lag] = jnp.broadcast_to(rows_in[:, lag : lag + 1], (channels, LANES))
            tap = jnp.broadcast_to(rows_in[:, SIDE + lag : SIDE + lag + 1], (channels, LANES))
            taps_h[lag] = jnp.where(lane % SIDE + lag < SIDE, tap, 0.0)
        sums_v[...] = jnp.zeros_like(sums_v)
        sums_h[...] = jnp.zeros_like(sums_h)
        small_ref[...] = jnp.zeros_like(small_ref)

    inside = image_mask(channels, heights[image], widths[image])
    values = feat_ref[...].astype(F32)
    masked = jnp.where(inside, values, 0.0)
    held[...] = masked
    wide = mgrad_ref.shape[2]
    parts = mgrad_ref.shape[0]
    grad = jnp.concatenate([mgrad_ref[j].astype(F32) for j in range(parts)], axis=1)
    grad = jnp.where(inside, grad, 0.0)
    back[...] = grad

    def body(group, carry):
        rows = pl.ds(pl.multiple_of(group * size, size), size)
        lane = lane_of(size)
        tiles = [held[rows, k * LANES : (k + 1) * LANES] for k in range(TILES)]
        tall = vertical(later(tiles, lane), taps_v, rows)
        flow = [back[rows, k * LANES : (k + 1) * LANES] for k in range(TILES)]
        wide_grad = [None] * TILES
        for lag in range(SIDE):
            tap = taps_h[lag, rows, :]
            total = None
            for k in range(TILES):
                moved = pltpu.roll(flow[k], LANES - lag, 1) if lag else flow[k]
                term = tap * moved
                wide_grad[k] = term if lag == 0 else wide_grad[k] + term
                term = moved * tall[k]
                total = term if total is None else total + term
            sums_h[lag, rows, :] += total
        moved_at = sooner(wide_grad, lane)
        skip = rows_in[rows, 2 * SIDE : 2 * SIDE + 1]
        out = [skip * flow[k] for k in range(TILES)]
        for lag in range(SIDE):
            tap = taps_v[lag, rows, :]
            high = lag // PER
            total = None
            for k in range(TILES - high):
                moved = moved_at[lag % PER][k + high]
                out[k] = out[k] + tap * moved
                term = moved * tiles[k]
                total = term if total is None else total + term
            sums_v[lag, rows, :] += total
        for k in range(TILES):
            turn[rows, k * LANES : (k + 1) * LANES] = out[k]
        return carry

    lax.fori_loop(0, channels // size, body, 0)
    cot = cot_ref[...].astype(F32)
    gfeat_ref[...] = cot + jnp.where(inside, turn[...], 0.0)

    shifted = jnp.concatenate([summed_ref[j].astype(F32) for j in range(parts)], axis=1)
    shifted = shifted + column(bias_ref[...])
    result = values + jnp.where(inside, column(scale_ref[...]) * shifted, 0.0)
    result_ref[...] = result.astype(BF16)
    weighted = jnp.where(inside, cot, 0.0)
    lane = lane_of(channels)
    add = jnp.where(lane == 64, jnp.sum(grad * masked, axis=1, keepdims=True), 0.0)
    add = jnp.where(lane == 65, jnp.sum(weighted * shifted, axis=1, keepdims=True), add)
    add = jnp.where(lane == 66, jnp.sum(weighted, axis=1, keepdims=True), add)
    small_ref[...] += add

    @pl.when(image == last)
    def _():
        total = small_ref[...]
        for lag in range(SIDE):
            part = jnp.sum(sums_v[lag], axis=1, keepdims=True)
            total = jnp.where(lane == lag, part, total)
            part = jnp.where(lane % SIDE + lag < SIDE, sums_h[lag], 0.0)
            part = jnp.sum(part, axis=1, keepdims=True)
            total = jnp.where(lane == SIDE + lag, part, total)
        small_ref[...] = total


def chain_kernel(
    own_ref, other_ref, step_h, step_w, rate_h, rate_w, read_h, read_w, scale_ref,
    gstep_h, grate_h, gread_h, gstep_w, grate_w, gread_w, gskip, gbias, gscale,
):
    total = own_ref[...] + other_ref[...]
    for first, step, rate, read, gstep, grate, gread in (
        (0, step_h, rate_h, read_h, gstep_h, grate_h, gread_h),
        (SIDE, step_w, rate_w, read_w, gstep_w, grate_w, gread_w),
    ):
        pace = jnp.exp(column(step[...]))
        decay = pace * rate[...]
        to_read = jnp.zeros_like(decay)
        to_decay = jnp.zeros_like(decay)
        for lag in range(SIDE):
            term = total[:, first + lag : first + lag + 1] * jnp.exp(-decay * lag)
            to_read = to_read + term
            if lag:
                to_decay = to_decay - float(lag) * term
        to_decay = to_decay * read[...]
        gread[...] = to_read
        grate[...] = pace * to_decay
        gstep[...] = as_row(jnp.sum(to_decay * decay, axis=1, keepdims=True))
    gskip[...] = as_row(total[:, 64:65])
    gscale[...] = as_row(total[:, 65:66])
    gbias[...] = as_row(total[:, 66:67]) * scale_ref[...]


def pack_kernel(half, in_ref, out_ref, bias_ref, gain_ref, shift_ref, pack_ref):
    copies, deep, wide = pack_ref.shape
    own, count = out_ref.shape
    channels = gain_ref.shape[1]
    keep = own // 2
    row = lax.broadcasted_iota(jnp.int32, (deep, own), 0)
    col = lax.broadcasted_iota(jnp.int32, (deep, own), 1)
    pick = jnp.where((col == row + half[0] * keep) & (row < keep), 1.0, 0.0).astype(BF16)
    nt = (((1,), (1,)), ((), ()))
    first = lax.dot_general(pick, in_ref[...], nt, preferred_element_type=F32)
    second = jnp.dot(pick, out_ref[...], preferred_element_type=F32)
    bias = jnp.broadcast_to(bias_ref[...], (LANES, own))
    third = lax.dot_general(pick, bias, nt, preferred_element_type=F32)
    row = lax.broadcasted_iota(jnp.int32, (deep, channels), 0)
    col = lax.broadcasted_iota(jnp.int32, (deep, channels), 1)
    pick = jnp.where(col == row, 1.0, 0.0).astype(BF16)
    gain = jnp.broadcast_to(gain_ref[...], (LANES, channels))
    gain = lax.dot_general(pick, gain, nt, preferred_element_type=F32)
    shift = jnp.broadcast_to(shift_ref[...], (LANES, channels))
    shift = lax.dot_general(pick, shift, nt, preferred_element_type=F32)
    lane = lane_of(deep)
    third = jnp.where(lane == 0, third, jnp.where(lane == 1, gain, jnp.where(lane == 2, shift, 0.0)))
    for j in range(copies):
        pack_ref[j, :, :count] = first.astype(BF16)
        pack_ref[j, :, count : 2 * count] = second.astype(BF16)
        pack_ref[j, :, 2 * count :] = third.astype(BF16)


ROOT = math.sqrt(2.0 / math.pi)


def mlp_kernel(
    mixed_ref, down_ref, gain_ref, shift_ref, own_ref, other_ref,
    summed_ref, mgrad_ref, gown_ref, gother_ref, gnorm_ref,
    active, mean_ref, inv_ref, sum_acc, grad_acc,
):
    step = pl.program_id(0)
    last = pl.num_programs(0) - 1
    count = mixed_ref.shape[0]
    block = own_ref.shape[0]

    @pl.when(step == 0)
    def _():
        value = mixed_ref[...].astype(F32)
        mean = jnp.mean(value, axis=0, keepdims=True)
        value = value - mean
        inv = lax.rsqrt(jnp.mean(value * value, axis=0, keepdims=True) + EPS)
        mean_ref[...] = mean
        inv_ref[...] = inv
        active[...] = (value * inv * gain_ref[...] + shift_ref[...]).astype(BF16)
        sum_acc[...] = jnp.zeros_like(sum_acc)
        grad_acc[...] = jnp.zeros_like(grad_acc)

    nt = (((1,), (1,)), ((), ()))
    tn = (((0,), (0,)), ((), ()))

    def process(ref):
        w_in = ref[:, :count]
        w_out = ref[:, count : 2 * count]
        act = active[...]
        down = down_ref[...]
        v = jnp.dot(w_in, act, preferred_element_type=F32)
        v = v + ref[:, 2 * count : 2 * count + 1].astype(F32)
        square = v * v
        bend = jnp.tanh(ROOT * v * (1.0 + 0.044715 * square))
        half = 0.5 * (1.0 + bend)
        hidden = (v * half).astype(BF16)
        slope = half + 0.5 * v * (1.0 - bend * bend) * (ROOT * (1.0 + 3.0 * 0.044715 * square))
        sum_acc[...] += lax.dot_general(w_out, hidden, tn, preferred_element_type=F32)
        hgrad = jnp.dot(w_out, down, preferred_element_type=F32)
        bgrad = hgrad * slope
        low = bgrad.astype(BF16)
        grad_acc[...] += lax.dot_general(w_in, low, tn, preferred_element_type=F32)
        g_in = lax.dot_general(low, act, nt, preferred_element_type=F32)
        g_out = lax.dot_general(hidden, down, nt, preferred_element_type=F32)
        g_bias = jnp.sum(low.astype(F32), axis=1, keepdims=True)
        return g_in, g_out, jnp.where(lane_of(block) == 0, g_bias, 0.0)

    g_in, g_out, g_ext = process(other_ref)
    gother_ref[:, :count] = g_in.astype(BF16)
    gother_ref[:, count : 2 * count] = g_out.astype(BF16)
    gother_ref[:, 2 * count :] = g_ext.astype(BF16)
    g_in, g_out, g_ext = process(own_ref)
    gown_ref[:, :count] = g_in
    gown_ref[:, count : 2 * count] = g_out
    gown_ref[:, 2 * count :] = g_ext

    @pl.when(step == last)
    def _():
        summed_ref[...] = sum_acc[...].astype(BF16)
        agrad = grad_acc[...]
        inv = inv_ref[...]
        normal = (mixed_ref[...].astype(F32) - mean_ref[...]) * inv
        scaled = agrad * gain_ref[...]
        first = jnp.mean(scaled, axis=0, keepdims=True)
        second = jnp.mean(scaled * normal, axis=0, keepdims=True)
        mgrad_ref[...] = ((scaled - first - normal * second) * inv).astype(BF16)
        lane = lane_of(count)
        ext = jnp.where(lane == 1, jnp.sum(agrad * normal, axis=1, keepdims=True), 0.0)
        gnorm_ref[...] = jnp.where(lane == 2, jnp.sum(agrad, axis=1, keepdims=True), ext)


def whole(shape):
    return pl.BlockSpec(shape, lambda i: (0,) * len(shape))


def params(**extra):
    return pltpu.CompilerParams(vmem_limit_bytes=VMEM_LIMIT, **extra)


SMEM = pl.BlockSpec(memory_space=pltpu.SMEM)


def per_device(
    ch, features, cotangent, heights, widths, step_height, rate_height, readout_height,
    step_width, rate_width, readout_width, skip_gain, norm_gain, norm_shift, in_weight,
    in_bias, out_weight, out_bias, layer_scale,
):
    channels, cells = features.shape
    count = in_weight.shape[0]
    units = in_weight.shape[1]
    states = rate_height.shape[1]
    images = cells // CELLS
    tokens = cells // ch
    parts = CELLS // tokens
    far = 4 if ch % 4 == 0 else 1
    near = ch // far
    deep = -(-(units // 2) // 16) * 16
    width = 2 * count + LANES
    near_groups = [[f * near + i for i in range(near)] for f in range(far)]
    far_groups = [[f * near + i for f in range(far)] for i in range(near)]
    row = lambda v: v.reshape(1, -1)
    exchange = lambda v: lax.ppermute(v, "img", [(0, 1), (1, 0)])
    swap = lambda v, groups=None: lax.all_to_all(
        v, "ch", split_axis=0, concat_axis=0, tiled=True, axis_index_groups=groups
    )
    half = lax.axis_index("img").astype(jnp.int32)

    full = pl.BlockSpec(memory_space=pltpu.VMEM)
    pack = pl.pallas_call(
        pack_kernel,
        out_shape=jax.ShapeDtypeStruct((far, deep, width), BF16),
        in_specs=[SMEM] + [full] * 5,
        out_specs=full,
        compiler_params=params(),
        name="pack",
    )(half.reshape(1), in_weight, out_weight, row(in_bias), row(norm_gain), row(norm_shift))
    pack = swap(pack, far_groups)
    pack = lax.all_gather(
        pack.reshape(far * deep, width), "ch", axis=0, tiled=True, axis_index_groups=near_groups
    )
    other = exchange(pack)
    vectors = pack.reshape(near, far, deep, width)[:, :, :channels, 2 * count + 1 : 2 * count + 3]
    vectors = vectors.transpose(1, 0, 2, 3).reshape(count, 2).astype(F32)

    cells_spec = pl.BlockSpec((channels, CELLS), lambda i: (0, i))
    token_spec = pl.BlockSpec((parts, channels, tokens), lambda i: (i, 0, 0))
    down = pl.pallas_call(
        down_kernel,
        grid=(images,),
        out_shape=jax.ShapeDtypeStruct((ch, channels, tokens), BF16),
        in_specs=[SMEM, SMEM, cells_spec, whole((1, channels))],
        out_specs=token_spec,
        compiler_params=params(),
        name="down",
    )(heights, widths, cotangent, row(layer_scale))
    down = swap(down).reshape(count, tokens)

    state = whole((channels, states))
    vector = whole((1, channels))
    tap = pltpu.VMEM((SIDE, channels, LANES), F32)
    plane = pltpu.VMEM((channels, CELLS), F32)
    mixed, taps = pl.pallas_call(
        forward_kernel,
        grid=(images,),
        out_shape=(
            jax.ShapeDtypeStruct((ch, channels, tokens), BF16),
            jax.ShapeDtypeStruct((channels, LANES), F32),
        ),
        in_specs=[SMEM, SMEM, cells_spec, vector, vector, state, state, state, state, vector],
        out_specs=(token_spec, whole((channels, LANES))),
        scratch_shapes=[tap, tap, plane, plane],
        compiler_params=params(),
        name="mixer_forward",
    )(
        heights, widths, features, row(step_height), row(step_width), rate_height, rate_width,
        readout_height, readout_width, row(skip_gain),
    )
    mixed = swap(mixed).reshape(count, tokens)

    rows = ch * deep
    blocks = 2
    span = rows // blocks
    token_full = whole((count, tokens))
    weight_spec = pl.BlockSpec((span, width), lambda i: (i, 0))
    summed, mgrad, gown, gother, gnorm = pl.pallas_call(
        mlp_kernel,
        grid=(blocks,),
        out_shape=(
            jax.ShapeDtypeStruct((count, tokens), BF16),
            jax.ShapeDtypeStruct((count, tokens), BF16),
            jax.ShapeDtypeStruct((rows, width), F32),
            jax.ShapeDtypeStruct((rows, width), BF16),
            jax.ShapeDtypeStruct((count, LANES), F32),
        ),
        in_specs=[token_full, token_full, whole((count, 1)), whole((count, 1)), weight_spec, weight_spec],
        out_specs=(token_full, token_full, weight_spec, weight_spec, whole((count, LANES))),
        scratch_shapes=[
            pltpu.VMEM((count, tokens), BF16),
            pltpu.VMEM((1, tokens), F32),
            pltpu.VMEM((1, tokens), F32),
            pltpu.VMEM((count, tokens), F32),
            pltpu.VMEM((count, tokens), F32),
        ],
        compiler_params=params(),
        name="mlp",
    )(mixed, down, vectors[:, 0:1], vectors[:, 1:2], pack, other)

    arrived = exchange(gother)
    mgrad = swap(mgrad.reshape(ch, channels, tokens))
    summed = swap(summed.reshape(ch, channels, tokens))

    gnorm = gnorm.reshape(far, near, channels, LANES).transpose(1, 0, 2, 3)
    gnorm = jnp.pad(gnorm, ((0, 0), (0, 0), (0, deep - channels), (2 * count, 0)))
    partial_sum = (gown + arrived.astype(F32)).reshape(near, far, deep, width) + gnorm
    partial_sum = swap(partial_sum.astype(BF16), near_groups)
    partial_sum = jnp.sum(partial_sum.astype(F32), axis=0)
    partial_sum = swap(partial_sum.astype(BF16), far_groups)
    partial_sum = jnp.sum(partial_sum.astype(F32), axis=0)
    sibling = exchange(partial_sum)
    keep = units // 2
    low = jnp.where(half == 0, partial_sum, sibling)[:keep]
    high = jnp.where(half == 0, sibling, partial_sum)[:keep]
    grads = jnp.concatenate([low, high], axis=0)
    grad_in_weight = grads[:, :count].T
    grad_out_weight = grads[:, count : 2 * count]
    grad_in_bias = grads[:, 2 * count]
    norms = (partial_sum + sibling)[:channels, 2 * count + 1 : 2 * count + 3]

    result, grad_features, small = pl.pallas_call(
        backward_kernel,
        grid=(images,),
        out_shape=(
            jax.ShapeDtypeStruct((channels, cells), BF16),
            jax.ShapeDtypeStruct((channels, cells), F32),
            jax.ShapeDtypeStruct((channels, LANES), F32),
        ),
        in_specs=[
            SMEM, SMEM, cells_spec, cells_spec, token_spec, token_spec, whole((channels, LANES)),
            vector, vector,
        ],
        out_specs=(cells_spec, cells_spec, whole((channels, LANES))),
        scratch_shapes=[tap, tap, tap, tap, plane, plane, plane],
        compiler_params=params(),
        name="mixer_backward",
    )(heights, widths, features, cotangent, mgrad, summed, taps, row(layer_scale), row(out_bias))

    vector_out = jax.ShapeDtypeStruct((1, channels), F32)
    state_out = jax.ShapeDtypeStruct((channels, states), F32)
    chained = pl.pallas_call(
        chain_kernel,
        out_shape=(
            vector_out, state_out, state_out, vector_out, state_out, state_out,
            vector_out, vector_out, vector_out,
        ),
        in_specs=[full] * 9,
        out_specs=(full,) * 9,
        compiler_params=params(),
        name="mixer_chain",
    )(
        small, exchange(small), row(step_height), row(step_width), rate_height, rate_width,
        readout_height, readout_width, row(layer_scale),
    )
    gstep_h, grate_h, gread_h, gstep_w, grate_w, gread_w, gskip, gbias, gscale = chained
    flat = lambda v: v.reshape(-1)
    return (
        result, grad_features, flat(gstep_h), grate_h, gread_h, flat(gstep_w), grate_w, gread_w,
        flat(gskip), norms[:, 0], norms[:, 1], grad_in_weight, grad_in_bias, grad_out_weight,
        flat(gbias), flat(gscale),
    )


def solution(mesh):
    wide, split, tall = P("ch", "img"), P("ch"), P("ch", None)
    return jax.shard_map(
        partial(per_device, mesh.shape["ch"]),
        mesh=mesh,
        in_specs=(
            wide, wide, P("img"), P("img"), split, tall, tall, split, tall, tall, split, split,
            split, P(None, "ch"), split, tall, split, split,
        ),
        out_specs=(
            wide, wide, split, tall, tall, split, tall, tall, split, split, split,
            P(None, "ch"), split, tall, split, split,
        ),
        check_vma=False,
    )
```

```python
import math
from functools import partial

import jax
import jax.numpy as jnp
from jax import lax
from jax.experimental import pallas as pl
from jax.experimental.pallas import tpu as pltpu
from jax.sharding import PartitionSpec as P

SIDE = 32
CELLS = SIDE * SIDE
LANES = 128
PER = LANES // SIDE
TILES = CELLS // LANES
EPS = 1e-06
F32 = jnp.float32
BF16 = jnp.bfloat16
VMEM_LIMIT = 56 * 1024 * 1024


def column(row):
    n = row.shape[1]
    eye = lax.broadcasted_iota(jnp.int32, (n, n), 0) == lax.broadcasted_iota(jnp.int32, (n, n), 1)
    return jnp.sum(jnp.where(eye, jnp.broadcast_to(row, (n, n)), 0.0), axis=1, keepdims=True)


def as_row(col):
    n = col.shape[0]
    eye = lax.broadcasted_iota(jnp.int32, (n, n), 0) == lax.broadcasted_iota(jnp.int32, (n, n), 1)
    return jnp.sum(jnp.where(eye, jnp.broadcast_to(col, (n, n)), 0.0), axis=0, keepdims=True)


def image_mask(rows, height, width):
    cell = lax.broadcasted_iota(jnp.int32, (rows, CELLS), 1)
    return (cell // SIDE < height) & (cell % SIDE < width)


def lane_of(rows):
    return lax.broadcasted_iota(jnp.int32, (rows, LANES), 1)


def later(tiles, lane):
    out = [tiles]
    for step in range(1, PER):
        turned = [pltpu.roll(t, SIDE * step, 1) for t in tiles]
        out.append(
            [
                jnp.where(lane < SIDE * step, turned[k - 1] if k else 0.0, turned[k])
                for k in range(TILES)
            ]
        )
    return out


def sooner(tiles, lane):
    out = [tiles]
    for step in range(1, PER):
        turned = [pltpu.roll(t, LANES - SIDE * step, 1) for t in tiles]
        out.append(
            [
                jnp.where(
                    lane >= LANES - SIDE * step, turned[k + 1] if k < TILES - 1 else 0.0, turned[k]
                )
                for k in range(TILES)
            ]
        )
    return out


def vertical(tiles_at, taps, rows):
    out = [None] * TILES
    for lag in range(SIDE):
        tap = taps[lag, rows, :]
        for k in range(lag // PER, TILES):
            term = tap * tiles_at[lag % PER][k - lag // PER]
            out[k] = term if out[k] is None else out[k] + term
    return out


def group_of(channels):
    return 8 if channels % 8 == 0 else channels


def down_kernel(heights, widths, cot_ref, scale_ref, out_ref):
    channels, cells = cot_ref.shape
    wide = out_ref.shape[2]
    parts = CELLS // wide
    scale = column(scale_ref[...])
    for image in range(cells // CELLS):
        inside = image_mask(1, heights[image], widths[image])
        value = cot_ref[:, image * CELLS : (image + 1) * CELLS].astype(F32)
        value = (value * jnp.where(inside, scale, 0.0)).astype(BF16)
        for j in range(parts):
            out_ref[image * parts + j] = value[:, j * wide : (j + 1) * wide]


def forward_kernel(
    heights, widths, feat_ref, step_h, step_w, rate_h, rate_w, read_h, read_w, skip_ref,
    out_ref, rows_ref, taps_v, taps_h, held, done,
):
    image = pl.program_id(0)
    channels = feat_ref.shape[0]
    size = group_of(channels)

    @pl.when(image == 0)
    def _():
        lane = lane_of(channels)
        kept = jnp.zeros((channels, LANES), F32)
        decay_h = jnp.exp(column(step_h[...])) * rate_h[...]
        decay_w = jnp.exp(column(step_w[...])) * rate_w[...]
        for lag in range(SIDE):
            tap = jnp.sum(read_h[...] * jnp.exp(-decay_h * lag), axis=1, keepdims=True)
            tap = jnp.broadcast_to(tap, (channels, LANES))
            taps_v[lag] = tap
            kept = jnp.where(lane == lag, tap, kept)
            tap = jnp.sum(read_w[...] * jnp.exp(-decay_w * lag), axis=1, keepdims=True)
            tap = jnp.broadcast_to(tap, (channels, LANES))
            taps_h[lag] = jnp.where(lane % SIDE >= lag, tap, 0.0)
            kept = jnp.where(lane == SIDE + lag, tap, kept)
        kept = jnp.where(lane == 2 * SIDE, column(skip_ref[...]), kept)
        rows_ref[...] = kept

    inside = image_mask(channels, heights[image], widths[image])
    held[...] = jnp.where(inside, feat_ref[...].astype(F32), 0.0)

    def body(group, carry):
        rows = pl.ds(pl.multiple_of(group * size, size), size)
        lane = lane_of(size)
        tiles = [held[rows, k * LANES : (k + 1) * LANES] for k in range(TILES)]
        tall = vertical(later(tiles, lane), taps_v, rows)
        skip = rows_ref[rows, 2 * SIDE : 2 * SIDE + 1]
        acc = [skip * t for t in tiles]
        for lag in range(SIDE):
            tap = taps_h[lag, rows, :]
            for k in range(TILES):
                acc[k] = acc[k] + tap * (pltpu.roll(tall[k], lag, 1) if lag else tall[k])
        for k in range(TILES):
            done[rows, k * LANES : (k + 1) * LANES] = acc[k]
        return carry

    lax.fori_loop(0, channels // size, body, 0)
    value = jnp.where(inside, done[...], 0.0)
    wide = out_ref.shape[2]
    for j in range(out_ref.shape[0]):
        out_ref[j] = value[:, j * wide : (j + 1) * wide].astype(BF16)


def backward_kernel(
    heights, widths, feat_ref, cot_ref, both_ref, rows_in, scale_ref, bias_ref,
    result_ref, gfeat_ref, small_ref, taps_v, taps_h, sums_v, sums_h, held, back, turn,
):
    image = pl.program_id(0)
    last = pl.num_programs(0) - 1
    channels = feat_ref.shape[0]
    size = group_of(channels)

    @pl.when(image == 0)
    def _():
        lane = lane_of(channels)
        for lag in range(SIDE):
            taps_v[lag] = jnp.broadcast_to(rows_in[:, lag : lag + 1], (channels, LANES))
            tap = jnp.broadcast_to(rows_in[:, SIDE + lag : SIDE + lag + 1], (channels, LANES))
            taps_h[lag] = jnp.where(lane % SIDE + lag < SIDE, tap, 0.0)
        sums_v[...] = jnp.zeros_like(sums_v)
        sums_h[...] = jnp.zeros_like(sums_h)
        small_ref[...] = jnp.zeros_like(small_ref)

    inside = image_mask(channels, heights[image], widths[image])
    values = feat_ref[...].astype(F32)
    masked = jnp.where(inside, values, 0.0)
    held[...] = masked
    parts = both_ref.shape[0]
    grad = jnp.concatenate([both_ref[j, 0].astype(F32) for j in range(parts)], axis=1)
    grad = jnp.where(inside, grad, 0.0)
    back[...] = grad

    def body(group, carry):
        rows = pl.ds(pl.multiple_of(group * size, size), size)
        lane = lane_of(size)
        tiles = [held[rows, k * LANES : (k + 1) * LANES] for k in range(TILES)]
        tall = vertical(later(tiles, lane), taps_v, rows)
        flow = [back[rows, k * LANES : (k + 1) * LANES] for k in range(TILES)]
        wide_grad = [None] * TILES
        for lag in range(SIDE):
            tap = taps_h[lag, rows, :]
            total = None
            for k in range(TILES):
                moved = pltpu.roll(flow[k], LANES - lag, 1) if lag else flow[k]
                term = tap * moved
                wide_grad[k] = term if lag == 0 else wide_grad[k] + term
                term = moved * tall[k]
                total = term if total is None else total + term
            sums_h[lag, rows, :] += total
        moved_at = sooner(wide_grad, lane)
        skip = rows_in[rows, 2 * SIDE : 2 * SIDE + 1]
        out = [skip * flow[k] for k in range(TILES)]
        for lag in range(SIDE):
            tap = taps_v[lag, rows, :]
            high = lag // PER
            total = None
            for k in range(TILES - high):
                moved = moved_at[lag % PER][k + high]
                out[k] = out[k] + tap * moved
                term = moved * tiles[k]
                total = term if total is None else total + term
            sums_v[lag, rows, :] += total
        for k in range(TILES):
            turn[rows, k * LANES : (k + 1) * LANES] = out[k]
        return carry

    lax.fori_loop(0, channels // size, body, 0)
    cot = cot_ref[...].astype(F32)
    gfeat_ref[...] = cot + jnp.where(inside, turn[...], 0.0)

    shifted = jnp.concatenate([both_ref[j, 1].astype(F32) for j in range(parts)], axis=1)
    shifted = shifted + column(bias_ref[...])
    result = values + jnp.where(inside, column(scale_ref[...]) * shifted, 0.0)
    result_ref[...] = result.astype(BF16)
    weighted = jnp.where(inside, cot, 0.0)
    lane = lane_of(channels)
    add = jnp.where(lane == 64, jnp.sum(grad * masked, axis=1, keepdims=True), 0.0)
    add = jnp.where(lane == 65, jnp.sum(weighted * shifted, axis=1, keepdims=True), add)
    add = jnp.where(lane == 66, jnp.sum(weighted, axis=1, keepdims=True), add)
    small_ref[...] += add

    @pl.when(image == last)
    def _():
        total = small_ref[...]
        for lag in range(SIDE):
            part = jnp.sum(sums_v[lag], axis=1, keepdims=True)
            total = jnp.where(lane == lag, part, total)
            part = jnp.where(lane % SIDE + lag < SIDE, sums_h[lag], 0.0)
            part = jnp.sum(part, axis=1, keepdims=True)
            total = jnp.where(lane == SIDE + lag, part, total)
        small_ref[...] = total


def chain_kernel(
    own_ref, other_ref, step_h, step_w, rate_h, rate_w, read_h, read_w, scale_ref,
    gstep_h, grate_h, gread_h, gstep_w, grate_w, gread_w, gskip, gbias, gscale,
):
    total = own_ref[...] + other_ref[...]
    for first, step, rate, read, gstep, grate, gread in (
        (0, step_h, rate_h, read_h, gstep_h, grate_h, gread_h),
        (SIDE, step_w, rate_w, read_w, gstep_w, grate_w, gread_w),
    ):
        pace = jnp.exp(column(step[...]))
        decay = pace * rate[...]
        to_read = jnp.zeros_like(decay)
        to_decay = jnp.zeros_like(decay)
        for lag in range(SIDE):
            term = total[:, first + lag : first + lag + 1] * jnp.exp(-decay * lag)
            to_read = to_read + term
            if lag:
                to_decay = to_decay - float(lag) * term
        to_decay = to_decay * read[...]
        gread[...] = to_read
        grate[...] = pace * to_decay
        gstep[...] = as_row(jnp.sum(to_decay * decay, axis=1, keepdims=True))
    gskip[...] = as_row(total[:, 64:65])
    gscale[...] = as_row(total[:, 65:66])
    gbias[...] = as_row(total[:, 66:67]) * scale_ref[...]


def pack_kernel(half, in_ref, out_ref, bias_ref, gain_ref, shift_ref, pack_ref):
    deep = pack_ref.shape[0]
    own, count = out_ref.shape
    channels = gain_ref.shape[1]
    keep = own // 2
    row = lax.broadcasted_iota(jnp.int32, (deep, own), 0)
    col = lax.broadcasted_iota(jnp.int32, (deep, own), 1)
    pick = jnp.where((col == row + half[0] * keep) & (row < keep), 1.0, 0.0).astype(BF16)
    nt = (((1,), (1,)), ((), ()))
    first = jnp.dot(pick, in_ref[...], preferred_element_type=F32)
    second = jnp.dot(pick, out_ref[...], preferred_element_type=F32)
    bias = jnp.broadcast_to(bias_ref[...], (LANES, own))
    third = lax.dot_general(pick, bias, nt, preferred_element_type=F32)
    row = lax.broadcasted_iota(jnp.int32, (deep, channels), 0)
    col = lax.broadcasted_iota(jnp.int32, (deep, channels), 1)
    pick = jnp.where(col == row, 1.0, 0.0).astype(BF16)
    gain = jnp.broadcast_to(gain_ref[...], (LANES, channels))
    gain = lax.dot_general(pick, gain, nt, preferred_element_type=F32)
    shift = jnp.broadcast_to(shift_ref[...], (LANES, channels))
    shift = lax.dot_general(pick, shift, nt, preferred_element_type=F32)
    lane = lane_of(deep)
    third = jnp.where(lane == 0, third, jnp.where(lane == 1, gain, jnp.where(lane == 2, shift, 0.0)))
    pack_ref[:, :count] = first.astype(BF16)
    pack_ref[:, count : 2 * count] = second.astype(BF16)
    pack_ref[:, 2 * count :] = third.astype(BF16)


ROOT = math.sqrt(2.0 / math.pi)


def place_of(quad, near, deep, z, xy, far_at, near_at):
    apart = far_at ^ z
    turn = ((apart & 1) << 1) | (apart >> 1)
    side = near_at ^ xy
    if not quad:
        return (near_at * 4 + turn) * deep
    swapped = ((side & 1) << 1) | (side >> 1)
    first = side * 2 + turn
    second = 8 + swapped * 2 + turn - 2
    return jnp.where(turn < 2, first, second) * deep


def mlp_kernel(quad, near, pieces, where_ref, mixed_ref, down_ref, *refs):
    own_in, refs = refs[:pieces], refs[pieces:]
    other_in, refs = refs[:pieces], refs[pieces:]
    both_ref, refs = refs[0], refs[1:]
    own_out, refs = refs[:pieces], refs[pieces:]
    gother_ref, weights, grads, active, normal, gains, sum_acc, grad_acc, sems = refs
    count, tokens = mixed_ref.shape
    devices, _, channels, _ = both_ref.shape
    rows = weights.shape[0] // 2
    tall = rows // pieces
    deep = rows // devices
    blocks = 4
    block = 2 * rows // blocks
    loads = []
    for index, ref in enumerate(own_in + other_in):
        span = weights.at[pl.ds(index * tall, tall), :]
        loads.append(pltpu.make_async_copy(ref, span, sems.at[index]))
    for copy in loads:
        copy.start()

    value = mixed_ref[...].astype(F32)
    mean = jnp.mean(value, axis=0, keepdims=True)
    value = value - mean
    inv = lax.rsqrt(jnp.mean(value * value, axis=0, keepdims=True) + EPS)
    normal[...] = value * inv
    sum_acc[...] = jnp.zeros_like(sum_acc)
    grad_acc[...] = jnp.zeros_like(grad_acc)
    for copy in loads:
        copy.wait()
    z, xy = where_ref[0], where_ref[1]
    spots = []
    for d in range(devices):
        spot = pl.multiple_of(place_of(quad, near, deep, z, xy, d // near, d % near), deep)
        spots.append(spot)
        tile = weights[pl.ds(spot, deep), 2 * count :].astype(F32)
        gains[d * channels : (d + 1) * channels] = tile[:channels]
    gain = gains[:, 1:2]
    active[...] = (normal[...] * gain + gains[:, 2:3]).astype(BF16)

    nt = (((1,), (1,)), ((), ()))
    tn = (((0,), (0,)), ((), ()))

    def process(step, carry):
        at = pl.ds(pl.multiple_of(step * block, block), block)
        w_in = weights[at, :count]
        w_out = weights[at, count : 2 * count]
        bias = weights[at, 2 * count :].astype(F32)[:, 0:1]
        act = active[...]
        down = down_ref[...]
        v = jnp.dot(w_in, act, preferred_element_type=F32) + bias
        square = v * v
        half = 0.5 * jnp.tanh(v * (ROOT * 0.044715 * square + ROOT)) + 0.5
        full = v * half
        hidden = full.astype(BF16)
        slope = half + full * (1.0 - half) * (6.0 * ROOT * 0.044715 * square + 2.0 * ROOT)
        sum_acc[...] += lax.dot_general(w_out, hidden, tn, preferred_element_type=F32)
        hgrad = jnp.dot(w_out, down, preferred_element_type=F32)
        low = (hgrad * slope).astype(BF16)
        grad_acc[...] += lax.dot_general(w_in, low, tn, preferred_element_type=F32)
        g_in = lax.dot_general(low, act, nt, preferred_element_type=F32)
        g_out = lax.dot_general(hidden, down, nt, preferred_element_type=F32)
        g_bias = jnp.sum(low.astype(F32), axis=1, keepdims=True)
        grads[at, :count] = g_in.astype(BF16)
        grads[at, count : 2 * count] = g_out.astype(BF16)
        g_bias = jnp.where(lane_of(block) == 0, g_bias, 0.0)
        grads[at, 2 * count :] = g_bias.astype(BF16)
        return carry

    lax.fori_loop(0, blocks, process, 0)
    stores = [pltpu.make_async_copy(grads.at[pl.ds(rows, rows), :], gother_ref, sems.at[0])]
    stores[0].start()

    agrad = grad_acc[...]
    norm = normal[...]
    scaled = agrad * gains[:, 1:2]
    first = jnp.mean(scaled, axis=0, keepdims=True)
    second = jnp.mean(scaled * norm, axis=0, keepdims=True)
    mgrad = (scaled - first - norm * second) * inv
    summed = sum_acc[...]
    for d in range(devices):
        both_ref[d, 0] = mgrad[d * channels : (d + 1) * channels].astype(BF16)
        both_ref[d, 1] = summed[d * channels : (d + 1) * channels].astype(BF16)
    lane = lane_of(count)
    ext = jnp.where(lane == 1, jnp.sum(agrad * norm, axis=1, keepdims=True), 0.0)
    ext = jnp.where(lane == 2, jnp.sum(agrad, axis=1, keepdims=True), ext)
    for d in range(devices):
        at = pl.ds(spots[d], deep)
        part = ext[d * channels : (d + 1) * channels]
        if channels < deep:
            part = jnp.concatenate([part, jnp.zeros((deep - channels, LANES), F32)], axis=0)
        grads[at, 2 * count :] = (grads[at, 2 * count :].astype(F32) + part).astype(BF16)
    for index, ref in enumerate(own_out):
        span = grads.at[pl.ds(index * tall, tall), :]
        copy = pltpu.make_async_copy(span, ref, sems.at[index + 1])
        copy.start()
        stores.append(copy)
    for copy in stores:
        copy.wait()


def whole(shape):
    return pl.BlockSpec(shape, lambda i: (0,) * len(shape))


def params(**extra):
    return pltpu.CompilerParams(vmem_limit_bytes=VMEM_LIMIT, **extra)


def cost(micros):
    return pl.CostEstimate(flops=0, transcendentals=0, bytes_accessed=micros * 3_000_000)


SMEM = pl.BlockSpec(memory_space=pltpu.SMEM)


def per_device(
    ch, features, cotangent, heights, widths, step_height, rate_height, readout_height,
    step_width, rate_width, readout_width, skip_gain, norm_gain, norm_shift, in_weight,
    in_bias, out_weight, out_bias, layer_scale,
):
    channels, cells = features.shape
    count = in_weight.shape[0]
    units = in_weight.shape[1]
    states = rate_height.shape[1]
    images = cells // CELLS
    tokens = cells // ch
    parts = CELLS // tokens
    far = 4
    near = ch // far
    deep = -(-(units // 2) // 16) * 16
    width = 2 * count + LANES
    quad = near == 4
    near_groups = [[f * near + i for i in range(near)] for f in range(far)]
    row = lambda v: v.reshape(1, -1)
    exchange = lambda v: lax.ppermute(v, "img", [(0, 1), (1, 0)])
    flip = lambda v, bits: lax.ppermute(v, "ch", [(i, i ^ bits) for i in range(ch)])
    swap = lambda v, groups=None: lax.all_to_all(
        v, "ch", split_axis=0, concat_axis=0, tiled=True, axis_index_groups=groups
    )
    half = lax.axis_index("img").astype(jnp.int32)
    place = lax.axis_index("ch").astype(jnp.int32)
    full = pl.BlockSpec(memory_space=pltpu.VMEM)
    raw = pl.BlockSpec(memory_space=pl.ANY)

    pack = pl.pallas_call(
        pack_kernel,
        out_shape=jax.ShapeDtypeStruct((deep, width), BF16),
        in_specs=[SMEM] + [full] * 5,
        out_specs=full,
        compiler_params=params(),
        cost_estimate=cost(2),
        name="pack",
    )(half.reshape(1), in_weight.T, out_weight, row(in_bias), row(norm_gain), row(norm_shift))
    even = jnp.concatenate([pack, flip(pack, 2 * near)], axis=0)
    odd = flip(even, near)

    cells_spec = pl.BlockSpec((channels, CELLS), lambda i: (0, i))
    down = pl.pallas_call(
        down_kernel,
        out_shape=jax.ShapeDtypeStruct((ch, channels, tokens), BF16),
        in_specs=[SMEM, SMEM, full, full],
        out_specs=full,
        compiler_params=params(),
        cost_estimate=cost(2),
        name="down",
    )(heights, widths, cotangent, row(layer_scale))
    features_after, down = lax.optimization_barrier((features, down))
    down = swap(down).reshape(count, tokens)

    state = whole((channels, states))
    vector = whole((1, channels))
    tap = pltpu.VMEM((SIDE, channels, LANES), F32)
    plane = pltpu.VMEM((channels, CELLS), F32)
    mixed, taps = pl.pallas_call(
        forward_kernel,
        grid=(images,),
        out_shape=(
            jax.ShapeDtypeStruct((ch, channels, tokens), BF16),
            jax.ShapeDtypeStruct((channels, LANES), F32),
        ),
        in_specs=[SMEM, SMEM, cells_spec, vector, vector, state, state, state, state, vector],
        out_specs=(
            pl.BlockSpec((parts, channels, tokens), lambda i: (i, 0, 0)),
            whole((channels, LANES)),
        ),
        scratch_shapes=[tap, tap, plane, plane],
        compiler_params=params(),
        cost_estimate=cost(12),
        name="mixer_forward",
    )(
        heights, widths, features_after, row(step_height), row(step_width), rate_height,
        rate_width, readout_height, readout_width, row(skip_gain),
    )
    if quad:
        even = jnp.concatenate([even, flip(even, 1)], axis=0)
        odd = jnp.concatenate([odd, flip(odd, 2)], axis=0)
        even, odd, mixed = lax.optimization_barrier((even, odd, mixed))
        own = [even, flip(even, 2), odd, flip(odd, 1)]
    else:
        both = jnp.concatenate([even, odd], axis=0)
        both = jnp.broadcast_to(both[None], (near, far * deep, width))
        own = [swap(both, near_groups).reshape(ch * deep, width)]
    mixed = swap(mixed).reshape(count, tokens)
    other = [exchange(piece) for piece in own]

    rows = ch * deep
    pieces = len(own)
    both_shape = (ch, 2, channels, tokens)
    piece_shape = jax.ShapeDtypeStruct((rows // pieces, width), BF16)
    outs = pl.pallas_call(
        partial(mlp_kernel, quad, near, pieces),
        out_shape=[jax.ShapeDtypeStruct(both_shape, BF16)]
        + [piece_shape] * pieces
        + [jax.ShapeDtypeStruct((rows, width), BF16)],
        in_specs=[SMEM, full, full] + [raw] * (2 * pieces),
        out_specs=[full] + [raw] * (pieces + 1),
        scratch_shapes=[
            pltpu.VMEM((2 * rows, width), BF16),
            pltpu.VMEM((2 * rows, width), BF16),
            pltpu.VMEM((count, tokens), BF16),
            pltpu.VMEM((count, tokens), F32),
            pltpu.VMEM((count, LANES), F32),
            pltpu.VMEM((count, tokens), F32),
            pltpu.VMEM((count, tokens), F32),
            pltpu.SemaphoreType.DMA((2 * pieces,)),
        ],
        compiler_params=params(),
        cost_estimate=cost(10),
        name="mlp",
    )(jnp.stack([place // near, place % near]), mixed, down, *own, *other)
    both, gown, gother = outs[0], outs[1:-1], outs[-1]

    arrived = exchange(gother).astype(F32)
    both = swap(both)
    if quad:
        tall = rows // 4
        part = [gown[i].astype(F32) + arrived[i * tall : (i + 1) * tall] for i in range(4)]
        even = part[0] + flip(part[1].astype(BF16), 2).astype(F32)
        odd = part[2] + flip(part[3].astype(BF16), 1).astype(F32)
        cut = tall // 2
        even = even[:cut] + flip(even[cut:].astype(BF16), 1).astype(F32)
        odd = odd[:cut] + flip(odd[cut:].astype(BF16), 2).astype(F32)
    else:
        total = (gown[0].astype(F32) + arrived).astype(BF16).reshape(near, far * deep, width)
        total = jnp.sum(swap(total, near_groups).astype(F32), axis=0)
        even, odd = total[: 2 * deep], total[2 * deep :]
    even = even + flip(odd.astype(BF16), near).astype(F32)

    result, grad_features, small = pl.pallas_call(
        backward_kernel,
        grid=(images,),
        out_shape=(
            jax.ShapeDtypeStruct((channels, cells), BF16),
            jax.ShapeDtypeStruct((channels, cells), F32),
            jax.ShapeDtypeStruct((channels, LANES), F32),
        ),
        in_specs=[
            SMEM, SMEM, cells_spec, cells_spec,
            pl.BlockSpec((parts, 2, channels, tokens), lambda i: (i, 0, 0, 0)),
            whole((channels, LANES)), vector, vector,
        ],
        out_specs=(cells_spec, cells_spec, whole((channels, LANES))),
        scratch_shapes=[tap, tap, tap, tap, plane, plane, plane],
        compiler_params=params(),
        cost_estimate=cost(15),
        name="mixer_backward",
    )(heights, widths, features, cotangent, both, taps, row(layer_scale), row(out_bias))

    even, small = lax.optimization_barrier((even, small))
    partial_sum = even[:deep] + flip(even[deep:].astype(BF16), 2 * near).astype(F32)
    sibling = exchange(partial_sum)
    keep = units // 2
    low = jnp.where(half == 0, partial_sum, sibling)[:keep]
    high = jnp.where(half == 0, sibling, partial_sum)[:keep]
    grads = jnp.concatenate([low, high], axis=0)
    grad_in_weight = grads[:, :count].T
    grad_out_weight = grads[:, count : 2 * count]
    grad_in_bias = grads[:, 2 * count]
    norms = (partial_sum + sibling)[:channels, 2 * count + 1 : 2 * count + 3]

    vector_out = jax.ShapeDtypeStruct((1, channels), F32)
    state_out = jax.ShapeDtypeStruct((channels, states), F32)
    chained = pl.pallas_call(
        chain_kernel,
        out_shape=(
            vector_out, state_out, state_out, vector_out, state_out, state_out,
            vector_out, vector_out, vector_out,
        ),
        in_specs=[full] * 9,
        out_specs=(full,) * 9,
        compiler_params=params(),
        cost_estimate=cost(2),
        name="mixer_chain",
    )(
        small, exchange(small), row(step_height), row(step_width), rate_height, rate_width,
        readout_height, readout_width, row(layer_scale),
    )
    gstep_h, grate_h, gread_h, gstep_w, grate_w, gread_w, gskip, gbias, gscale = chained
    flat = lambda v: v.reshape(-1)
    return (
        result, grad_features, flat(gstep_h), grate_h, gread_h, flat(gstep_w), grate_w, gread_w,
        flat(gskip), norms[:, 0], norms[:, 1], grad_in_weight, grad_in_bias, grad_out_weight,
        flat(gbias), flat(gscale),
    )


def solution(mesh):
    wide, split, tall = P("ch", "img"), P("ch"), P("ch", None)
    return jax.shard_map(
        partial(per_device, mesh.shape["ch"]),
        mesh=mesh,
        in_specs=(
            wide, wide, P("img"), P("img"), split, tall, tall, split, tall, tall, split, split,
            split, P(None, "ch"), split, tall, split, split,
        ),
        out_specs=(
            wide, wide, split, tall, tall, split, tall, tall, split, split, split,
            P(None, "ch"), split, tall, split, split,
        ),
        check_vma=False,
    )
```

```python
import math
from functools import partial

import jax
import jax.numpy as jnp
from jax import lax
from jax.experimental import pallas as pl
from jax.experimental.pallas import tpu as pltpu
from jax.sharding import PartitionSpec as P

SIDE = 32
CELLS = SIDE * SIDE
LANES = 128
PER = LANES // SIDE
SLOT = 8
TILES = CELLS // LANES
EPS = 1e-06
F32 = jnp.float32
BF16 = jnp.bfloat16


def column(row):
    n = row.shape[1]
    eye = lax.broadcasted_iota(jnp.int32, (n, n), 0) == lax.broadcasted_iota(jnp.int32, (n, n), 1)
    return jnp.sum(jnp.where(eye, jnp.broadcast_to(row, (n, n)), 0.0), axis=1, keepdims=True)


def as_row(col):
    n = col.shape[0]
    eye = lax.broadcasted_iota(jnp.int32, (n, n), 0) == lax.broadcasted_iota(jnp.int32, (n, n), 1)
    return jnp.sum(jnp.where(eye, jnp.broadcast_to(col, (n, n)), 0.0), axis=0, keepdims=True)


def image_mask(rows, height, width):
    cell = lax.broadcasted_iota(jnp.int32, (rows, CELLS), 1)
    return (cell // SIDE < height) & (cell % SIDE < width)


def lane_of(rows):
    return lax.broadcasted_iota(jnp.int32, (rows, LANES), 1)


def fill_slots(slots, value, image):
    channels = value.shape[0]
    for group in range(slots.shape[0]):
        live = min(SLOT, channels - group * SLOT)
        for k in range(TILES):
            at = (image * TILES + k) * SLOT
            part = value[group * SLOT : group * SLOT + live, k * LANES : (k + 1) * LANES]
            slots[group, pl.ds(at, live), :] = part


def read_slots(slots, image, channels):
    rows = []
    for group in range(slots.shape[0]):
        live = min(SLOT, channels - group * SLOT)
        at = [(image * TILES + k) * SLOT for k in range(TILES)]
        rows.append(jnp.concatenate([slots[group, pl.ds(a, live), :] for a in at], axis=1))
    return jnp.concatenate(rows, axis=0) if len(rows) > 1 else rows[0]


def cross(tiles, lane):
    for bit, far in ((2, 64), (1, 32)):
        low = (lane & far) == 0
        out = list(tiles)
        for k in range(len(tiles)):
            if not k & bit:
                one, two = tiles[k], tiles[k | bit]
                out[k] = jnp.where(low, one, pltpu.roll(two, far, 1))
                out[k | bit] = jnp.where(low, pltpu.roll(one, LANES - far, 1), two)
        tiles = out
    return tiles


def load_channel(slots, group, c, lane):
    count = slots.shape[1] // SLOT
    value = slots[group, pl.ds(c, count, stride=SLOT), :]
    return cross([value[k * SLOT : (k + 1) * SLOT] for k in range(count // SLOT)], lane)


def store_channel(slots, group, c, tiles, lane):
    count = slots.shape[1] // SLOT
    slots[group, pl.ds(c, count, stride=SLOT), :] = jnp.concatenate(cross(tiles, lane), axis=0)


def split(value):
    high = value.astype(BF16)
    return high, (value - high.astype(F32)).astype(BF16)


def pick(row, index):
    spread = jnp.broadcast_to(row, index.shape)
    value = jnp.take_along_axis(spread, jnp.clip(index, 0, LANES - 1), axis=1)
    return value


def build_down(row, c, high_ref, low_ref, lane, sub):
    place = lane % SIDE
    source = (place % TILES) * PER + place // TILES
    here = lane // SIDE == c % PER
    parts = []
    for turn in range(PER):
        index = PER * sub + turn - source
        parts.append(jnp.where(here & (index >= 0), pick(row, index), 0.0))
    high, low = split(jnp.concatenate(parts, axis=0))
    at = (slice(c * SIDE, (c + 1) * SIDE), slice(c // PER * LANES, (c // PER + 1) * LANES))
    high_ref[at] = high
    low_ref[at] = low


def build_across(row, turned, lane, sub):
    place = lane % SIDE
    highs, lows = [], []
    for part in range(PER):
        own = part * SLOT + sub
        index = own - place if turned else place - own
        value = jnp.where(index >= 0, pick(row, index + SIDE), 0.0)
        high = value.astype(BF16).astype(F32)
        highs.append(high)
        lows.append(value - high)
    spread = lambda parts: jnp.concatenate(
        [jnp.where(lane // SIDE == i, p, 0.0) for i in range(PER) for p in parts], axis=0
    ).astype(BF16)
    return spread(highs), spread(lows)


def taps_of(step_h, step_w, rate_h, rate_w, read_h, read_w, skip_ref):
    channels = rate_h.shape[0]
    lane = lane_of(channels)
    kept = jnp.zeros((channels, LANES), F32)
    decay_h = jnp.exp(column(step_h[...])) * rate_h[...]
    decay_w = jnp.exp(column(step_w[...])) * rate_w[...]
    for lag in range(SIDE):
        tap = jnp.sum(read_h[...] * jnp.exp(-decay_h * lag), axis=1, keepdims=True)
        kept = jnp.where(lane == lag, tap, kept)
        tap = jnp.sum(read_w[...] * jnp.exp(-decay_w * lag), axis=1, keepdims=True)
        kept = jnp.where(lane == SIDE + lag, tap, kept)
    return jnp.where(lane == 2 * SIDE, column(skip_ref[...]), kept)


def dot(a, b, dims=(((1,), (0,)), ((), ()))):
    return lax.dot_general(a, b, dims, preferred_element_type=F32)


NT = (((1,), (1,)), ((), ()))
TN = (((0,), (0,)), ((), ()))


def forward_kernel(
    heights, widths, feat_ref, cot_ref, scale_ref, step_h, step_w, rate_h, rate_w, read_h,
    read_w, skip_ref, out_ref, rows_ref, slots, high_a, low_a, field, tall,
):
    channels, cells = feat_ref.shape
    images = cells // CELLS
    rows_ref[0:channels] = taps_of(step_h, step_w, rate_h, rate_w, read_h, read_w, skip_ref)
    for ref in (high_a, low_a, field):
        ref[...] = jnp.zeros_like(ref)
    for image in range(images):
        inside = image_mask(1, heights[image], widths[image])
        value = feat_ref[:, image * CELLS : (image + 1) * CELLS].astype(F32)
        fill_slots(slots, jnp.where(inside, value, 0.0), image)
    live = min(SLOT, channels)
    sides = images // PER

    def body(group, carry):
        lane = lane_of(SLOT)
        sub = lax.broadcasted_iota(jnp.int32, (SLOT, LANES), 0)
        for c in range(live):
            row = rows_ref[pl.ds(group * SLOT + c, 1), :]
            build_down(row, c, high_a, low_a, lane, sub)
            tiles = load_channel(slots, group, c, lane)
            for s in range(sides):
                value = jnp.concatenate(tiles[s * PER : (s + 1) * PER], axis=0)
                field[c * SIDE : (c + 1) * SIDE, s * LANES : (s + 1) * LANES] = value.astype(BF16)
        source = field[...]
        tall[...] = dot(high_a[...], source) + dot(low_a[...], source)
        for c in range(live):
            row = rows_ref[pl.ds(group * SLOT + c, 1), :]
            high_b, low_b = build_across(row, False, lane, sub)
            value = jnp.concatenate(
                [tall[c * SIDE : (c + 1) * SIDE, s * LANES : (s + 1) * LANES] for s in range(sides)],
                axis=0,
            )
            high, low = split(value)
            value = dot(
                jnp.concatenate([high, low, high], axis=1),
                jnp.concatenate([high_b, high_b, low_b], axis=0),
            )
            tiles = [value[k * SLOT : (k + 1) * SLOT] for k in range(images)]
            store_channel(slots, group, c, tiles, lane)
        return carry

    lax.fori_loop(0, slots.shape[0], body, 0)
    wide = out_ref.shape[3]
    parts = CELLS // wide
    skip = rows_ref[0:channels, 2 * SIDE : 2 * SIDE + 1]
    scale = column(scale_ref[...])
    for image in range(images):
        span = slice(image * CELLS, (image + 1) * CELLS)
        inside = image_mask(1, heights[image], widths[image])
        value = read_slots(slots, image, channels) + skip * feat_ref[:, span].astype(F32)
        value = jnp.where(inside, value, 0.0).astype(BF16)
        down = cot_ref[:, span].astype(F32) * scale
        down = jnp.where(inside, down, 0.0).astype(BF16)
        for j in range(parts):
            out_ref[image * parts + j, 0] = value[:, j * wide : (j + 1) * wide]
            out_ref[image * parts + j, 1] = down[:, j * wide : (j + 1) * wide]


def backward_kernel(
    heights, widths, feat_ref, cot_ref, both_ref, rows_ref, scale_ref, bias_ref,
    result_ref, gfeat_ref, small_ref,
    slots, slots_g, high_a, low_a, field, field_g, tall, high_d, low_d, wide_ref, sums,
):
    channels, cells = feat_ref.shape
    images = cells // CELLS
    live = min(SLOT, channels)
    sides = images // PER
    wide = both_ref.shape[3]
    parts = CELLS // wide
    for ref in (high_a, low_a, sums, field, field_g, high_d, low_d):
        ref[...] = jnp.zeros_like(ref)
    lane_c = lane_of(channels)
    scale = column(scale_ref[...])
    bias = column(bias_ref[...])
    small = jnp.zeros((channels, LANES), F32)
    for image in range(images):
        span = slice(image * CELLS, (image + 1) * CELLS)
        inside = image_mask(1, heights[image], widths[image])
        values = feat_ref[:, span].astype(F32)
        masked = jnp.where(inside, values, 0.0)
        fill_slots(slots, masked, image)
        grad = jnp.concatenate(
            [both_ref[image * parts + j, 0].astype(F32) for j in range(parts)], axis=1
        )
        grad = jnp.where(inside, grad, 0.0)
        fill_slots(slots_g, grad, image)
        shifted = jnp.concatenate(
            [both_ref[image * parts + j, 1].astype(F32) for j in range(parts)], axis=1
        )
        shifted = shifted + bias
        result = values + jnp.where(inside, scale * shifted, 0.0)
        result_ref[:, span] = result.astype(BF16)
        weighted = jnp.where(inside, cot_ref[:, span].astype(F32), 0.0)
        small = small + jnp.where(
            lane_c == 64,
            jnp.sum(grad * masked, axis=1, keepdims=True),
            jnp.where(
                lane_c == 65,
                jnp.sum(weighted * shifted, axis=1, keepdims=True),
                jnp.where(lane_c == 66, jnp.sum(weighted, axis=1, keepdims=True), 0.0),
            ),
        )

    def body(group, carry):
        lane = lane_of(SLOT)
        sub = lax.broadcasted_iota(jnp.int32, (SLOT, LANES), 0)
        place = lane % SIDE
        half = lambda ref, c, s: ref[c * SIDE : (c + 1) * SIDE, s * LANES : (s + 1) * LANES]
        stack = lambda ref, c: jnp.concatenate([half(ref, c, s) for s in range(sides)], axis=0)
        for c in range(live):
            row = rows_ref[pl.ds(group * SLOT + c, 1), :]
            build_down(row, c, high_a, low_a, lane, sub)
            for slot, out in ((slots, field), (slots_g, field_g)):
                tiles = load_channel(slot, group, c, lane)
                for s in range(sides):
                    value = jnp.concatenate(tiles[s * PER : (s + 1) * PER], axis=0)
                    at = (slice(c * SIDE, (c + 1) * SIDE), slice(s * LANES, (s + 1) * LANES))
                    out[at] = value.astype(BF16)
        source = field[...]
        tall[...] = dot(high_a[...], source) + dot(low_a[...], source)
        for c in range(live):
            row = rows_ref[pl.ds(group * SLOT + c, 1), :]
            high_b, low_b = build_across(row, True, lane, sub)
            grad = stack(field_g, c)
            flow = dot(
                jnp.concatenate([grad, grad], axis=1), jnp.concatenate([high_b, low_b], axis=0)
            )
            high, low = split(flow)
            for s in range(sides):
                at = (slice(c * SIDE, (c + 1) * SIDE), slice(s * LANES, (s + 1) * LANES))
                high_d[at] = high[s * SIDE : (s + 1) * SIDE]
                low_d[at] = low[s * SIDE : (s + 1) * SIDE]
            high, low = split(stack(tall, c))
            outer = dot(
                jnp.concatenate([grad, grad], axis=0), jnp.concatenate([high, low], axis=0), TN
            )
            total = None
            for part in range(PER):
                value = None
                for i in range(PER):
                    at = i * SIDE + part * SLOT
                    term = jnp.where(lane // SIDE == i, outer[at : at + SLOT], 0.0)
                    value = term if value is None else value + term
                index = part * SLOT + sub - place
                value = jnp.take_along_axis(
                    value, jnp.clip(index, 0, SIDE - 1) + lane // SIDE * SIDE, axis=1
                )
                value = jnp.where(index >= 0, value, 0.0)
                total = value if total is None else total + value
            total = jnp.sum(total, axis=0, keepdims=True)
            total = total + pltpu.roll(total, 64, 1)
            total = total + pltpu.roll(total, 32, 1)
            sums[pl.ds(group * SLOT + c, 1), :] = jnp.where(lane[0:1] // SIDE == 1, total, 0.0)
        high, low = high_d[...], low_d[...]
        back = dot(high_a[...], high, TN) + dot(high_a[...], low, TN) + dot(low_a[...], high, TN)
        wide_ref[...] = back
        outer = dot(high, source, NT) + dot(low, source, NT)
        tall[...] = outer
        for c in range(live):
            value = stack(wide_ref, c)
            tiles = [value[k * SLOT : (k + 1) * SLOT] for k in range(images)]
            store_channel(slots, group, c, tiles, lane)
            total = None
            for turn in range(PER):
                at = c * SIDE + turn * SLOT
                value = tall[at : at + SLOT, c // PER * LANES : (c // PER + 1) * LANES]
                index = PER * sub + turn - lane
                safe = jnp.clip(index, 0, SIDE - 1)
                index_at = (safe % PER) * TILES + safe // PER + c % PER * SIDE
                value = jnp.take_along_axis(value, index_at, axis=1)
                value = jnp.where(index >= 0, value, 0.0)
                total = value if total is None else total + value
            total = jnp.sum(total, axis=0, keepdims=True)
            total = jnp.where(lane[0:1] < SIDE, total, 0.0)
            sums[pl.ds(group * SLOT + c, 1), :] += total
        return carry

    lax.fori_loop(0, slots.shape[0], body, 0)
    skip = rows_ref[0:channels, 2 * SIDE : 2 * SIDE + 1]
    for image in range(images):
        span = slice(image * CELLS, (image + 1) * CELLS)
        inside = image_mask(1, heights[image], widths[image])
        grad = read_slots(slots_g, image, channels)
        value = read_slots(slots, image, channels) + skip * grad
        gfeat_ref[:, span] = cot_ref[:, span].astype(F32) + jnp.where(inside, value, 0.0)
    small_ref[...] = small + sums[0:channels]


def chain_kernel(
    own_ref, other_ref, step_h, step_w, rate_h, rate_w, read_h, read_w, scale_ref,
    gstep_h, grate_h, gread_h, gstep_w, grate_w, gread_w, gskip, gbias, gscale,
):
    total = own_ref[...] + other_ref[...]
    for first, step, rate, read, gstep, grate, gread in (
        (0, step_h, rate_h, read_h, gstep_h, grate_h, gread_h),
        (SIDE, step_w, rate_w, read_w, gstep_w, grate_w, gread_w),
    ):
        pace = jnp.exp(column(step[...]))
        decay = pace * rate[...]
        to_read = jnp.zeros_like(decay)
        to_decay = jnp.zeros_like(decay)
        for lag in range(SIDE):
            term = total[:, first + lag : first + lag + 1] * jnp.exp(-decay * lag)
            to_read = to_read + term
            if lag:
                to_decay = to_decay - float(lag) * term
        to_decay = to_decay * read[...]
        gread[...] = to_read
        grate[...] = pace * to_decay
        gstep[...] = as_row(jnp.sum(to_decay * decay, axis=1, keepdims=True))
    gskip[...] = as_row(total[:, 64:65])
    gscale[...] = as_row(total[:, 65:66])
    gbias[...] = as_row(total[:, 66:67]) * scale_ref[...]


def join_kernel(count, *refs):
    given, outs = refs[:count], refs[count:]
    tall = outs[0].shape[0]
    for index, out in enumerate(outs):
        at = slice(index * tall, (index + 1) * tall)
        total = given[0][at].astype(F32)
        for ref in given[1:]:
            total = total + ref[at].astype(F32)
        out[...] = total.astype(out.dtype)


def relay_kernel(one_ref, two_ref, arrived_ref, first_ref, second_ref, out_one, out_two):
    tall = one_ref.shape[0]
    cut = tall // 2
    one = one_ref[...].astype(F32) + arrived_ref[tall : 2 * tall].astype(F32)
    two = two_ref[...].astype(F32) + arrived_ref[2 * tall : 3 * tall].astype(F32)
    out_one[:cut] = (one[:cut] + first_ref[...].astype(F32)).astype(BF16)
    out_one[cut:] = one[cut:].astype(BF16)
    out_two[:cut] = two[:cut].astype(BF16)
    out_two[cut:] = (two[cut:] + second_ref[...].astype(F32)).astype(BF16)


def finish_kernel(half, mine_ref, other_ref, ggain, gshift, gin, ginb, gout):
    units, count = gin.shape
    channels = ggain.shape[1]
    keep = units // 2
    first = half[0] == 0
    mine, other = mine_ref[...], other_ref[...]
    low = jnp.where(first, mine, other)[:keep]
    high = jnp.where(first, other, mine)[:keep]
    for at, part in ((0, low), (keep, high)):
        gin[at : at + keep] = part[:, :count]
        gout[at : at + keep] = part[:, count : 2 * count]
    bias = jnp.concatenate([low[:, 2 * count :], high[:, 2 * count :]], axis=0)
    ginb[...] = as_row(bias[:, 0:1])
    norms = (mine[:, 2 * count :] + other[:, 2 * count :])[:channels]
    ggain[...] = as_row(norms[:, 1:2])
    gshift[...] = as_row(norms[:, 2:3])


def pack_kernel(half, in_ref, out_ref, bias_ref, gain_ref, shift_ref, pack_ref):
    deep = pack_ref.shape[0]
    own, count = out_ref.shape
    channels = gain_ref.shape[1]
    keep = own // 2
    row = lax.broadcasted_iota(jnp.int32, (deep, own), 0)
    col = lax.broadcasted_iota(jnp.int32, (deep, own), 1)
    pick = jnp.where((col == row + half[0] * keep) & (row < keep), 1.0, 0.0).astype(BF16)
    nt = (((1,), (1,)), ((), ()))
    first = jnp.dot(pick, in_ref[...], preferred_element_type=F32)
    second = jnp.dot(pick, out_ref[...], preferred_element_type=F32)
    bias = jnp.broadcast_to(bias_ref[...], (LANES, own))
    third = lax.dot_general(pick, bias, nt, preferred_element_type=F32)
    row = lax.broadcasted_iota(jnp.int32, (deep, channels), 0)
    col = lax.broadcasted_iota(jnp.int32, (deep, channels), 1)
    pick = jnp.where(col == row, 1.0, 0.0).astype(BF16)
    gain = jnp.broadcast_to(gain_ref[...], (LANES, channels))
    gain = lax.dot_general(pick, gain, nt, preferred_element_type=F32)
    shift = jnp.broadcast_to(shift_ref[...], (LANES, channels))
    shift = lax.dot_general(pick, shift, nt, preferred_element_type=F32)
    lane = lane_of(deep)
    third = jnp.where(lane == 0, third, jnp.where(lane == 1, gain, jnp.where(lane == 2, shift, 0.0)))
    pack_ref[:, :count] = first.astype(BF16)
    pack_ref[:, count : 2 * count] = second.astype(BF16)
    pack_ref[:, 2 * count :] = third.astype(BF16)


ROOT = math.sqrt(2.0 / math.pi)


def mlp_kernel(near, pieces, where_ref, given_ref, *refs):
    own_in, refs = refs[:pieces], refs[pieces:]
    other_in, refs = refs[:pieces], refs[pieces:]
    both_ref, refs = refs[0], refs[1:]
    own_out, refs = refs[:pieces], refs[pieces:]
    gother_ref, active, downs, normal, gains, sum_acc, grad_acc, ext, gext = refs
    count, tokens = normal.shape
    devices, _, channels, _ = both_ref.shape
    spans, rows = [], 0
    for ref in own_in:
        spans.append(slice(rows, rows + ref.shape[0]))
        rows += ref.shape[0]
    deep = rows // devices

    value = jnp.concatenate([given_ref[d, 0].astype(F32) for d in range(devices)], axis=0)
    mean = jnp.mean(value, axis=0, keepdims=True)
    value = value - mean
    inv = lax.rsqrt(jnp.mean(value * value, axis=0, keepdims=True) + EPS)
    normal[...] = value * inv
    value = jnp.concatenate([given_ref[d, 1].astype(F32) for d in range(devices)], axis=0)
    downs[...] = value.astype(BF16)
    for at, ref in zip(spans, own_in):
        ext[at] = ref[:, 2 * count :].astype(F32)
    z, xy = where_ref[0], where_ref[1]
    spots = []
    for d in range(devices):
        spot = ((d % near) ^ xy) * (devices // near) + ((d // near) ^ z)
        spot = pl.multiple_of(spot * deep, deep)
        spots.append(spot)
        gains[d * channels : (d + 1) * channels] = ext[pl.ds(spot, deep), :][:channels]
    active[...] = (normal[...] * gains[:, 1:2] + gains[:, 2:3]).astype(BF16)

    def process(refs, first):
        w_in = jnp.concatenate([ref[:, :count] for ref in refs], axis=0)
        w_out = jnp.concatenate([ref[:, count : 2 * count] for ref in refs], axis=0)
        bias = jnp.concatenate([ref[:, 2 * count :] for ref in refs], axis=0).astype(F32)[:, 0:1]
        act = active[...]
        down = downs[...]
        v = dot(w_in, act) + bias
        square = v * v
        half = 0.5 * jnp.tanh(v * (ROOT * 0.044715 * square + ROOT)) + 0.5
        full = v * half
        hidden = full.astype(BF16)
        slope = half + full * (1.0 - half) * (6.0 * ROOT * 0.044715 * square + 2.0 * ROOT)
        low = (dot(w_out, down) * slope).astype(BF16)
        if first:
            sum_acc[...] = dot(w_out, hidden, TN)
            grad_acc[...] = dot(w_in, low, TN)
        else:
            sum_acc[...] += dot(w_out, hidden, TN)
            grad_acc[...] += dot(w_in, low, TN)
        g_bias = jnp.sum(low.astype(F32), axis=1, keepdims=True)
        g_bias = jnp.where(lane_of(low.shape[0]) == 0, g_bias, 0.0)
        return dot(low, act, NT), dot(hidden, down, NT), g_bias

    g_in, g_out, g_bias = process(other_in, True)
    gother_ref[:, :count] = g_in.astype(BF16)
    gother_ref[:, count : 2 * count] = g_out.astype(BF16)
    gother_ref[:, 2 * count :] = g_bias.astype(BF16)
    g_in, g_out, g_bias = process(own_in, False)
    gext[...] = g_bias
    for at, ref in zip(spans, own_out):
        ref[:, :count] = g_in[at].astype(BF16)
        ref[:, count : 2 * count] = g_out[at].astype(BF16)

    agrad = grad_acc[...]
    norm = normal[...]
    scaled = agrad * gains[:, 1:2]
    first = jnp.mean(scaled, axis=0, keepdims=True)
    second = jnp.mean(scaled * norm, axis=0, keepdims=True)
    mgrad = (scaled - first - norm * second) * inv
    summed = sum_acc[...]
    for d in range(devices):
        both_ref[d, 0] = mgrad[d * channels : (d + 1) * channels].astype(BF16)
        both_ref[d, 1] = summed[d * channels : (d + 1) * channels].astype(BF16)
    lane = lane_of(count)
    tile = jnp.where(lane == 1, jnp.sum(agrad * norm, axis=1, keepdims=True), 0.0)
    tile = jnp.where(lane == 2, jnp.sum(agrad, axis=1, keepdims=True), tile)
    for d in range(devices):
        part = tile[d * channels : (d + 1) * channels]
        if channels < deep:
            part = jnp.concatenate([part, jnp.zeros((deep - channels, LANES), F32)], axis=0)
        gext[pl.ds(spots[d], deep), :] += part
    for at, ref in zip(spans, own_out):
        ref[:, 2 * count :] = gext[at].astype(BF16)


def whole(shape):
    return pl.BlockSpec(shape, lambda i: (0,) * len(shape))


def params(mebibytes):
    return pltpu.CompilerParams(vmem_limit_bytes=mebibytes << 20)


def cost(micros):
    return pl.CostEstimate(flops=0, transcendentals=0, bytes_accessed=micros * 3_000_000)


def join(deep, arrays, count):
    full = pl.BlockSpec(memory_space=pltpu.VMEM)
    width = arrays[0].shape[1]
    return pl.pallas_call(
        partial(join_kernel, len(arrays)),
        out_shape=[
            jax.ShapeDtypeStruct((deep, width), BF16 if i else F32) for i in range(count)
        ],
        in_specs=[full] * len(arrays),
        out_specs=[full] * count,
        compiler_params=params(8),
        cost_estimate=cost(1),
        name="join",
    )(*arrays)


def relay(*arrays):
    full = pl.BlockSpec(memory_space=pltpu.VMEM)
    shape = jax.ShapeDtypeStruct(arrays[0].shape, BF16)
    return pl.pallas_call(
        relay_kernel,
        out_shape=(shape, shape),
        in_specs=[full] * 5,
        out_specs=(full, full),
        compiler_params=params(8),
        cost_estimate=cost(1),
        name="relay",
    )(*arrays)


SMEM = pl.BlockSpec(memory_space=pltpu.SMEM)


def per_device(
    ch, features, cotangent, heights, widths, step_height, rate_height, readout_height,
    step_width, rate_width, readout_width, skip_gain, norm_gain, norm_shift, in_weight,
    in_bias, out_weight, out_bias, layer_scale,
):
    channels, cells = features.shape
    count = in_weight.shape[0]
    pin = lambda v: pltpu.with_memory_space_constraint(v, pltpu.HBM)
    units = in_weight.shape[1]
    states = rate_height.shape[1]
    images = cells // CELLS
    tokens = cells // ch
    parts = CELLS // tokens
    far = 4
    near = ch // far
    deep = -(-(units // 2) // 16) * 16
    width = 2 * count + LANES
    near_groups = [[f * near + i for i in range(near)] for f in range(far)]
    row = lambda v: v.reshape(1, -1)
    exchange = lambda v: lax.ppermute(v, "img", [(0, 1), (1, 0)])
    flip = lambda v, bits: lax.ppermute(v, "ch", [(i, i ^ bits) for i in range(ch)])
    swap = lambda v, groups=None: lax.all_to_all(
        v, "ch", split_axis=0, concat_axis=0, tiled=True, axis_index_groups=groups
    )
    pair = lambda *arrays: lax.optimization_barrier(arrays)
    half = lax.axis_index("img").astype(jnp.int32)
    place = lax.axis_index("ch").astype(jnp.int32)
    full = pl.BlockSpec(memory_space=pltpu.VMEM)

    pack = pl.pallas_call(
        pack_kernel,
        out_shape=jax.ShapeDtypeStruct((deep, width), BF16),
        in_specs=[SMEM] + [full] * 5,
        out_specs=full,
        compiler_params=params(4),
        cost_estimate=cost(2),
        name="pack",
    )(
        half.reshape(1), pin(in_weight.T), pin(out_weight), pin(row(in_bias)), pin(row(norm_gain)),
        pin(row(norm_shift)),
    )
    pack, features_after = lax.optimization_barrier((pack, features))
    shards = [pack] + [flip(pack, bits * near) for bits in range(1, far)]

    groups = -(-channels // SLOT)
    slots = pltpu.VMEM((groups, images * TILES * SLOT, LANES), F32)
    square = (SLOT * SIDE, images // PER * LANES)
    toeplitz = pltpu.VMEM((SLOT * SIDE, SLOT * SIDE), BF16)
    both_shape = (ch, 2, channels, tokens)
    given, taps = pl.pallas_call(
        forward_kernel,
        out_shape=(
            jax.ShapeDtypeStruct(both_shape, BF16),
            jax.ShapeDtypeStruct((groups * SLOT, LANES), F32),
        ),
        in_specs=[SMEM, SMEM] + [full] * 10,
        out_specs=(full, full),
        scratch_shapes=[
            slots, toeplitz, toeplitz, pltpu.VMEM(square, BF16), pltpu.VMEM(square, F32),
        ],
        compiler_params=params(12),
        cost_estimate=cost(6),
        name="mixer_forward",
    )(
        pin(heights), pin(widths), pin(features_after), pin(cotangent), pin(row(layer_scale)),
        pin(row(step_height)), pin(row(step_width)), pin(rate_height), pin(rate_width),
        pin(readout_height), pin(readout_width), pin(row(skip_gain)),
    )
    given, *shards = lax.optimization_barrier((given, *shards))
    given = swap(given)
    shard = jnp.concatenate(shards, axis=0)
    if near == 4:
        cut = far * deep // 2
        beside, above = pair(flip(shard, 1), flip(shard, 2))
        own = [shard, beside, above, flip(beside[:cut], 2), flip(above[cut:], 1)]
        where = jnp.stack([place // near, place % near])
    else:
        own = [swap(jnp.broadcast_to(shard[None], (near,) + shard.shape), near_groups)]
        own = [own[0].reshape(ch * deep, width)]
        where = jnp.stack([place // near, place * 0])
    other = [exchange(piece) for piece in own]

    rows = ch * deep
    pieces = len(own)
    outs = pl.pallas_call(
        partial(mlp_kernel, near, pieces),
        out_shape=[jax.ShapeDtypeStruct(both_shape, BF16)]
        + [jax.ShapeDtypeStruct(piece.shape, BF16) for piece in own]
        + [jax.ShapeDtypeStruct((rows, width), BF16)],
        in_specs=[SMEM] + [full] * (2 * pieces + 1),
        out_specs=[full] * (pieces + 2),
        scratch_shapes=[
            pltpu.VMEM((count, tokens), BF16),
            pltpu.VMEM((count, tokens), BF16),
            pltpu.VMEM((count, tokens), F32),
            pltpu.VMEM((count, LANES), F32),
            pltpu.VMEM((count, tokens), F32),
            pltpu.VMEM((count, tokens), F32),
            pltpu.VMEM((rows, LANES), F32),
            pltpu.VMEM((rows, LANES), F32),
        ],
        compiler_params=params(24),
        cost_estimate=cost(8),
        name="mlp",
    )(where, given, *map(pin, own), *map(pin, other))
    both, gown, gother = outs[0], outs[1:-1], outs[-1]

    arrived = exchange(gother)
    both = swap(both)
    tall = far * deep
    if near == 4:
        cut = tall // 2
        add = lambda v, at: (v.astype(F32) + arrived[at : at + v.shape[0]].astype(F32)).astype(BF16)
        one, two = pair(add(gown[3], 3 * tall), add(gown[4], 3 * tall + cut))
        one, two = pair(flip(one, 2), flip(two, 1))
        one, two = relay(gown[1], gown[2], arrived, one, two)
        first, second, *sent = gown[0], arrived, flip(one, 1), flip(two, 2)
    else:
        total = (gown[0].astype(F32) + arrived.astype(F32)).astype(BF16)
        sent = list(swap(total.reshape(near, tall, width), near_groups))
        first, second, *sent = sent
    landed = [first, second, *sent]
    result, grad_features, small = pl.pallas_call(
        backward_kernel,
        out_shape=(
            jax.ShapeDtypeStruct((channels, cells), BF16),
            jax.ShapeDtypeStruct((channels, cells), F32),
            jax.ShapeDtypeStruct((channels, LANES), F32),
        ),
        in_specs=[SMEM, SMEM] + [full] * 6,
        out_specs=(full,) * 3,
        scratch_shapes=[
            slots, slots, toeplitz, toeplitz, pltpu.VMEM(square, BF16), pltpu.VMEM(square, BF16),
            pltpu.VMEM((SLOT * SIDE, max(SLOT * SIDE, square[1])), F32), pltpu.VMEM(square, BF16),
            pltpu.VMEM(square, BF16), pltpu.VMEM(square, F32),
            pltpu.VMEM((groups * SLOT, LANES), F32),
        ],
        compiler_params=params(16),
        cost_estimate=cost(7),
        name="mixer_backward",
    )(
        pin(heights), pin(widths), pin(features), pin(cotangent), both, taps,
        pin(row(layer_scale)), pin(row(out_bias)),
    )

    *landed, small = lax.optimization_barrier((*landed, small))
    shards = join(deep, landed, far)
    shards = [shards[0]] + [flip(v, (i + 1) * near) for i, v in enumerate(shards[1:])]
    vector_out = jax.ShapeDtypeStruct((1, channels), F32)
    state_out = jax.ShapeDtypeStruct((channels, states), F32)
    chained = pl.pallas_call(
        chain_kernel,
        out_shape=(
            vector_out, state_out, state_out, vector_out, state_out, state_out,
            vector_out, vector_out, vector_out,
        ),
        in_specs=[full] * 9,
        out_specs=(full,) * 9,
        compiler_params=params(4),
        cost_estimate=cost(2),
        name="mixer_chain",
    )(
        small, exchange(small), pin(row(step_height)), pin(row(step_width)), pin(rate_height),
        pin(rate_width), pin(readout_height), pin(readout_width), pin(row(layer_scale)),
    )
    *shards, chained = lax.optimization_barrier((*shards, chained))
    gstep_h, grate_h, gread_h, gstep_w, grate_w, gread_w, gskip, gbias, gscale = chained
    (mine,) = join(deep, shards, 1)
    ggain, gshift, gin, ginb, gout = pl.pallas_call(
        finish_kernel,
        out_shape=(
            vector_out, vector_out, jax.ShapeDtypeStruct((units, count), F32),
            jax.ShapeDtypeStruct((1, units), F32), jax.ShapeDtypeStruct((units, count), F32),
        ),
        in_specs=[SMEM, full, full],
        out_specs=(full,) * 5,
        compiler_params=params(4),
        cost_estimate=cost(1),
        name="finish",
    )(half.reshape(1), mine, exchange(mine))
    flat = lambda v: v.reshape(-1)
    return (
        result, grad_features, flat(gstep_h), grate_h, gread_h, flat(gstep_w), grate_w, gread_w,
        flat(gskip), flat(ggain), flat(gshift), gin.T, flat(ginb), gout, flat(gbias),
        flat(gscale),
    )


def solution(mesh):
    wide, split, tall = P("ch", "img"), P("ch"), P("ch", None)
    return jax.shard_map(
        partial(per_device, mesh.shape["ch"]),
        mesh=mesh,
        in_specs=(
            wide, wide, P("img"), P("img"), split, tall, tall, split, tall, tall, split, split,
            split, P(None, "ch"), split, tall, split, split,
        ),
        out_specs=(
            wide, wide, split, tall, tall, split, tall, tall, split, split, split,
            P(None, "ch"), split, tall, split, split,
        ),
        check_vma=False,
    )
```

```python
import math
from functools import partial

import jax
import jax.numpy as jnp
from jax import lax
from jax.experimental import pallas as pl
from jax.experimental.pallas import tpu as pltpu
from jax.sharding import PartitionSpec as P

SIDE = 32
CELLS = SIDE * SIDE
LANES = 128
PER = LANES // SIDE
SLOT = 8
TILES = CELLS // LANES
EPS = 1e-06
F32 = jnp.float32
BF16 = jnp.bfloat16


def column(row):
    n = row.shape[1]
    eye = lax.broadcasted_iota(jnp.int32, (n, n), 0) == lax.broadcasted_iota(jnp.int32, (n, n), 1)
    return jnp.sum(jnp.where(eye, jnp.broadcast_to(row, (n, n)), 0.0), axis=1, keepdims=True)


def as_row(col):
    n = col.shape[0]
    eye = lax.broadcasted_iota(jnp.int32, (n, n), 0) == lax.broadcasted_iota(jnp.int32, (n, n), 1)
    return jnp.sum(jnp.where(eye, jnp.broadcast_to(col, (n, n)), 0.0), axis=0, keepdims=True)


def image_mask(rows, height, width):
    cell = lax.broadcasted_iota(jnp.int32, (rows, CELLS), 1)
    return (cell // SIDE < height) & (cell % SIDE < width)


def lane_of(rows):
    return lax.broadcasted_iota(jnp.int32, (rows, LANES), 1)


def fill_slots(slots, value, image):
    channels = value.shape[0]
    for group in range(slots.shape[0]):
        live = min(SLOT, channels - group * SLOT)
        for k in range(TILES):
            at = (image * TILES + k) * SLOT
            part = value[group * SLOT : group * SLOT + live, k * LANES : (k + 1) * LANES]
            slots[group, pl.ds(at, live), :] = part


def read_slots(slots, image, channels):
    rows = []
    for group in range(slots.shape[0]):
        live = min(SLOT, channels - group * SLOT)
        at = [(image * TILES + k) * SLOT for k in range(TILES)]
        rows.append(jnp.concatenate([slots[group, pl.ds(a, live), :] for a in at], axis=1))
    return jnp.concatenate(rows, axis=0) if len(rows) > 1 else rows[0]


def cross(tiles, lane):
    for bit, far in ((2, 64), (1, 32)):
        low = (lane & far) == 0
        out = list(tiles)
        for k in range(len(tiles)):
            if not k & bit:
                one, two = tiles[k], tiles[k | bit]
                out[k] = jnp.where(low, one, pltpu.roll(two, far, 1))
                out[k | bit] = jnp.where(low, pltpu.roll(one, LANES - far, 1), two)
        tiles = out
    return tiles


def load_channel(slots, group, c, lane):
    count = slots.shape[1] // SLOT
    value = slots[group, pl.ds(c, count, stride=SLOT), :]
    return cross([value[k * SLOT : (k + 1) * SLOT] for k in range(count // SLOT)], lane)


def store_channel(slots, group, c, tiles, lane):
    count = slots.shape[1] // SLOT
    slots[group, pl.ds(c, count, stride=SLOT), :] = jnp.concatenate(cross(tiles, lane), axis=0)


def split(value):
    high = value.astype(BF16)
    return high, (value - high.astype(F32)).astype(BF16)


def pick(row, index):
    spread = jnp.broadcast_to(row, index.shape)
    value = jnp.take_along_axis(spread, jnp.clip(index, 0, LANES - 1), axis=1)
    return value


def build_down(row, c, high_ref, low_ref, lane, sub):
    place = lane % SIDE
    source = (place % TILES) * PER + place // TILES
    here = lane // SIDE == c % PER
    parts = []
    for turn in range(PER):
        index = PER * sub + turn - source
        parts.append(jnp.where(here & (index >= 0), pick(row, index), 0.0))
    high, low = split(jnp.concatenate(parts, axis=0))
    at = (slice(c * SIDE, (c + 1) * SIDE), slice(c // PER * LANES, (c // PER + 1) * LANES))
    high_ref[at] = high
    low_ref[at] = low


def build_across(row, turned, lane, sub):
    place = lane % SIDE
    highs, lows = [], []
    for part in range(PER):
        own = part * SLOT + sub
        index = own - place if turned else place - own
        value = jnp.where(index >= 0, pick(row, index + SIDE), 0.0)
        high = value.astype(BF16).astype(F32)
        highs.append(high)
        lows.append(value - high)
    spread = lambda parts: jnp.concatenate(
        [jnp.where(lane // SIDE == i, p, 0.0) for i in range(PER) for p in parts], axis=0
    ).astype(BF16)
    return spread(highs), spread(lows)


def taps_of(step_h, step_w, rate_h, rate_w, read_h, read_w, skip_ref):
    channels = rate_h.shape[0]
    lane = lane_of(channels)
    kept = jnp.zeros((channels, LANES), F32)
    decay_h = jnp.exp(column(step_h[...])) * rate_h[...]
    decay_w = jnp.exp(column(step_w[...])) * rate_w[...]
    for lag in range(SIDE):
        tap = jnp.sum(read_h[...] * jnp.exp(-decay_h * lag), axis=1, keepdims=True)
        kept = jnp.where(lane == lag, tap, kept)
        tap = jnp.sum(read_w[...] * jnp.exp(-decay_w * lag), axis=1, keepdims=True)
        kept = jnp.where(lane == SIDE + lag, tap, kept)
    return jnp.where(lane == 2 * SIDE, column(skip_ref[...]), kept)


def dot(a, b, dims=(((1,), (0,)), ((), ()))):
    return lax.dot_general(a, b, dims, preferred_element_type=F32)


NT = (((1,), (1,)), ((), ()))
TN = (((0,), (0,)), ((), ()))


def forward_kernel(
    heights, widths, feat_ref, cot_ref, scale_ref, step_h, step_w, rate_h, rate_w, read_h,
    read_w, skip_ref, out_ref, rows_ref, slots, high_a, low_a, field, tall,
):
    channels, cells = feat_ref.shape
    images = cells // CELLS
    rows_ref[0:channels] = taps_of(step_h, step_w, rate_h, rate_w, read_h, read_w, skip_ref)
    for ref in (high_a, low_a, field):
        ref[...] = jnp.zeros_like(ref)
    for image in range(images):
        inside = image_mask(1, heights[image], widths[image])
        value = feat_ref[:, image * CELLS : (image + 1) * CELLS].astype(F32)
        fill_slots(slots, jnp.where(inside, value, 0.0), image)
    live = min(SLOT, channels)
    sides = images // PER

    def body(group, carry):
        lane = lane_of(SLOT)
        sub = lax.broadcasted_iota(jnp.int32, (SLOT, LANES), 0)
        for c in range(live):
            row = rows_ref[pl.ds(group * SLOT + c, 1), :]
            build_down(row, c, high_a, low_a, lane, sub)
            tiles = load_channel(slots, group, c, lane)
            for s in range(sides):
                value = jnp.concatenate(tiles[s * PER : (s + 1) * PER], axis=0)
                field[c * SIDE : (c + 1) * SIDE, s * LANES : (s + 1) * LANES] = value.astype(BF16)
        source = field[...]
        tall[...] = dot(high_a[...], source) + dot(low_a[...], source)
        for c in range(live):
            row = rows_ref[pl.ds(group * SLOT + c, 1), :]
            high_b, low_b = build_across(row, False, lane, sub)
            value = jnp.concatenate(
                [tall[c * SIDE : (c + 1) * SIDE, s * LANES : (s + 1) * LANES] for s in range(sides)],
                axis=0,
            )
            high, low = split(value)
            value = dot(
                jnp.concatenate([high, low, high], axis=1),
                jnp.concatenate([high_b, high_b, low_b], axis=0),
            )
            tiles = [value[k * SLOT : (k + 1) * SLOT] for k in range(images)]
            store_channel(slots, group, c, tiles, lane)
        return carry

    lax.fori_loop(0, slots.shape[0], body, 0)
    wide = out_ref.shape[3]
    parts = CELLS // wide
    skip = rows_ref[0:channels, 2 * SIDE : 2 * SIDE + 1]
    scale = column(scale_ref[...])
    for image in range(images):
        span = slice(image * CELLS, (image + 1) * CELLS)
        inside = image_mask(1, heights[image], widths[image])
        value = read_slots(slots, image, channels) + skip * feat_ref[:, span].astype(F32)
        value = jnp.where(inside, value, 0.0).astype(BF16)
        down = cot_ref[:, span].astype(F32) * scale
        down = jnp.where(inside, down, 0.0).astype(BF16)
        for j in range(parts):
            out_ref[image * parts + j, 0] = value[:, j * wide : (j + 1) * wide]
            out_ref[image * parts + j, 1] = down[:, j * wide : (j + 1) * wide]


def backward_kernel(
    heights, widths, feat_ref, cot_ref, both_ref, rows_ref, scale_ref, bias_ref,
    step_h, step_w, rate_h, rate_w, read_h, read_w, result_ref, gfeat_ref, small_ref,
    slots, slots_g, high_a, low_a, field, field_g, tall, high_d, low_d, wide_ref, sums,
):
    channels, cells = feat_ref.shape
    images = cells // CELLS
    live = min(SLOT, channels)
    sides = images // PER
    wide = both_ref.shape[3]
    parts = CELLS // wide
    for ref in (high_a, low_a, sums, field, field_g, high_d, low_d):
        ref[...] = jnp.zeros_like(ref)
    lane_c = lane_of(channels)
    scale = column(scale_ref[...])
    bias = column(bias_ref[...])
    small = jnp.zeros((channels, LANES), F32)
    for image in range(images):
        span = slice(image * CELLS, (image + 1) * CELLS)
        inside = image_mask(1, heights[image], widths[image])
        values = feat_ref[:, span].astype(F32)
        masked = jnp.where(inside, values, 0.0)
        fill_slots(slots, masked, image)
        grad = jnp.concatenate(
            [both_ref[image * parts + j, 0].astype(F32) for j in range(parts)], axis=1
        )
        grad = jnp.where(inside, grad, 0.0)
        fill_slots(slots_g, grad, image)
        shifted = jnp.concatenate(
            [both_ref[image * parts + j, 1].astype(F32) for j in range(parts)], axis=1
        )
        shifted = shifted + bias
        result = values + jnp.where(inside, scale * shifted, 0.0)
        result_ref[:, span] = result.astype(BF16)
        weighted = jnp.where(inside, cot_ref[:, span].astype(F32), 0.0)
        small = small + jnp.where(
            lane_c == 64,
            jnp.sum(grad * masked, axis=1, keepdims=True),
            jnp.where(
                lane_c == 65,
                jnp.sum(weighted * shifted, axis=1, keepdims=True),
                jnp.where(lane_c == 66, jnp.sum(weighted, axis=1, keepdims=True), 0.0),
            ),
        )

    def body(group, carry):
        lane = lane_of(SLOT)
        sub = lax.broadcasted_iota(jnp.int32, (SLOT, LANES), 0)
        place = lane % SIDE
        half = lambda ref, c, s: ref[c * SIDE : (c + 1) * SIDE, s * LANES : (s + 1) * LANES]
        stack = lambda ref, c: jnp.concatenate([half(ref, c, s) for s in range(sides)], axis=0)
        for c in range(live):
            row = rows_ref[pl.ds(group * SLOT + c, 1), :]
            build_down(row, c, high_a, low_a, lane, sub)
            for slot, out in ((slots, field), (slots_g, field_g)):
                tiles = load_channel(slot, group, c, lane)
                for s in range(sides):
                    value = jnp.concatenate(tiles[s * PER : (s + 1) * PER], axis=0)
                    at = (slice(c * SIDE, (c + 1) * SIDE), slice(s * LANES, (s + 1) * LANES))
                    out[at] = value.astype(BF16)
        source = field[...]
        tall[...] = dot(high_a[...], source) + dot(low_a[...], source)
        for c in range(live):
            row = rows_ref[pl.ds(group * SLOT + c, 1), :]
            high_b, low_b = build_across(row, True, lane, sub)
            grad = stack(field_g, c)
            flow = dot(
                jnp.concatenate([grad, grad], axis=1), jnp.concatenate([high_b, low_b], axis=0)
            )
            high, low = split(flow)
            for s in range(sides):
                at = (slice(c * SIDE, (c + 1) * SIDE), slice(s * LANES, (s + 1) * LANES))
                high_d[at] = high[s * SIDE : (s + 1) * SIDE]
                low_d[at] = low[s * SIDE : (s + 1) * SIDE]
            high, low = split(stack(tall, c))
            outer = dot(
                jnp.concatenate([grad, grad], axis=0), jnp.concatenate([high, low], axis=0), TN
            )
            total = None
            for part in range(PER):
                value = None
                for i in range(PER):
                    at = i * SIDE + part * SLOT
                    term = jnp.where(lane // SIDE == i, outer[at : at + SLOT], 0.0)
                    value = term if value is None else value + term
                index = part * SLOT + sub - place
                value = jnp.take_along_axis(
                    value, jnp.clip(index, 0, SIDE - 1) + lane // SIDE * SIDE, axis=1
                )
                value = jnp.where(index >= 0, value, 0.0)
                total = value if total is None else total + value
            total = jnp.sum(total, axis=0, keepdims=True)
            total = total + pltpu.roll(total, 64, 1)
            total = total + pltpu.roll(total, 32, 1)
            sums[pl.ds(group * SLOT + c, 1), :] = jnp.where(lane[0:1] // SIDE == 1, total, 0.0)
        high, low = high_d[...], low_d[...]
        back = dot(high_a[...], high, TN) + dot(high_a[...], low, TN) + dot(low_a[...], high, TN)
        wide_ref[...] = back
        outer = dot(high, source, NT) + dot(low, source, NT)
        tall[...] = outer
        for c in range(live):
            value = stack(wide_ref, c)
            tiles = [value[k * SLOT : (k + 1) * SLOT] for k in range(images)]
            store_channel(slots, group, c, tiles, lane)
            total = None
            for turn in range(PER):
                at = c * SIDE + turn * SLOT
                value = tall[at : at + SLOT, c // PER * LANES : (c // PER + 1) * LANES]
                index = PER * sub + turn - lane
                safe = jnp.clip(index, 0, SIDE - 1)
                index_at = (safe % PER) * TILES + safe // PER + c % PER * SIDE
                value = jnp.take_along_axis(value, index_at, axis=1)
                value = jnp.where(index >= 0, value, 0.0)
                total = value if total is None else total + value
            total = jnp.sum(total, axis=0, keepdims=True)
            total = jnp.where(lane[0:1] < SIDE, total, 0.0)
            sums[pl.ds(group * SLOT + c, 1), :] += total
        return carry

    lax.fori_loop(0, slots.shape[0], body, 0)
    skip = rows_ref[0:channels, 2 * SIDE : 2 * SIDE + 1]
    for image in range(images):
        span = slice(image * CELLS, (image + 1) * CELLS)
        inside = image_mask(1, heights[image], widths[image])
        grad = read_slots(slots_g, image, channels)
        value = read_slots(slots, image, channels) + skip * grad
        gfeat_ref[:, span] = cot_ref[:, span].astype(F32) + jnp.where(inside, value, 0.0)
    small = small + sums[0:channels]
    states, small = chain(small, step_h, step_w, rate_h, rate_w, read_h, read_w)
    for index in range(2):
        pair = jnp.concatenate(states[2 * index : 2 * index + 2], axis=1)
        small_ref[:, index * pair.shape[1] : (index + 1) * pair.shape[1]] = pair
    small_ref[:, 2 * pair.shape[1] :] = small


def chain(total, step_h, step_w, rate_h, rate_w, read_h, read_w):
    out, tail = [], total
    lane = lane_of(total.shape[0])
    for place, first, step, rate, read in (
        (67, 0, step_h, rate_h, read_h), (68, SIDE, step_w, rate_w, read_w),
    ):
        pace = jnp.exp(column(step[...]))
        decay = pace * rate[...]
        to_read = jnp.zeros_like(decay)
        to_decay = jnp.zeros_like(decay)
        for lag in range(SIDE):
            term = total[:, first + lag : first + lag + 1] * jnp.exp(-decay * lag)
            to_read = to_read + term
            if lag:
                to_decay = to_decay - float(lag) * term
        to_decay = to_decay * read[...]
        out += [to_read, pace * to_decay]
        tail = jnp.where(lane == place, jnp.sum(to_decay * decay, axis=1, keepdims=True), tail)
    return out, tail


def join_kernel(count, *refs):
    given, outs = refs[:count], refs[count:]
    tall = outs[0].shape[0]
    for index, out in enumerate(outs):
        at = slice(index * tall, (index + 1) * tall)
        total = given[0][at].astype(F32)
        for ref in given[1:]:
            total = total + ref[at].astype(F32)
        out[...] = total.astype(out.dtype)


def cut_kernel(one_ref, two_ref, first_ref, second_ref):
    cut = first_ref.shape[0]
    first_ref[...] = one_ref[:cut]
    second_ref[...] = two_ref[cut:]


def relay_kernel(one_ref, two_ref, arrived_ref, first_ref, second_ref, out_one, out_two):
    tall = one_ref.shape[0]
    cut = tall // 2
    one = one_ref[...].astype(F32) + arrived_ref[tall : 2 * tall].astype(F32)
    two = two_ref[...].astype(F32) + arrived_ref[2 * tall : 3 * tall].astype(F32)
    out_one[:cut] = (one[:cut] + first_ref[...].astype(F32)).astype(BF16)
    out_one[cut:] = one[cut:].astype(BF16)
    out_two[:cut] = two[:cut].astype(BF16)
    out_two[cut:] = (two[cut:] + second_ref[...].astype(F32)).astype(BF16)


def finish_kernel(
    half, mine_ref, other_ref, small_ref, sibling_ref, scale_ref,
    gstep_h, grate_h, gread_h, gstep_w, grate_w, gread_w, gskip, ggain, gshift, gin, ginb, gout,
    gbias, gscale,
):
    units, count = gin.shape
    channels, states = grate_h.shape
    keep = units // 2
    first = half[0] == 0
    mine, other = mine_ref[...], other_ref[...]
    low = jnp.where(first, mine, other)[:keep]
    high = jnp.where(first, other, mine)[:keep]
    for at, part in ((0, low), (keep, high)):
        gin[at : at + keep] = part[:, :count]
        gout[at : at + keep] = part[:, count : 2 * count]
    bias = jnp.concatenate([low[:, 2 * count :], high[:, 2 * count :]], axis=0)
    ginb[...] = as_row(bias[:, 0:1])
    norms = (mine[:, 2 * count :] + other[:, 2 * count :])[:channels]
    ggain[...] = as_row(norms[:, 1:2])
    gshift[...] = as_row(norms[:, 2:3])
    total = small_ref[...] + sibling_ref[...]
    for index, ref in enumerate((gread_h, grate_h, gread_w, grate_w)):
        ref[...] = total[:, index * states : (index + 1) * states]
    total = total[:, 4 * states :]
    gskip[...] = as_row(total[:, 64:65])
    gscale[...] = as_row(total[:, 65:66])
    gbias[...] = as_row(total[:, 66:67]) * scale_ref[...]
    gstep_h[...] = as_row(total[:, 67:68])
    gstep_w[...] = as_row(total[:, 68:69])


def pack_kernel(half, in_ref, out_ref, bias_ref, gain_ref, shift_ref, pack_ref):
    deep = pack_ref.shape[0]
    own, count = out_ref.shape
    channels = gain_ref.shape[1]
    keep = own // 2
    row = lax.broadcasted_iota(jnp.int32, (deep, own), 0)
    col = lax.broadcasted_iota(jnp.int32, (deep, own), 1)
    pick = jnp.where((col == row + half[0] * keep) & (row < keep), 1.0, 0.0).astype(BF16)
    nt = (((1,), (1,)), ((), ()))
    first = jnp.dot(pick, in_ref[...], preferred_element_type=F32)
    second = jnp.dot(pick, out_ref[...], preferred_element_type=F32)
    bias = jnp.broadcast_to(bias_ref[...], (LANES, own))
    third = lax.dot_general(pick, bias, nt, preferred_element_type=F32)
    row = lax.broadcasted_iota(jnp.int32, (deep, channels), 0)
    col = lax.broadcasted_iota(jnp.int32, (deep, channels), 1)
    pick = jnp.where(col == row, 1.0, 0.0).astype(BF16)
    gain = jnp.broadcast_to(gain_ref[...], (LANES, channels))
    gain = lax.dot_general(pick, gain, nt, preferred_element_type=F32)
    shift = jnp.broadcast_to(shift_ref[...], (LANES, channels))
    shift = lax.dot_general(pick, shift, nt, preferred_element_type=F32)
    lane = lane_of(deep)
    third = jnp.where(lane == 0, third, jnp.where(lane == 1, gain, jnp.where(lane == 2, shift, 0.0)))
    pack_ref[:, :count] = first.astype(BF16)
    pack_ref[:, count : 2 * count] = second.astype(BF16)
    pack_ref[:, 2 * count :] = third.astype(BF16)


ROOT = math.sqrt(2.0 / math.pi)


def perceptron(refs, act, down):
    count = act.shape[0]
    w_in = jnp.concatenate([ref[:, :count] for ref in refs], axis=0)
    w_out = jnp.concatenate([ref[:, count : 2 * count] for ref in refs], axis=0)
    bias = jnp.concatenate([ref[:, 2 * count :] for ref in refs], axis=0).astype(F32)[:, 0:1]
    v = dot(w_in, act) + bias
    square = v * v
    half = 0.5 * jnp.tanh(v * (ROOT * 0.044715 * square + ROOT)) + 0.5
    full = v * half
    hidden = full.astype(BF16)
    slope = half + full * (1.0 - half) * (6.0 * ROOT * 0.044715 * square + 2.0 * ROOT)
    low = (dot(w_out, down) * slope).astype(BF16)
    g_bias = jnp.sum(low.astype(F32), axis=1, keepdims=True)
    g_bias = jnp.where(lane_of(low.shape[0]) == 0, g_bias, 0.0)
    grads = (dot(low, act, NT), dot(hidden, down, NT), g_bias)
    return dot(w_out, hidden, TN), dot(w_in, low, TN), grads


def put(ref, grads, start):
    count = grads[0].shape[1]
    at = slice(start, start + ref.shape[0])
    ref[:, :count] = grads[0][at].astype(BF16)
    ref[:, count : 2 * count] = grads[1][at].astype(BF16)
    ref[:, 2 * count :] = grads[2][at].astype(BF16)
    return start + ref.shape[0]


def spots_of(near, devices, deep, where_ref):
    z, xy = where_ref[0], where_ref[1]
    for d in range(devices):
        spot = ((d % near) ^ xy) * (devices // near) + ((d // near) ^ z)
        yield d, pl.multiple_of(spot * deep, deep)


def mlp_first(near, pieces, where_ref, given_ref, *refs):
    own_in, refs = refs[:pieces], refs[pieces:]
    other_in, refs = refs[:pieces], refs[pieces:]
    gother_ref, active, downs, normal, inv_ref, gains, sum_ref, grad_ref, ext = refs
    devices, _, channels, _ = given_ref.shape
    deep = ext.shape[0] // devices
    count = active.shape[0]

    value = jnp.concatenate([given_ref[d, 0].astype(F32) for d in range(devices)], axis=0)
    mean = jnp.mean(value, axis=0, keepdims=True)
    value = value - mean
    inv = lax.rsqrt(jnp.mean(value * value, axis=0, keepdims=True) + EPS)
    value = value * inv
    normal[...] = value
    inv_ref[...] = inv
    down = jnp.concatenate([given_ref[d, 1].astype(F32) for d in range(devices)], axis=0)
    downs[...] = down.astype(BF16)
    at = 0
    for ref in own_in:
        ext[at : at + ref.shape[0]] = ref[:, 2 * count :].astype(F32)
        at += ref.shape[0]
    for d, spot in spots_of(near, devices, deep, where_ref):
        gains[d * channels : (d + 1) * channels] = ext[pl.ds(spot, deep), :][:channels]
    active[...] = (value * gains[:, 1:2] + gains[:, 2:3]).astype(BF16)
    sums, total, grads = perceptron(other_in, active[...], downs[...])
    put(gother_ref, grads, 0)
    sum_ref[...] = sums
    grad_ref[...] = total


def mlp_second(
    near, pieces, where_ref, active, downs, normal_ref, inv_ref, gains, sum_ref, grad_ref, *refs
):
    own_in, refs = refs[:pieces], refs[pieces:]
    both_ref, refs = refs[0], refs[1:]
    own_out, (gext,) = refs[:pieces], refs[pieces:]
    count = active.shape[0]
    devices, _, channels, _ = both_ref.shape
    deep = gext.shape[0] // devices

    sums, total, grads = perceptron(own_in, active[...], downs[...])
    gext[...] = grads[2]
    start = 0
    for ref in own_out:
        start = put(ref, grads, start)
    summed = sum_ref[...] + sums
    agrad = grad_ref[...] + total
    norm = normal_ref[...]
    scaled = agrad * gains[:, 1:2]
    first = jnp.mean(scaled, axis=0, keepdims=True)
    second = jnp.mean(scaled * norm, axis=0, keepdims=True)
    mgrad = (scaled - first - norm * second) * inv_ref[...]
    for d in range(devices):
        both_ref[d, 0] = mgrad[d * channels : (d + 1) * channels].astype(BF16)
        both_ref[d, 1] = summed[d * channels : (d + 1) * channels].astype(BF16)
    lane = lane_of(count)
    tile = jnp.where(lane == 1, jnp.sum(agrad * norm, axis=1, keepdims=True), 0.0)
    tile = jnp.where(lane == 2, jnp.sum(agrad, axis=1, keepdims=True), tile)
    for d, spot in spots_of(near, devices, deep, where_ref):
        part = tile[d * channels : (d + 1) * channels]
        if channels < deep:
            part = jnp.concatenate([part, jnp.zeros((deep - channels, LANES), F32)], axis=0)
        gext[pl.ds(spot, deep), :] += part
    start = 0
    for ref in own_out:
        ref[:, 2 * count :] = gext[start : start + ref.shape[0]].astype(BF16)
        start += ref.shape[0]


def whole(shape):
    return pl.BlockSpec(shape, lambda i: (0,) * len(shape))


def params(mebibytes):
    return pltpu.CompilerParams(vmem_limit_bytes=mebibytes << 20)


def cost(micros):
    return pl.CostEstimate(flops=0, transcendentals=0, bytes_accessed=micros * 3_000_000)


def join(deep, arrays, count):
    full = pl.BlockSpec(memory_space=pltpu.VMEM)
    width = arrays[0].shape[1]
    return pl.pallas_call(
        partial(join_kernel, len(arrays)),
        out_shape=[
            jax.ShapeDtypeStruct((deep, width), BF16 if i else F32) for i in range(count)
        ],
        in_specs=[full] * len(arrays),
        out_specs=[full] * count,
        compiler_params=params(8),
        cost_estimate=pl.CostEstimate(flops=1 if count > 1 else 1, transcendentals=0, bytes_accessed=1_000_000),
        name="join",
    )(*arrays)


def relay(*arrays):
    full = pl.BlockSpec(memory_space=pltpu.VMEM)
    shape = jax.ShapeDtypeStruct(arrays[0].shape, BF16)
    return pl.pallas_call(
        relay_kernel,
        out_shape=(shape, shape),
        in_specs=[full] * 5,
        out_specs=(full, full),
        compiler_params=params(8),
        cost_estimate=pl.CostEstimate(flops=100_000_000_000, transcendentals=0, bytes_accessed=1_000_000),
        name="relay",
    )(*arrays)


SMEM = pl.BlockSpec(memory_space=pltpu.SMEM)


def per_device(
    ch, features, cotangent, heights, widths, step_height, rate_height, readout_height,
    step_width, rate_width, readout_width, skip_gain, norm_gain, norm_shift, in_weight,
    in_bias, out_weight, out_bias, layer_scale,
):
    channels, cells = features.shape
    count = in_weight.shape[0]
    pin = lambda v: pltpu.with_memory_space_constraint(v, pltpu.HBM)
    units = in_weight.shape[1]
    states = rate_height.shape[1]
    images = cells // CELLS
    tokens = cells // ch
    parts = CELLS // tokens
    far = 4
    near = ch // far
    deep = -(-(units // 2) // 16) * 16
    width = 2 * count + LANES
    near_groups = [[f * near + i for i in range(near)] for f in range(far)]
    row = lambda v: v.reshape(1, -1)
    exchange = lambda v: lax.ppermute(v, "img", [(0, 1), (1, 0)])
    flip = lambda v, bits: lax.ppermute(v, "ch", [(i, i ^ bits) for i in range(ch)])
    swap = lambda v, groups=None: lax.all_to_all(
        v, "ch", split_axis=0, concat_axis=0, tiled=True, axis_index_groups=groups
    )
    pair = lambda *arrays: lax.optimization_barrier(arrays)
    half = lax.axis_index("img").astype(jnp.int32)
    place = lax.axis_index("ch").astype(jnp.int32)
    full = pl.BlockSpec(memory_space=pltpu.VMEM)

    pack = pl.pallas_call(
        pack_kernel,
        out_shape=jax.ShapeDtypeStruct((deep, width), BF16),
        in_specs=[SMEM] + [full] * 5,
        out_specs=full,
        compiler_params=params(4),
        cost_estimate=cost(2),
        name="pack",
    )(
        half.reshape(1), pin(in_weight.T), pin(out_weight), pin(row(in_bias)), pin(row(norm_gain)),
        pin(row(norm_shift)),
    )
    pack, features_after = pair(pack, features)
    shards = [pack] + [flip(pack, bits * near) for bits in range(1, far)]

    groups = -(-channels // SLOT)
    square = (SLOT * SIDE, images // PER * LANES)
    toeplitz = pltpu.VMEM((SLOT * SIDE, SLOT * SIDE), BF16)
    slots = pltpu.VMEM((groups, images * TILES * SLOT, LANES), F32)
    both_shape = (ch, 2, channels, tokens)
    given, taps = pl.pallas_call(
        forward_kernel,
        out_shape=(
            jax.ShapeDtypeStruct(both_shape, BF16),
            jax.ShapeDtypeStruct((groups * SLOT, LANES), F32),
        ),
        in_specs=[SMEM, SMEM] + [full] * 10,
        out_specs=(full, full),
        scratch_shapes=[
            slots, toeplitz, toeplitz, pltpu.VMEM(square, BF16), pltpu.VMEM(square, F32),
        ],
        compiler_params=params(12),
        cost_estimate=cost(6),
        name="mixer_forward",
    )(
        pin(heights), pin(widths), pin(features_after), pin(cotangent), pin(row(layer_scale)),
        pin(row(step_height)), pin(row(step_width)), pin(rate_height), pin(rate_width),
        pin(readout_height), pin(readout_width), pin(row(skip_gain)),
    )
    given, *shards = pair(given, *shards)
    given = swap(given)
    shard = jnp.concatenate(shards, axis=0)
    if near == 4:
        cut = far * deep // 2
        beside, above = pair(flip(shard, 1), flip(shard, 2))
        ends = pl.pallas_call(
            cut_kernel,
            out_shape=[jax.ShapeDtypeStruct((cut, width), BF16)] * 2,
            in_specs=[full] * 2,
            out_specs=[full] * 2,
            compiler_params=params(4),
            cost_estimate=pl.CostEstimate(flops=100_000_000_000, transcendentals=0, bytes_accessed=1_000_000),
            name="ends",
        )(beside, above)
        own = [shard, beside, above, flip(ends[0], 2), flip(ends[1], 1)]
        where = jnp.stack([place // near, place % near])
    else:
        own = [swap(jnp.broadcast_to(shard[None], (near,) + shard.shape), near_groups)]
        own = [own[0].reshape(ch * deep, width)]
        where = jnp.stack([place // near, place * 0])
    other = [exchange(piece) for piece in own]

    rows = ch * deep
    pieces = len(own)
    plane = jax.ShapeDtypeStruct((count, tokens), F32)
    token_low = jax.ShapeDtypeStruct((count, tokens), BF16)
    gother, *state = pl.pallas_call(
        partial(mlp_first, near, pieces),
        out_shape=[
            jax.ShapeDtypeStruct((rows, width), BF16), token_low, token_low, plane,
            jax.ShapeDtypeStruct((1, tokens), F32), jax.ShapeDtypeStruct((count, LANES), F32),
            plane, plane,
        ],
        in_specs=[SMEM] + [full] * (1 + 2 * pieces),
        out_specs=[full] * 8,
        scratch_shapes=[pltpu.VMEM((rows, LANES), F32)],
        compiler_params=params(16),
        cost_estimate=cost(5),
        name="mlp_first",
    )(where, given, *own, *map(pin, other))
    arrived = exchange(gother)
    both, *gown = pl.pallas_call(
        partial(mlp_second, near, pieces),
        out_shape=[jax.ShapeDtypeStruct(both_shape, BF16)]
        + [jax.ShapeDtypeStruct(piece.shape, BF16) for piece in own],
        in_specs=[SMEM] + [full] * (7 + pieces),
        out_specs=[full] * (1 + pieces),
        scratch_shapes=[pltpu.VMEM((rows, LANES), F32)],
        compiler_params=params(16),
        cost_estimate=cost(5),
        name="mlp_second",
    )(where, *state, *own)
    both = swap(both)
    tall = far * deep
    if near == 4:
        cut = tall // 2
        add = lambda v, at: (v.astype(F32) + arrived[at : at + v.shape[0]].astype(F32)).astype(BF16)
        one, two = pair(add(gown[3], 3 * tall), add(gown[4], 3 * tall + cut))
        one, two = pair(flip(one, 2), flip(two, 1))
        one, two = relay(gown[1], gown[2], arrived, one, two)
        first, second, *sent = gown[0], arrived, flip(one, 1), flip(two, 2)
    else:
        total = (gown[0].astype(F32) + arrived.astype(F32)).astype(BF16)
        sent = list(swap(total.reshape(near, tall, width), near_groups))
        first, second, *sent = sent
    landed = [first, second, *sent]
    shards = join(deep, landed, far)
    shards = [shards[0]] + [flip(v, (i + 1) * near) for i, v in enumerate(shards[1:])]
    result, grad_features, small = pl.pallas_call(
        backward_kernel,
        out_shape=(
            jax.ShapeDtypeStruct((channels, cells), BF16),
            jax.ShapeDtypeStruct((channels, cells), F32),
            jax.ShapeDtypeStruct((channels, LANES + 4 * states), F32),
        ),
        in_specs=[SMEM, SMEM] + [full] * 12,
        out_specs=(full,) * 3,
        scratch_shapes=[
            slots, slots, toeplitz, toeplitz, pltpu.VMEM(square, BF16),
            pltpu.VMEM(square, BF16), pltpu.VMEM((SLOT * SIDE, max(SLOT * SIDE, square[1])), F32),
            pltpu.VMEM(square, BF16), pltpu.VMEM(square, BF16), pltpu.VMEM(square, F32),
            pltpu.VMEM((groups * SLOT, LANES), F32),
        ],
        compiler_params=params(16),
        cost_estimate=cost(7),
        name="mixer_backward",
    )(
        pin(heights), pin(widths), pin(features), pin(cotangent), both, taps,
        pin(row(layer_scale)), pin(row(out_bias)), pin(row(step_height)), pin(row(step_width)),
        pin(rate_height), pin(rate_width), pin(readout_height), pin(readout_width),
    )
    *shards, small = pair(*shards, small)
    (mine,) = join(deep, shards, 1)
    vector_out = jax.ShapeDtypeStruct((1, channels), F32)
    state_out = jax.ShapeDtypeStruct((channels, states), F32)
    weight_out = jax.ShapeDtypeStruct((units, count), F32)
    outs = pl.pallas_call(
        finish_kernel,
        out_shape=(
            vector_out, state_out, state_out, vector_out, state_out, state_out, vector_out,
            vector_out, vector_out, weight_out, jax.ShapeDtypeStruct((1, units), F32), weight_out,
            vector_out, vector_out,
        ),
        in_specs=[SMEM] + [full] * 5,
        out_specs=(full,) * 14,
        compiler_params=params(4),
        cost_estimate=cost(1),
        name="finish",
    )(half.reshape(1), mine, exchange(mine), small, exchange(small), pin(row(layer_scale)))
    outs = [v.reshape(-1) if v.shape[0] == 1 else v for v in outs]
    outs[9] = outs[9].T
    return (result, grad_features, *outs)


def solution(mesh):
    wide, split, tall = P("ch", "img"), P("ch"), P("ch", None)
    return jax.shard_map(
        partial(per_device, mesh.shape["ch"]),
        mesh=mesh,
        in_specs=(
            wide, wide, P("img"), P("img"), split, tall, tall, split, tall, tall, split, split,
            split, P(None, "ch"), split, tall, split, split,
        ),
        out_specs=(
            wide, wide, split, tall, tall, split, tall, tall, split, split, split,
            P(None, "ch"), split, tall, split, split,
        ),
        check_vma=False,
    )
```

```python
import math
from functools import partial

import jax
import jax.numpy as jnp
from jax import lax
from jax.experimental import pallas as pl
from jax.experimental.pallas import tpu as pltpu
from jax.sharding import PartitionSpec as P

SIDE = 32
CELLS = SIDE * SIDE
LANES = 128
PER = LANES // SIDE
SLOT = 8
TILES = CELLS // LANES
EPS = 1e-06
F32 = jnp.float32
BF16 = jnp.bfloat16


def column(row):
    n = row.shape[1]
    eye = lax.broadcasted_iota(jnp.int32, (n, n), 0) == lax.broadcasted_iota(jnp.int32, (n, n), 1)
    return jnp.sum(jnp.where(eye, jnp.broadcast_to(row, (n, n)), 0.0), axis=1, keepdims=True)


def as_row(col):
    n = col.shape[0]
    eye = lax.broadcasted_iota(jnp.int32, (n, n), 0) == lax.broadcasted_iota(jnp.int32, (n, n), 1)
    return jnp.sum(jnp.where(eye, jnp.broadcast_to(col, (n, n)), 0.0), axis=0, keepdims=True)


def image_mask(rows, height, width):
    cell = lax.broadcasted_iota(jnp.int32, (rows, CELLS), 1)
    return (cell // SIDE < height) & (cell % SIDE < width)


def lane_of(rows):
    return lax.broadcasted_iota(jnp.int32, (rows, LANES), 1)


def fill_slots(slots, value, image):
    channels = value.shape[0]
    for group in range(slots.shape[0]):
        live = min(SLOT, channels - group * SLOT)
        for k in range(TILES):
            at = (image * TILES + k) * SLOT
            part = value[group * SLOT : group * SLOT + live, k * LANES : (k + 1) * LANES]
            slots[group, pl.ds(at, live), :] = part


def read_slots(slots, image, channels):
    rows = []
    for group in range(slots.shape[0]):
        live = min(SLOT, channels - group * SLOT)
        at = [(image * TILES + k) * SLOT for k in range(TILES)]
        rows.append(jnp.concatenate([slots[group, pl.ds(a, live), :] for a in at], axis=1))
    return jnp.concatenate(rows, axis=0) if len(rows) > 1 else rows[0]


def cross(tiles, lane):
    for bit, far in ((2, 64), (1, 32)):
        low = (lane & far) == 0
        out = list(tiles)
        for k in range(len(tiles)):
            if not k & bit:
                one, two = tiles[k], tiles[k | bit]
                out[k] = jnp.where(low, one, pltpu.roll(two, far, 1))
                out[k | bit] = jnp.where(low, pltpu.roll(one, LANES - far, 1), two)
        tiles = out
    return tiles


def load_channel(slots, group, c, lane):
    count = slots.shape[1] // SLOT
    value = slots[group, pl.ds(c, count, stride=SLOT), :]
    return cross([value[k * SLOT : (k + 1) * SLOT] for k in range(count // SLOT)], lane)


def store_channel(slots, group, c, tiles, lane):
    count = slots.shape[1] // SLOT
    slots[group, pl.ds(c, count, stride=SLOT), :] = jnp.concatenate(cross(tiles, lane), axis=0)


def split(value):
    high = value.astype(BF16)
    return high, (value - high.astype(F32)).astype(BF16)


def pick(row, index):
    spread = jnp.broadcast_to(row, index.shape)
    value = jnp.take_along_axis(spread, jnp.clip(index, 0, LANES - 1), axis=1)
    return value


def build_down(row, c, high_ref, low_ref, lane, sub):
    place = lane % SIDE
    source = (place % TILES) * PER + place // TILES
    here = lane // SIDE == c % PER
    parts = []
    for turn in range(PER):
        index = PER * sub + turn - source
        parts.append(jnp.where(here & (index >= 0), pick(row, index), 0.0))
    high, low = split(jnp.concatenate(parts, axis=0))
    at = (slice(c * SIDE, (c + 1) * SIDE), slice(c // PER * LANES, (c // PER + 1) * LANES))
    high_ref[at] = high
    low_ref[at] = low


def build_across(row, turned, lane, sub):
    place = lane % SIDE
    highs, lows = [], []
    for part in range(PER):
        own = part * SLOT + sub
        index = own - place if turned else place - own
        value = jnp.where(index >= 0, pick(row, index + SIDE), 0.0)
        high = value.astype(BF16).astype(F32)
        highs.append(high)
        lows.append(value - high)
    spread = lambda parts: jnp.concatenate(
        [jnp.where(lane // SIDE == i, p, 0.0) for i in range(PER) for p in parts], axis=0
    ).astype(BF16)
    return spread(highs), spread(lows)


def taps_of(step_h, step_w, rate_h, rate_w, read_h, read_w, skip_ref):
    channels = rate_h.shape[0]
    lane = lane_of(channels)
    kept = jnp.zeros((channels, LANES), F32)
    decay_h = jnp.exp(column(step_h[...])) * rate_h[...]
    decay_w = jnp.exp(column(step_w[...])) * rate_w[...]
    for lag in range(SIDE):
        tap = jnp.sum(read_h[...] * jnp.exp(-decay_h * lag), axis=1, keepdims=True)
        kept = jnp.where(lane == lag, tap, kept)
        tap = jnp.sum(read_w[...] * jnp.exp(-decay_w * lag), axis=1, keepdims=True)
        kept = jnp.where(lane == SIDE + lag, tap, kept)
    return jnp.where(lane == 2 * SIDE, column(skip_ref[...]), kept)


def dot(a, b, dims=(((1,), (0,)), ((), ()))):
    return lax.dot_general(a, b, dims, preferred_element_type=F32)


NT = (((1,), (1,)), ((), ()))
TN = (((0,), (0,)), ((), ()))


def forward_kernel(
    heights, widths, feat_ref, cot_ref, scale_ref, step_h, step_w, rate_h, rate_w, read_h,
    read_w, skip_ref, out_ref, rows_ref, slots, high_a, low_a, field, tall,
):
    channels, cells = feat_ref.shape
    images = cells // CELLS
    rows_ref[0:channels] = taps_of(step_h, step_w, rate_h, rate_w, read_h, read_w, skip_ref)
    for ref in (high_a, low_a, field):
        ref[...] = jnp.zeros_like(ref)
    for image in range(images):
        inside = image_mask(1, heights[image], widths[image])
        value = feat_ref[:, image * CELLS : (image + 1) * CELLS].astype(F32)
        fill_slots(slots, jnp.where(inside, value, 0.0), image)
    live = min(SLOT, channels)
    sides = images // PER

    def body(group, carry):
        lane = lane_of(SLOT)
        sub = lax.broadcasted_iota(jnp.int32, (SLOT, LANES), 0)
        for c in range(live):
            row = rows_ref[pl.ds(group * SLOT + c, 1), :]
            build_down(row, c, high_a, low_a, lane, sub)
            tiles = load_channel(slots, group, c, lane)
            for s in range(sides):
                value = jnp.concatenate(tiles[s * PER : (s + 1) * PER], axis=0)
                field[c * SIDE : (c + 1) * SIDE, s * LANES : (s + 1) * LANES] = value.astype(BF16)
        source = field[...]
        tall[...] = dot(high_a[...], source) + dot(low_a[...], source)
        for c in range(live):
            row = rows_ref[pl.ds(group * SLOT + c, 1), :]
            high_b, low_b = build_across(row, False, lane, sub)
            value = jnp.concatenate(
                [tall[c * SIDE : (c + 1) * SIDE, s * LANES : (s + 1) * LANES] for s in range(sides)],
                axis=0,
            )
            high, low = split(value)
            value = dot(
                jnp.concatenate([high, low, high], axis=1),
                jnp.concatenate([high_b, high_b, low_b], axis=0),
            )
            tiles = [value[k * SLOT : (k + 1) * SLOT] for k in range(images)]
            store_channel(slots, group, c, tiles, lane)
        return carry

    lax.fori_loop(0, slots.shape[0], body, 0)
    wide = out_ref.shape[3]
    parts = CELLS // wide
    skip = rows_ref[0:channels, 2 * SIDE : 2 * SIDE + 1]
    scale = column(scale_ref[...])
    for image in range(images):
        span = slice(image * CELLS, (image + 1) * CELLS)
        inside = image_mask(1, heights[image], widths[image])
        value = read_slots(slots, image, channels) + skip * feat_ref[:, span].astype(F32)
        value = jnp.where(inside, value, 0.0).astype(BF16)
        down = cot_ref[:, span].astype(F32) * scale
        down = jnp.where(inside, down, 0.0).astype(BF16)
        for j in range(parts):
            out_ref[image * parts + j, 0] = value[:, j * wide : (j + 1) * wide]
            out_ref[image * parts + j, 1] = down[:, j * wide : (j + 1) * wide]


def prepare_kernel(
    heights, widths, feat_ref, rows_ref, field_ref, high_a, low_a, high_s, low_s, slots, tall
):
    channels, cells = feat_ref.shape
    images = cells // CELLS
    live = min(SLOT, channels)
    sides = images // PER
    for ref in (field_ref, high_a, low_a):
        ref[...] = jnp.zeros_like(ref)
    for image in range(images):
        inside = image_mask(1, heights[image], widths[image])
        value = feat_ref[:, image * CELLS : (image + 1) * CELLS].astype(F32)
        fill_slots(slots, jnp.where(inside, value, 0.0), image)

    def body(group, carry):
        lane = lane_of(SLOT)
        sub = lax.broadcasted_iota(jnp.int32, (SLOT, LANES), 0)
        for c in range(live):
            row = rows_ref[pl.ds(group * SLOT + c, 1), :]
            build_down(row, c, high_a.at[group], low_a.at[group], lane, sub)
            tiles = load_channel(slots, group, c, lane)
            for s in range(sides):
                value = jnp.concatenate(tiles[s * PER : (s + 1) * PER], axis=0)
                at = (group, slice(c * SIDE, (c + 1) * SIDE), slice(s * LANES, (s + 1) * LANES))
                field_ref[at] = value.astype(BF16)
        source = field_ref[group]
        tall[...] = dot(high_a[group], source) + dot(low_a[group], source)
        for c in range(live):
            value = jnp.concatenate(
                [tall[c * SIDE : (c + 1) * SIDE, s * LANES : (s + 1) * LANES] for s in range(sides)],
                axis=0,
            )
            high, low = split(value)
            high_s[group, c] = high
            low_s[group, c] = low
        return carry

    lax.fori_loop(0, slots.shape[0], body, 0)


def backward_kernel(
    heights, widths, feat_ref, cot_ref, both_ref, rows_ref, scale_ref, bias_ref,
    step_h, step_w, rate_h, rate_w, read_h, read_w, field_ref, high_a, low_a, high_s, low_s,
    result_ref, gfeat_ref, small_ref, slots, slots_g, field_g, outer_ref, high_d, low_d, wide_ref, sums,
):
    channels, cells = feat_ref.shape
    images = cells // CELLS
    live = min(SLOT, channels)
    sides = images // PER
    wide = both_ref.shape[3]
    parts = CELLS // wide
    for ref in (sums, field_g, high_d, low_d):
        ref[...] = jnp.zeros_like(ref)
    lane_c = lane_of(channels)
    scale = column(scale_ref[...])
    bias = column(bias_ref[...])
    small = jnp.zeros((channels, LANES), F32)
    for image in range(images):
        span = slice(image * CELLS, (image + 1) * CELLS)
        inside = image_mask(1, heights[image], widths[image])
        values = feat_ref[:, span].astype(F32)
        grad = jnp.concatenate(
            [both_ref[image * parts + j, 0].astype(F32) for j in range(parts)], axis=1
        )
        grad = jnp.where(inside, grad, 0.0)
        fill_slots(slots_g, grad, image)
        shifted = jnp.concatenate(
            [both_ref[image * parts + j, 1].astype(F32) for j in range(parts)], axis=1
        )
        shifted = shifted + bias
        result = values + jnp.where(inside, scale * shifted, 0.0)
        result_ref[:, span] = result.astype(BF16)
        weighted = jnp.where(inside, cot_ref[:, span].astype(F32), 0.0)
        small = small + jnp.where(
            lane_c == 64,
            jnp.sum(grad * values, axis=1, keepdims=True),
            jnp.where(
                lane_c == 65,
                jnp.sum(weighted * shifted, axis=1, keepdims=True),
                jnp.where(lane_c == 66, scale * jnp.sum(weighted, axis=1, keepdims=True), 0.0),
            ),
        )

    def body(group, carry):
        lane = lane_of(SLOT)
        sub = lax.broadcasted_iota(jnp.int32, (SLOT, LANES), 0)
        place = lane % SIDE
        half = lambda ref, c, s: ref[c * SIDE : (c + 1) * SIDE, s * LANES : (s + 1) * LANES]
        stack = lambda ref, c: jnp.concatenate([half(ref, c, s) for s in range(sides)], axis=0)
        for c in range(live):
            tiles = load_channel(slots_g, group, c, lane)
            for s in range(sides):
                value = jnp.concatenate(tiles[s * PER : (s + 1) * PER], axis=0)
                at = (slice(c * SIDE, (c + 1) * SIDE), slice(s * LANES, (s + 1) * LANES))
                field_g[at] = value.astype(BF16)
        for c in range(live):
            row = rows_ref[pl.ds(group * SLOT + c, 1), :]
            high_b, low_b = build_across(row, True, lane, sub)
            grad = stack(field_g, c)
            flow = dot(
                jnp.concatenate([grad, grad], axis=1), jnp.concatenate([high_b, low_b], axis=0)
            )
            high, low = split(flow)
            for s in range(sides):
                at = (slice(c * SIDE, (c + 1) * SIDE), slice(s * LANES, (s + 1) * LANES))
                high_d[at] = high[s * SIDE : (s + 1) * SIDE]
                low_d[at] = low[s * SIDE : (s + 1) * SIDE]
            outer = dot(
                jnp.concatenate([grad, grad], axis=0),
                jnp.concatenate([high_s[group, c], low_s[group, c]], axis=0),
                TN,
            )
            total = None
            for part in range(PER):
                value = None
                for i in range(PER):
                    at = i * SIDE + part * SLOT
                    term = jnp.where(lane // SIDE == i, outer[at : at + SLOT], 0.0)
                    value = term if value is None else value + term
                index = part * SLOT + sub - place
                value = jnp.take_along_axis(
                    value, jnp.clip(index, 0, SIDE - 1) + lane // SIDE * SIDE, axis=1
                )
                value = jnp.where(index >= 0, value, 0.0)
                total = value if total is None else total + value
            total = jnp.sum(total, axis=0, keepdims=True)
            total = total + pltpu.roll(total, 64, 1)
            total = total + pltpu.roll(total, 32, 1)
            sums[pl.ds(group * SLOT + c, 1), :] = jnp.where(lane[0:1] // SIDE == 1, total, 0.0)
        high, low = high_d[...], low_d[...]
        down = high_a[group]
        back = dot(down, high, TN) + dot(down, low, TN) + dot(low_a[group], high, TN)
        wide_ref[...] = back
        source = field_ref[group]
        outer_ref[...] = dot(high, source, NT) + dot(low, source, NT)
        for c in range(live):
            value = stack(wide_ref, c)
            tiles = [value[k * SLOT : (k + 1) * SLOT] for k in range(images)]
            store_channel(slots, group, c, tiles, lane)
            total = None
            for turn in range(PER):
                at = c * SIDE + turn * SLOT
                value = outer_ref[at : at + SLOT, c // PER * LANES : (c // PER + 1) * LANES]
                index = PER * sub + turn - lane
                safe = jnp.clip(index, 0, SIDE - 1)
                index_at = (safe % PER) * TILES + safe // PER + c % PER * SIDE
                value = jnp.take_along_axis(value, index_at, axis=1)
                value = jnp.where(index >= 0, value, 0.0)
                total = value if total is None else total + value
            total = jnp.sum(total, axis=0, keepdims=True)
            total = jnp.where(lane[0:1] < SIDE, total, 0.0)
            sums[pl.ds(group * SLOT + c, 1), :] += total
        return carry

    lax.fori_loop(0, slots.shape[0], body, 0)
    skip = rows_ref[0:channels, 2 * SIDE : 2 * SIDE + 1]
    for image in range(images):
        span = slice(image * CELLS, (image + 1) * CELLS)
        inside = image_mask(1, heights[image], widths[image])
        grad = read_slots(slots_g, image, channels)
        value = read_slots(slots, image, channels) + skip * grad
        gfeat_ref[:, span] = cot_ref[:, span].astype(F32) + jnp.where(inside, value, 0.0)
    small = small + sums[0:channels]
    states, small = chain(small, step_h, step_w, rate_h, rate_w, read_h, read_w)
    for index in range(2):
        pair = jnp.concatenate(states[2 * index : 2 * index + 2], axis=1)
        small_ref[:, index * pair.shape[1] : (index + 1) * pair.shape[1]] = pair
    small_ref[:, 2 * pair.shape[1] :] = small


def chain(total, step_h, step_w, rate_h, rate_w, read_h, read_w):
    out, tail = [], total
    lane = lane_of(total.shape[0])
    for place, first, step, rate, read in (
        (67, 0, step_h, rate_h, read_h), (68, SIDE, step_w, rate_w, read_w),
    ):
        pace = jnp.exp(column(step[...]))
        decay = pace * rate[...]
        to_read = jnp.zeros_like(decay)
        to_decay = jnp.zeros_like(decay)
        for lag in range(SIDE):
            term = total[:, first + lag : first + lag + 1] * jnp.exp(-decay * lag)
            to_read = to_read + term
            if lag:
                to_decay = to_decay - float(lag) * term
        to_decay = to_decay * read[...]
        out += [to_read, pace * to_decay]
        tail = jnp.where(lane == place, jnp.sum(to_decay * decay, axis=1, keepdims=True), tail)
    return out, tail


def join_kernel(count, *refs):
    given, outs = refs[:count], refs[count:]
    tall = outs[0].shape[0]
    for index, out in enumerate(outs):
        at = slice(index * tall, (index + 1) * tall)
        total = given[0][at].astype(F32)
        for ref in given[1:]:
            total = total + ref[at].astype(F32)
        out[...] = total.astype(out.dtype)


def cut_kernel(one_ref, two_ref, first_ref, second_ref):
    cut = first_ref.shape[0]
    first_ref[...] = one_ref[:cut]
    second_ref[...] = two_ref[cut:]


def relay_kernel(one_ref, two_ref, arrived_ref, first_ref, second_ref, out_one, out_two):
    tall = one_ref.shape[0]
    cut = tall // 2
    one = one_ref[...].astype(F32) + arrived_ref[tall : 2 * tall].astype(F32)
    two = two_ref[...].astype(F32) + arrived_ref[2 * tall : 3 * tall].astype(F32)
    out_one[:cut] = (one[:cut] + first_ref[...].astype(F32)).astype(BF16)
    out_one[cut:] = one[cut:].astype(BF16)
    out_two[:cut] = two[:cut].astype(BF16)
    out_two[cut:] = (two[cut:] + second_ref[...].astype(F32)).astype(BF16)


def finish_kernel(
    half, mine_ref, other_ref, small_ref, sibling_ref,
    gstep_h, grate_h, gread_h, gstep_w, grate_w, gread_w, gskip, ggain, gshift, gin, ginb, gout,
    gbias, gscale,
):
    units, count = gin.shape
    channels, states = grate_h.shape
    keep = units // 2
    first = half[0] == 0
    mine, other = mine_ref[...], other_ref[...]
    low = jnp.where(first, mine, other)[:keep]
    high = jnp.where(first, other, mine)[:keep]
    for at, part in ((0, low), (keep, high)):
        gin[at : at + keep] = part[:, :count]
        gout[at : at + keep] = part[:, count : 2 * count]
    bias = jnp.concatenate([low[:, 2 * count :], high[:, 2 * count :]], axis=0)
    ginb[...] = as_row(bias[:, 0:1])
    norms = (mine[:, 2 * count :] + other[:, 2 * count :])[:channels]
    ggain[...] = as_row(norms[:, 1:2])
    gshift[...] = as_row(norms[:, 2:3])
    total = small_ref[...] + sibling_ref[...]
    for index, ref in enumerate((gread_h, grate_h, gread_w, grate_w)):
        ref[...] = total[:, index * states : (index + 1) * states]
    total = total[:, 4 * states :]
    gskip[...] = as_row(total[:, 64:65])
    gscale[...] = as_row(total[:, 65:66])
    gbias[...] = as_row(total[:, 66:67])
    gstep_h[...] = as_row(total[:, 67:68])
    gstep_w[...] = as_row(total[:, 68:69])


def pack_kernel(half, in_ref, out_ref, bias_ref, gain_ref, shift_ref, pack_ref):
    deep = pack_ref.shape[0]
    own, count = out_ref.shape
    channels = gain_ref.shape[1]
    keep = own // 2
    row = lax.broadcasted_iota(jnp.int32, (deep, own), 0)
    col = lax.broadcasted_iota(jnp.int32, (deep, own), 1)
    pick = jnp.where((col == row + half[0] * keep) & (row < keep), 1.0, 0.0).astype(BF16)
    nt = (((1,), (1,)), ((), ()))
    first = jnp.dot(pick, in_ref[...], preferred_element_type=F32)
    second = jnp.dot(pick, out_ref[...], preferred_element_type=F32)
    bias = jnp.broadcast_to(bias_ref[...], (LANES, own))
    third = lax.dot_general(pick, bias, nt, preferred_element_type=F32)
    row = lax.broadcasted_iota(jnp.int32, (deep, channels), 0)
    col = lax.broadcasted_iota(jnp.int32, (deep, channels), 1)
    pick = jnp.where(col == row, 1.0, 0.0).astype(BF16)
    gain = jnp.broadcast_to(gain_ref[...], (LANES, channels))
    gain = lax.dot_general(pick, gain, nt, preferred_element_type=F32)
    shift = jnp.broadcast_to(shift_ref[...], (LANES, channels))
    shift = lax.dot_general(pick, shift, nt, preferred_element_type=F32)
    lane = lane_of(deep)
    third = jnp.where(lane == 0, third, jnp.where(lane == 1, gain, jnp.where(lane == 2, shift, 0.0)))
    pack_ref[:, :count] = first.astype(BF16)
    pack_ref[:, count : 2 * count] = second.astype(BF16)
    pack_ref[:, 2 * count :] = third.astype(BF16)


ROOT = math.sqrt(2.0 / math.pi)


def perceptron(refs, act, down):
    count = act.shape[0]
    w_in = jnp.concatenate([ref[:, :count] for ref in refs], axis=0)
    w_out = jnp.concatenate([ref[:, count : 2 * count] for ref in refs], axis=0)
    bias = jnp.concatenate([ref[:, 2 * count :] for ref in refs], axis=0).astype(F32)[:, 0:1]
    v = dot(w_in, act) + bias
    square = v * v
    half = 0.5 * jnp.tanh(v * (ROOT * 0.044715 * square + ROOT)) + 0.5
    full = v * half
    hidden = full.astype(BF16)
    slope = half + full * (1.0 - half) * (6.0 * ROOT * 0.044715 * square + 2.0 * ROOT)
    low = (dot(w_out, down) * slope).astype(BF16)
    g_bias = jnp.sum(low.astype(F32), axis=1, keepdims=True)
    g_bias = jnp.where(lane_of(low.shape[0]) == 0, g_bias, 0.0)
    grads = (dot(low, act, NT), dot(hidden, down, NT), g_bias)
    return dot(w_out, hidden, TN), dot(w_in, low, TN), grads


def put(ref, grads, start):
    count = grads[0].shape[1]
    at = slice(start, start + ref.shape[0])
    ref[:, :count] = grads[0][at].astype(BF16)
    ref[:, count : 2 * count] = grads[1][at].astype(BF16)
    ref[:, 2 * count :] = grads[2][at].astype(BF16)
    return start + ref.shape[0]


def spots_of(near, devices, deep, where_ref):
    z, xy = where_ref[0], where_ref[1]
    for d in range(devices):
        spot = ((d % near) ^ xy) * (devices // near) + ((d // near) ^ z)
        yield d, pl.multiple_of(spot * deep, deep)


def mlp_first(near, pieces, where_ref, given_ref, *refs):
    own_in, refs = refs[:pieces], refs[pieces:]
    other_in, refs = refs[:pieces], refs[pieces:]
    gother_ref, active, downs, normal, inv_ref, gains, sum_ref, grad_ref, ext = refs
    devices, _, channels, _ = given_ref.shape
    deep = ext.shape[0] // devices
    count = active.shape[0]

    value = jnp.concatenate([given_ref[d, 0].astype(F32) for d in range(devices)], axis=0)
    mean = jnp.mean(value, axis=0, keepdims=True)
    value = value - mean
    inv = lax.rsqrt(jnp.mean(value * value, axis=0, keepdims=True) + EPS)
    value = value * inv
    normal[...] = value
    inv_ref[...] = inv
    down = jnp.concatenate([given_ref[d, 1].astype(F32) for d in range(devices)], axis=0)
    downs[...] = down.astype(BF16)
    at = 0
    for ref in own_in:
        ext[at : at + ref.shape[0]] = ref[:, 2 * count :].astype(F32)
        at += ref.shape[0]
    for d, spot in spots_of(near, devices, deep, where_ref):
        gains[d * channels : (d + 1) * channels] = ext[pl.ds(spot, deep), :][:channels]
    active[...] = (value * gains[:, 1:2] + gains[:, 2:3]).astype(BF16)
    sums, total, grads = perceptron(other_in, active[...], downs[...])
    put(gother_ref, grads, 0)
    sum_ref[...] = sums
    grad_ref[...] = total


def mlp_second(
    near, pieces, where_ref, active, downs, normal_ref, inv_ref, gains, sum_ref, grad_ref, *refs
):
    own_in, refs = refs[:pieces], refs[pieces:]
    both_ref, refs = refs[0], refs[1:]
    own_out, (gext,) = refs[:pieces], refs[pieces:]
    count = active.shape[0]
    devices, _, channels, _ = both_ref.shape
    deep = gext.shape[0] // devices

    sums, total, grads = perceptron(own_in, active[...], downs[...])
    gext[...] = grads[2]
    start = 0
    for ref in own_out:
        start = put(ref, grads, start)
    summed = sum_ref[...] + sums
    agrad = grad_ref[...] + total
    norm = normal_ref[...]
    scaled = agrad * gains[:, 1:2]
    first = jnp.mean(scaled, axis=0, keepdims=True)
    second = jnp.mean(scaled * norm, axis=0, keepdims=True)
    mgrad = (scaled - first - norm * second) * inv_ref[...]
    for d in range(devices):
        both_ref[d, 0] = mgrad[d * channels : (d + 1) * channels].astype(BF16)
        both_ref[d, 1] = summed[d * channels : (d + 1) * channels].astype(BF16)
    lane = lane_of(count)
    tile = jnp.where(lane == 1, jnp.sum(agrad * norm, axis=1, keepdims=True), 0.0)
    tile = jnp.where(lane == 2, jnp.sum(agrad, axis=1, keepdims=True), tile)
    for d, spot in spots_of(near, devices, deep, where_ref):
        part = tile[d * channels : (d + 1) * channels]
        if channels < deep:
            part = jnp.concatenate([part, jnp.zeros((deep - channels, LANES), F32)], axis=0)
        gext[pl.ds(spot, deep), :] += part
    start = 0
    for ref in own_out:
        ref[:, 2 * count :] = gext[start : start + ref.shape[0]].astype(BF16)
        start += ref.shape[0]


def whole(shape):
    return pl.BlockSpec(shape, lambda i: (0,) * len(shape))


def params(mebibytes):
    return pltpu.CompilerParams(vmem_limit_bytes=mebibytes << 20)


def cost(micros):
    return pl.CostEstimate(flops=0, transcendentals=0, bytes_accessed=micros * 3_000_000)


def join(deep, arrays, count):
    full = pl.BlockSpec(memory_space=pltpu.VMEM)
    width = arrays[0].shape[1]
    return pl.pallas_call(
        partial(join_kernel, len(arrays)),
        out_shape=[
            jax.ShapeDtypeStruct((deep, width), BF16 if i else F32) for i in range(count)
        ],
        in_specs=[full] * len(arrays),
        out_specs=[full] * count,
        compiler_params=params(8),
        cost_estimate=pl.CostEstimate(flops=1 if count > 1 else 1, transcendentals=0, bytes_accessed=1_000_000),
        name="join",
    )(*arrays)


def relay(*arrays):
    full = pl.BlockSpec(memory_space=pltpu.VMEM)
    shape = jax.ShapeDtypeStruct(arrays[0].shape, BF16)
    return pl.pallas_call(
        relay_kernel,
        out_shape=(shape, shape),
        in_specs=[full] * 5,
        out_specs=(full, full),
        compiler_params=params(8),
        cost_estimate=pl.CostEstimate(flops=100_000_000_000, transcendentals=0, bytes_accessed=1_000_000),
        name="relay",
    )(*arrays)


SMEM = pl.BlockSpec(memory_space=pltpu.SMEM)


def per_device(
    ch, features, cotangent, heights, widths, step_height, rate_height, readout_height,
    step_width, rate_width, readout_width, skip_gain, norm_gain, norm_shift, in_weight,
    in_bias, out_weight, out_bias, layer_scale,
):
    channels, cells = features.shape
    count = in_weight.shape[0]
    pin = lambda v: pltpu.with_memory_space_constraint(v, pltpu.HBM)
    units = in_weight.shape[1]
    states = rate_height.shape[1]
    images = cells // CELLS
    tokens = cells // ch
    parts = CELLS // tokens
    far = 4
    near = ch // far
    deep = -(-(units // 2) // 16) * 16
    width = 2 * count + LANES
    near_groups = [[f * near + i for i in range(near)] for f in range(far)]
    row = lambda v: v.reshape(1, -1)
    exchange = lambda v: lax.ppermute(v, "img", [(0, 1), (1, 0)])
    flip = lambda v, bits: lax.ppermute(v, "ch", [(i, i ^ bits) for i in range(ch)])
    swap = lambda v, groups=None: lax.all_to_all(
        v, "ch", split_axis=0, concat_axis=0, tiled=True, axis_index_groups=groups
    )
    pair = lambda *arrays: lax.optimization_barrier(arrays)
    half = lax.axis_index("img").astype(jnp.int32)
    place = lax.axis_index("ch").astype(jnp.int32)
    full = pl.BlockSpec(memory_space=pltpu.VMEM)

    pack = pl.pallas_call(
        pack_kernel,
        out_shape=jax.ShapeDtypeStruct((deep, width), BF16),
        in_specs=[SMEM] + [full] * 5,
        out_specs=full,
        compiler_params=params(4),
        cost_estimate=cost(2),
        name="pack",
    )(
        half.reshape(1), pin(in_weight.T), pin(out_weight), pin(row(in_bias)), pin(row(norm_gain)),
        pin(row(norm_shift)),
    )
    pack, features_after = pair(pack, features)
    shards = [pack] + [flip(pack, bits * near) for bits in range(1, far)]

    groups = -(-channels // SLOT)
    square = (SLOT * SIDE, images // PER * LANES)
    toeplitz = pltpu.VMEM((SLOT * SIDE, SLOT * SIDE), BF16)
    slots = pltpu.VMEM((groups, images * TILES * SLOT, LANES), F32)
    both_shape = (ch, 2, channels, tokens)
    given, taps = pl.pallas_call(
        forward_kernel,
        out_shape=(
            jax.ShapeDtypeStruct(both_shape, BF16),
            jax.ShapeDtypeStruct((groups * SLOT, LANES), F32),
        ),
        in_specs=[SMEM, SMEM] + [full] * 10,
        out_specs=(full, full),
        scratch_shapes=[
            slots, toeplitz, toeplitz, pltpu.VMEM(square, BF16), pltpu.VMEM(square, F32),
        ],
        compiler_params=params(12),
        cost_estimate=cost(6),
        name="mixer_forward",
    )(
        pin(heights), pin(widths), pin(features_after), pin(cotangent), pin(row(layer_scale)),
        pin(row(step_height)), pin(row(step_width)), pin(rate_height), pin(rate_width),
        pin(readout_height), pin(readout_width), pin(row(skip_gain)),
    )
    given, *shards = pair(given, *shards)
    given = swap(given)
    shard = jnp.concatenate(shards, axis=0)
    if near == 4:
        cut = far * deep // 2
        beside, above = pair(flip(shard, 1), flip(shard, 2))
        ends = pl.pallas_call(
            cut_kernel,
            out_shape=[jax.ShapeDtypeStruct((cut, width), BF16)] * 2,
            in_specs=[full] * 2,
            out_specs=[full] * 2,
            compiler_params=params(4),
            cost_estimate=pl.CostEstimate(flops=100_000_000_000, transcendentals=0, bytes_accessed=1_000_000),
            name="ends",
        )(beside, above)
        own = [shard, beside, above, flip(ends[0], 2), flip(ends[1], 1)]
        where = jnp.stack([place // near, place % near])
    else:
        own = [swap(jnp.broadcast_to(shard[None], (near,) + shard.shape), near_groups)]
        own = [own[0].reshape(ch * deep, width)]
        where = jnp.stack([place // near, place * 0])
    other = [exchange(piece) for piece in own]

    rows = ch * deep
    pieces = len(own)
    plane = jax.ShapeDtypeStruct((count, tokens), F32)
    token_low = jax.ShapeDtypeStruct((count, tokens), BF16)
    gother, *state = pl.pallas_call(
        partial(mlp_first, near, pieces),
        out_shape=[
            jax.ShapeDtypeStruct((rows, width), BF16), token_low, token_low, plane,
            jax.ShapeDtypeStruct((1, tokens), F32), jax.ShapeDtypeStruct((count, LANES), F32),
            plane, plane,
        ],
        in_specs=[SMEM] + [full] * (1 + 2 * pieces),
        out_specs=[full] * 8,
        scratch_shapes=[pltpu.VMEM((rows, LANES), F32)],
        compiler_params=params(16),
        cost_estimate=cost(5),
        name="mlp_first",
    )(where, given, *own, *map(pin, other))
    arrived = exchange(gother)
    both, *gown = pl.pallas_call(
        partial(mlp_second, near, pieces),
        out_shape=[jax.ShapeDtypeStruct(both_shape, BF16)]
        + [jax.ShapeDtypeStruct(piece.shape, BF16) for piece in own],
        in_specs=[SMEM] + [full] * (7 + pieces),
        out_specs=[full] * (1 + pieces),
        scratch_shapes=[pltpu.VMEM((rows, LANES), F32)],
        compiler_params=params(16),
        cost_estimate=cost(5),
        name="mlp_second",
    )(where, *state, *own)
    both = swap(both)
    tall = far * deep
    if near == 4:
        cut = tall // 2
        add = lambda v, at: (v.astype(F32) + arrived[at : at + v.shape[0]].astype(F32)).astype(BF16)
        one, two = pair(add(gown[3], 3 * tall), add(gown[4], 3 * tall + cut))
        one, two = pair(flip(one, 2), flip(two, 1))
        one, two = relay(gown[1], gown[2], arrived, one, two)
        features_last, one, two = pair(features, one, two)
        first, second, *sent = gown[0], arrived, flip(one, 1), flip(two, 2)
    else:
        features_last = features
        total = (gown[0].astype(F32) + arrived.astype(F32)).astype(BF16)
        sent = list(swap(total.reshape(near, tall, width), near_groups))
        first, second, *sent = sent
    landed = [first, second, *sent]
    table = pltpu.HBM((groups,) + toeplitz.shape, BF16)
    strip = pltpu.HBM((groups, SLOT, images * SLOT, LANES), BF16)
    prepared = pl.pallas_call(
        prepare_kernel,
        out_shape=(
            pltpu.HBM((groups,) + square, BF16), table, table, strip, strip,
        ),
        in_specs=[SMEM, SMEM, full, full],
        out_specs=(full,) * 5,
        scratch_shapes=[slots, pltpu.VMEM(square, F32)],
        compiler_params=params(12),
        cost_estimate=cost(4),
        name="mixer_prepare",
    )(pin(heights), pin(widths), pin(features_last), taps)
    *landed, _ = pair(*landed, prepared[0])
    shards = join(deep, landed, far)
    shards = [shards[0]] + [flip(v, (i + 1) * near) for i, v in enumerate(shards[1:])]
    result, grad_features, small = pl.pallas_call(
        backward_kernel,
        out_shape=(
            jax.ShapeDtypeStruct((channels, cells), BF16),
            jax.ShapeDtypeStruct((channels, cells), F32),
            jax.ShapeDtypeStruct((channels, LANES + 4 * states), F32),
        ),
        in_specs=[SMEM, SMEM] + [full] * 17,
        out_specs=(full,) * 3,
        scratch_shapes=[
            slots, slots, pltpu.VMEM(square, BF16),
            pltpu.VMEM((SLOT * SIDE, SLOT * SIDE), F32), pltpu.VMEM(square, BF16),
            pltpu.VMEM(square, BF16), pltpu.VMEM(square, F32),
            pltpu.VMEM((groups * SLOT, LANES), F32),
        ],
        compiler_params=params(16),
        cost_estimate=cost(7),
        name="mixer_backward",
    )(
        pin(heights), pin(widths), pin(features), pin(cotangent), both, taps,
        pin(row(layer_scale)), pin(row(out_bias)), pin(row(step_height)), pin(row(step_width)),
        pin(rate_height), pin(rate_width), pin(readout_height), pin(readout_width),
        *map(pin, prepared),
    )
    *shards, small = pair(*shards, small)
    (mine,) = join(deep, shards, 1)
    vector_out = jax.ShapeDtypeStruct((1, channels), F32)
    state_out = jax.ShapeDtypeStruct((channels, states), F32)
    weight_out = jax.ShapeDtypeStruct((units, count), F32)
    outs = pl.pallas_call(
        finish_kernel,
        out_shape=(
            vector_out, state_out, state_out, vector_out, state_out, state_out, vector_out,
            vector_out, vector_out, weight_out, jax.ShapeDtypeStruct((1, units), F32), weight_out,
            vector_out, vector_out,
        ),
        in_specs=[SMEM] + [full] * 4,
        out_specs=(full,) * 14,
        compiler_params=params(4),
        cost_estimate=cost(1),
        name="finish",
    )(half.reshape(1), mine, exchange(mine), small, exchange(small))
    outs = [v.reshape(-1) if v.shape[0] == 1 else v for v in outs]
    outs[9] = outs[9].T
    return (result, grad_features, *outs)


def solution(mesh):
    wide, split, tall = P("ch", "img"), P("ch"), P("ch", None)
    return jax.shard_map(
        partial(per_device, mesh.shape["ch"]),
        mesh=mesh,
        in_specs=(
            wide, wide, P("img"), P("img"), split, tall, tall, split, tall, tall, split, split,
            split, P(None, "ch"), split, tall, split, split,
        ),
        out_specs=(
            wide, wide, split, tall, tall, split, tall, tall, split, split, split,
            P(None, "ch"), split, tall, split, split,
        ),
        check_vma=False,
    )
```

```python
import math
from functools import partial

import jax
import jax.numpy as jnp
from jax import lax
from jax.experimental import pallas as pl
from jax.experimental.pallas import tpu as pltpu
from jax.sharding import PartitionSpec as P

SIDE = 32
CELLS = SIDE * SIDE
LANES = 128
PER = LANES // SIDE
SLOT = 8
EDGE = 16
TILES = CELLS // LANES
EPS = 1e-06
F32 = jnp.float32
BF16 = jnp.bfloat16


def column(row):
    n = row.shape[1]
    eye = lax.broadcasted_iota(jnp.int32, (n, n), 0) == lax.broadcasted_iota(jnp.int32, (n, n), 1)
    return jnp.sum(jnp.where(eye, jnp.broadcast_to(row, (n, n)), 0.0), axis=1, keepdims=True)


def as_row(col):
    n = col.shape[0]
    eye = lax.broadcasted_iota(jnp.int32, (n, n), 0) == lax.broadcasted_iota(jnp.int32, (n, n), 1)
    return jnp.sum(jnp.where(eye, jnp.broadcast_to(col, (n, n)), 0.0), axis=0, keepdims=True)


def image_mask(rows, height, width):
    cell = lax.broadcasted_iota(jnp.int32, (rows, CELLS), 1)
    return (cell // SIDE < height) & (cell % SIDE < width)


def lane_of(rows):
    return lax.broadcasted_iota(jnp.int32, (rows, LANES), 1)


def fill_slots(slots, value, image):
    channels = value.shape[0]
    for group in range(slots.shape[0]):
        live = min(SLOT, channels - group * SLOT)
        for k in range(TILES):
            at = (image * TILES + k) * SLOT
            part = value[group * SLOT : group * SLOT + live, k * LANES : (k + 1) * LANES]
            slots[group, pl.ds(at, live), :] = part


def read_slots(slots, image, channels):
    rows = []
    for group in range(slots.shape[0]):
        live = min(SLOT, channels - group * SLOT)
        at = [(image * TILES + k) * SLOT for k in range(TILES)]
        rows.append(jnp.concatenate([slots[group, pl.ds(a, live), :] for a in at], axis=1))
    return jnp.concatenate(rows, axis=0) if len(rows) > 1 else rows[0]


def cross(tiles, lane):
    for bit, far in ((2, 64), (1, 32)):
        low = (lane & far) == 0
        out = list(tiles)
        for k in range(len(tiles)):
            if not k & bit:
                one, two = tiles[k], tiles[k | bit]
                out[k] = jnp.where(low, one, pltpu.roll(two, far, 1))
                out[k | bit] = jnp.where(low, pltpu.roll(one, LANES - far, 1), two)
        tiles = out
    return tiles


def load_channel(slots, group, c, lane):
    count = slots.shape[1] // SLOT
    value = slots[group, pl.ds(c, count, stride=SLOT), :]
    return cross([value[k * SLOT : (k + 1) * SLOT] for k in range(count // SLOT)], lane)


def store_channel(slots, group, c, tiles, lane):
    count = slots.shape[1] // SLOT
    slots[group, pl.ds(c, count, stride=SLOT), :] = jnp.concatenate(cross(tiles, lane), axis=0)


def split(value):
    high = value.astype(BF16)
    return high, (value - high.astype(F32)).astype(BF16)


def pick(row, index):
    spread = jnp.broadcast_to(row, index.shape)
    value = jnp.take_along_axis(spread, jnp.clip(index, 0, LANES - 1), axis=1)
    return value


def build_down(row, c, high_ref, low_ref, lane, sub):
    place = lane % SIDE
    source = (place % TILES) * PER + place // TILES
    here = lane // SIDE == c % PER
    parts = []
    for turn in range(PER):
        index = PER * sub + turn - source
        parts.append(jnp.where(here & (index >= 0), pick(row, index), 0.0))
    high, low = split(jnp.concatenate(parts, axis=0))
    at = (slice(c * SIDE, (c + 1) * SIDE), slice(c // PER * LANES, (c // PER + 1) * LANES))
    high_ref[at] = high
    low_ref[at] = low


def build_across(row, turned, lane, sub):
    place = lane % SIDE
    highs, lows = [], []
    for part in range(PER):
        own = part * SLOT + sub
        index = own - place if turned else place - own
        value = jnp.where(index >= 0, pick(row, index + SIDE), 0.0)
        high = value.astype(BF16).astype(F32)
        highs.append(high)
        lows.append(value - high)
    spread = lambda parts: jnp.concatenate(
        [jnp.where(lane // SIDE == i, p, 0.0) for i in range(PER) for p in parts], axis=0
    ).astype(BF16)
    return spread(highs), spread(lows)


def taps_of(step_h, step_w, rate_h, rate_w, read_h, read_w, skip_ref):
    channels = rate_h.shape[0]
    lane = lane_of(channels)
    kept = jnp.zeros((channels, LANES), F32)
    decay_h = jnp.exp(column(step_h[...])) * rate_h[...]
    decay_w = jnp.exp(column(step_w[...])) * rate_w[...]
    for lag in range(SIDE):
        tap = jnp.sum(read_h[...] * jnp.exp(-decay_h * lag), axis=1, keepdims=True)
        kept = jnp.where(lane == lag, tap, kept)
        tap = jnp.sum(read_w[...] * jnp.exp(-decay_w * lag), axis=1, keepdims=True)
        kept = jnp.where(lane == SIDE + lag, tap, kept)
    return jnp.where(lane == 2 * SIDE, column(skip_ref[...]), kept)


def dot(a, b, dims=(((1,), (0,)), ((), ()))):
    return lax.dot_general(a, b, dims, preferred_element_type=F32)


NT = (((1,), (1,)), ((), ()))
TN = (((0,), (0,)), ((), ()))


def forward_kernel(
    heights, widths, feat_ref, cot_ref, scale_ref, step_h, step_w, rate_h, rate_w, read_h,
    read_w, skip_ref, out_ref, rows_ref, slots, high_a, low_a, field, tall,
):
    channels, cells = feat_ref.shape
    images = cells // CELLS
    rows_ref[0:channels] = taps_of(step_h, step_w, rate_h, rate_w, read_h, read_w, skip_ref)
    for ref in (high_a, low_a, field):
        ref[...] = jnp.zeros_like(ref)
    for image in range(images):
        inside = image_mask(1, heights[image], widths[image])
        value = feat_ref[:, image * CELLS : (image + 1) * CELLS].astype(F32)
        fill_slots(slots, jnp.where(inside, value, 0.0), image)
    live = min(SLOT, channels)
    sides = images // PER

    def body(group, carry):
        lane = lane_of(SLOT)
        sub = lax.broadcasted_iota(jnp.int32, (SLOT, LANES), 0)
        for c in range(live):
            row = rows_ref[pl.ds(group * SLOT + c, 1), :]
            build_down(row, c, high_a, low_a, lane, sub)
            tiles = load_channel(slots, group, c, lane)
            for s in range(sides):
                value = jnp.concatenate(tiles[s * PER : (s + 1) * PER], axis=0)
                field[c * SIDE : (c + 1) * SIDE, s * LANES : (s + 1) * LANES] = value.astype(BF16)
        source = field[...]
        tall[...] = dot(high_a[...], source) + dot(low_a[...], source)
        for c in range(live):
            row = rows_ref[pl.ds(group * SLOT + c, 1), :]
            high_b, low_b = build_across(row, False, lane, sub)
            value = jnp.concatenate(
                [tall[c * SIDE : (c + 1) * SIDE, s * LANES : (s + 1) * LANES] for s in range(sides)],
                axis=0,
            )
            high, low = split(value)
            value = dot(
                jnp.concatenate([high, low, high], axis=1),
                jnp.concatenate([high_b, high_b, low_b], axis=0),
            )
            tiles = [value[k * SLOT : (k + 1) * SLOT] for k in range(images)]
            store_channel(slots, group, c, tiles, lane)
        return carry

    lax.fori_loop(0, slots.shape[0], body, 0)
    wide = out_ref.shape[3]
    parts = CELLS // wide
    skip = rows_ref[0:channels, 2 * SIDE : 2 * SIDE + 1]
    scale = column(scale_ref[...])
    for image in range(images):
        span = slice(image * CELLS, (image + 1) * CELLS)
        inside = image_mask(1, heights[image], widths[image])
        value = read_slots(slots, image, channels) + skip * feat_ref[:, span].astype(F32)
        value = jnp.where(inside, value, 0.0).astype(BF16)
        down = cot_ref[:, span].astype(F32) * scale
        down = jnp.where(inside, down, 0.0).astype(BF16)
        for j in range(parts):
            out_ref[image * parts + j, 0] = value[:, j * wide : (j + 1) * wide]
            out_ref[image * parts + j, 1] = down[:, j * wide : (j + 1) * wide]


def prepare_kernel(
    heights, widths, feat_ref, rows_ref, field_ref, high_a, low_a, high_s, low_s, slots, tall
):
    channels, cells = feat_ref.shape
    images = cells // CELLS
    live = min(SLOT, channels)
    sides = images // PER
    for ref in (field_ref, high_a, low_a):
        ref[...] = jnp.zeros_like(ref)
    for image in range(images):
        inside = image_mask(1, heights[image], widths[image])
        value = feat_ref[:, image * CELLS : (image + 1) * CELLS].astype(F32)
        fill_slots(slots, jnp.where(inside, value, 0.0), image)

    def body(group, carry):
        lane = lane_of(SLOT)
        sub = lax.broadcasted_iota(jnp.int32, (SLOT, LANES), 0)
        for c in range(live):
            row = rows_ref[pl.ds(group * SLOT + c, 1), :]
            build_down(row, c, high_a.at[group], low_a.at[group], lane, sub)
            tiles = load_channel(slots, group, c, lane)
            for s in range(sides):
                value = jnp.concatenate(tiles[s * PER : (s + 1) * PER], axis=0)
                at = (group, slice(c * SIDE, (c + 1) * SIDE), slice(s * LANES, (s + 1) * LANES))
                field_ref[at] = value.astype(BF16)
        source = field_ref[group]
        tall[...] = dot(high_a[group], source) + dot(low_a[group], source)
        for c in range(live):
            value = jnp.concatenate(
                [tall[c * SIDE : (c + 1) * SIDE, s * LANES : (s + 1) * LANES] for s in range(sides)],
                axis=0,
            )
            high, low = split(value)
            high_s[group, c] = high
            low_s[group, c] = low
        return carry

    lax.fori_loop(0, slots.shape[0], body, 0)


def backward_kernel(
    heights, widths, feat_ref, cot_ref, both_ref, rows_ref, scale_ref, bias_ref,
    step_h, step_w, rate_h, rate_w, read_h, read_w, field_ref, high_a, low_a, high_s, low_s,
    result_ref, gfeat_ref, small_ref, slots, slots_g, field_g, outer_ref, high_d, low_d, wide_ref, sums,
):
    channels, cells = feat_ref.shape
    images = cells // CELLS
    live = min(SLOT, channels)
    sides = images // PER
    wide = both_ref.shape[3]
    parts = CELLS // wide
    for ref in (sums, field_g, high_d, low_d):
        ref[...] = jnp.zeros_like(ref)
    lane_c = lane_of(channels)
    scale = column(scale_ref[...])
    bias = column(bias_ref[...])
    small = jnp.zeros((channels, LANES), F32)
    for image in range(images):
        span = slice(image * CELLS, (image + 1) * CELLS)
        inside = image_mask(1, heights[image], widths[image])
        values = feat_ref[:, span].astype(F32)
        grad = jnp.concatenate(
            [both_ref[image * parts + j, 0].astype(F32) for j in range(parts)], axis=1
        )
        grad = jnp.where(inside, grad, 0.0)
        fill_slots(slots_g, grad, image)
        shifted = jnp.concatenate(
            [both_ref[image * parts + j, 1].astype(F32) for j in range(parts)], axis=1
        )
        shifted = shifted + bias
        result = values + jnp.where(inside, scale * shifted, 0.0)
        result_ref[:, span] = result.astype(BF16)
        weighted = jnp.where(inside, cot_ref[:, span].astype(F32), 0.0)
        small = small + jnp.where(
            lane_c == 64,
            jnp.sum(grad * values, axis=1, keepdims=True),
            jnp.where(
                lane_c == 65,
                jnp.sum(weighted * shifted, axis=1, keepdims=True),
                jnp.where(lane_c == 66, scale * jnp.sum(weighted, axis=1, keepdims=True), 0.0),
            ),
        )

    def body(group, carry):
        lane = lane_of(SLOT)
        sub = lax.broadcasted_iota(jnp.int32, (SLOT, LANES), 0)
        place = lane % SIDE
        half = lambda ref, c, s: ref[c * SIDE : (c + 1) * SIDE, s * LANES : (s + 1) * LANES]
        stack = lambda ref, c: jnp.concatenate([half(ref, c, s) for s in range(sides)], axis=0)
        for c in range(live):
            tiles = load_channel(slots_g, group, c, lane)
            for s in range(sides):
                value = jnp.concatenate(tiles[s * PER : (s + 1) * PER], axis=0)
                at = (slice(c * SIDE, (c + 1) * SIDE), slice(s * LANES, (s + 1) * LANES))
                field_g[at] = value.astype(BF16)
        for c in range(live):
            row = rows_ref[pl.ds(group * SLOT + c, 1), :]
            high_b, low_b = build_across(row, True, lane, sub)
            grad = stack(field_g, c)
            flow = dot(
                jnp.concatenate([grad, grad], axis=1), jnp.concatenate([high_b, low_b], axis=0)
            )
            high, low = split(flow)
            for s in range(sides):
                at = (slice(c * SIDE, (c + 1) * SIDE), slice(s * LANES, (s + 1) * LANES))
                high_d[at] = high[s * SIDE : (s + 1) * SIDE]
                low_d[at] = low[s * SIDE : (s + 1) * SIDE]
            outer = dot(
                jnp.concatenate([grad, grad], axis=0),
                jnp.concatenate([high_s[group, c], low_s[group, c]], axis=0),
                TN,
            )
            total = None
            for part in range(PER):
                value = None
                for i in range(PER):
                    at = i * SIDE + part * SLOT
                    term = jnp.where(lane // SIDE == i, outer[at : at + SLOT], 0.0)
                    value = term if value is None else value + term
                index = part * SLOT + sub - place
                value = jnp.take_along_axis(
                    value, jnp.clip(index, 0, SIDE - 1) + lane // SIDE * SIDE, axis=1
                )
                value = jnp.where(index >= 0, value, 0.0)
                total = value if total is None else total + value
            total = jnp.sum(total, axis=0, keepdims=True)
            total = total + pltpu.roll(total, 64, 1)
            total = total + pltpu.roll(total, 32, 1)
            sums[pl.ds(group * SLOT + c, 1), :] = jnp.where(lane[0:1] // SIDE == 1, total, 0.0)
        high, low = high_d[...], low_d[...]
        down = high_a[group]
        back = dot(down, high, TN) + dot(down, low, TN) + dot(low_a[group], high, TN)
        wide_ref[...] = back
        source = field_ref[group]
        outer_ref[...] = dot(high, source, NT) + dot(low, source, NT)
        for c in range(live):
            value = stack(wide_ref, c)
            tiles = [value[k * SLOT : (k + 1) * SLOT] for k in range(images)]
            store_channel(slots, group, c, tiles, lane)
            total = None
            for turn in range(PER):
                at = c * SIDE + turn * SLOT
                value = outer_ref[at : at + SLOT, c // PER * LANES : (c // PER + 1) * LANES]
                index = PER * sub + turn - lane
                safe = jnp.clip(index, 0, SIDE - 1)
                index_at = (safe % PER) * TILES + safe // PER + c % PER * SIDE
                value = jnp.take_along_axis(value, index_at, axis=1)
                value = jnp.where(index >= 0, value, 0.0)
                total = value if total is None else total + value
            total = jnp.sum(total, axis=0, keepdims=True)
            total = jnp.where(lane[0:1] < SIDE, total, 0.0)
            sums[pl.ds(group * SLOT + c, 1), :] += total
        return carry

    lax.fori_loop(0, slots.shape[0], body, 0)
    skip = rows_ref[0:channels, 2 * SIDE : 2 * SIDE + 1]
    for image in range(images):
        span = slice(image * CELLS, (image + 1) * CELLS)
        inside = image_mask(1, heights[image], widths[image])
        grad = read_slots(slots_g, image, channels)
        value = read_slots(slots, image, channels) + skip * grad
        gfeat_ref[:, span] = cot_ref[:, span].astype(F32) + jnp.where(inside, value, 0.0)
    small = small + sums[0:channels]
    states, small = chain(small, step_h, step_w, rate_h, rate_w, read_h, read_w)
    for index in range(2):
        pair = jnp.concatenate(states[2 * index : 2 * index + 2], axis=1)
        small_ref[:, index * pair.shape[1] : (index + 1) * pair.shape[1]] = pair
    small_ref[:, 2 * pair.shape[1] :] = small


def chain(total, step_h, step_w, rate_h, rate_w, read_h, read_w):
    out, tail = [], total
    lane = lane_of(total.shape[0])
    for place, first, step, rate, read in (
        (67, 0, step_h, rate_h, read_h), (68, SIDE, step_w, rate_w, read_w),
    ):
        pace = jnp.exp(column(step[...]))
        decay = pace * rate[...]
        to_read = jnp.zeros_like(decay)
        to_decay = jnp.zeros_like(decay)
        for lag in range(SIDE):
            term = total[:, first + lag : first + lag + 1] * jnp.exp(-decay * lag)
            to_read = to_read + term
            if lag:
                to_decay = to_decay - float(lag) * term
        to_decay = to_decay * read[...]
        out += [to_read, pace * to_decay]
        tail = jnp.where(lane == place, jnp.sum(to_decay * decay, axis=1, keepdims=True), tail)
    return out, tail


def join_kernel(count, *refs):
    given, outs = refs[:count], refs[count:]
    tall = outs[0].shape[0]
    for index, out in enumerate(outs):
        at = slice(index * tall, (index + 1) * tall)
        total = given[0][at].astype(F32)
        for ref in given[1:]:
            total = total + ref[at].astype(F32)
        out[...] = total.astype(out.dtype)


def cut_kernel(one_ref, two_ref, first_ref, second_ref):
    cut = first_ref.shape[0]
    first_ref[...] = one_ref[:cut]
    second_ref[...] = two_ref[cut:]


def start_kernel(one_ref, two_ref, arrived_ref, out_one, out_two):
    cut = one_ref.shape[0]
    at = arrived_ref.shape[0] - 2 * cut
    for start, ref, out in ((at, one_ref, out_one), (at + cut, two_ref, out_two)):
        total = ref[...].astype(F32) + arrived_ref[start : start + cut].astype(F32)
        out[...] = total.astype(BF16)


def relay_kernel(one_ref, two_ref, arrived_ref, first_ref, second_ref, out_one, out_two):
    tall = one_ref.shape[0]
    cut = tall // 2
    one = one_ref[...].astype(F32) + arrived_ref[tall : 2 * tall].astype(F32)
    two = two_ref[...].astype(F32) + arrived_ref[2 * tall : 3 * tall].astype(F32)
    out_one[:cut] = (one[:cut] + first_ref[...].astype(F32)).astype(BF16)
    out_one[cut:] = one[cut:].astype(BF16)
    out_two[:cut] = two[:cut].astype(BF16)
    out_two[cut:] = (two[cut:] + second_ref[...].astype(F32)).astype(BF16)


def finish_kernel(
    half, mine_ref, other_ref, small_ref, sibling_ref,
    gstep_h, grate_h, gread_h, gstep_w, grate_w, gread_w, gskip, ggain, gshift, gin, ginb, gout,
    gbias, gscale,
):
    units, count = gin.shape
    channels, states = grate_h.shape
    keep = units // 2
    deep = deep_of(mine_ref, count)
    first = half[0] == 0
    mine, other = mine_ref[...], other_ref[...]
    bias = []
    for at, part in ((0, jnp.where(first, mine, other)), (keep, jnp.where(first, other, mine))):
        for index in range(2 * count // LANES):
            out = gin if index < count // LANES else gout
            lanes = pl.ds(index * LANES % count, LANES)
            out[at : at + keep, lanes] = part[index * deep : index * deep + keep]
        bias.append(unfold(part[-EDGE:], 0, deep)[:keep])
    ginb[...] = as_row(jnp.concatenate(bias, axis=0))
    norms = mine[-EDGE:] + other[-EDGE:]
    ggain[...] = as_row(unfold(norms, 1, deep)[:channels])
    gshift[...] = as_row(unfold(norms, 2, deep)[:channels])
    total = small_ref[...] + sibling_ref[...]
    for index, ref in enumerate((gread_h, grate_h, gread_w, grate_w)):
        ref[...] = total[:, index * states : (index + 1) * states]
    total = total[:, 4 * states :]
    gskip[...] = as_row(total[:, 64:65])
    gscale[...] = as_row(total[:, 65:66])
    gbias[...] = as_row(total[:, 66:67])
    gstep_h[...] = as_row(total[:, 67:68])
    gstep_w[...] = as_row(total[:, 68:69])


def deep_of(ref, count, shards=1):
    return (ref.shape[0] // shards - EDGE) * LANES // (2 * count)


def fold(columns, deep):
    lane = lane_of(EDGE)
    pieces = deep // EDGE
    tile = jnp.zeros((EDGE, LANES), F32)
    for index, value in enumerate(columns):
        if value is not None:
            for p in range(pieces):
                part = value[p * EDGE : (p + 1) * EDGE]
                tile = jnp.where(lane == index * pieces + p, part, tile)
    return tile


def unfold(tile, index, deep):
    pieces = deep // EDGE
    first = index * pieces
    return jnp.concatenate([tile[:, first + p : first + p + 1] for p in range(pieces)], axis=0)


def pack_kernel(half, in_ref, out_ref, bias_ref, gain_ref, shift_ref, pack_ref):
    own, count = out_ref.shape
    deep = deep_of(pack_ref, count)
    channels = gain_ref.shape[1]
    keep = own // 2
    row = lax.broadcasted_iota(jnp.int32, (deep, own), 0)
    col = lax.broadcasted_iota(jnp.int32, (deep, own), 1)
    pick = jnp.where((col == row + half[0] * keep) & (row < keep), 1.0, 0.0).astype(BF16)
    first = dot(pick, in_ref[...]).astype(BF16)
    second = dot(pick, out_ref[...]).astype(BF16)
    bias = dot(pick, jnp.broadcast_to(bias_ref[...], (LANES, own)), NT)
    row = lax.broadcasted_iota(jnp.int32, (deep, channels), 0)
    col = lax.broadcasted_iota(jnp.int32, (deep, channels), 1)
    pick = jnp.where(col == row, 1.0, 0.0).astype(BF16)
    gain = dot(pick, jnp.broadcast_to(gain_ref[...], (LANES, channels)), NT)
    shift = dot(pick, jnp.broadcast_to(shift_ref[...], (LANES, channels)), NT)
    half_tiles = count // LANES
    for index in range(2 * half_tiles):
        source = first if index < half_tiles else second
        lanes = slice(index % half_tiles * LANES, (index % half_tiles + 1) * LANES)
        pack_ref[index * deep : (index + 1) * deep] = source[:, lanes]
    pack_ref[2 * half_tiles * deep :] = fold((bias, gain, shift), deep).astype(BF16)


ROOT = math.sqrt(2.0 / math.pi)


def shards_of(ref, count, deep):
    height = 2 * count // LANES * deep + EDGE
    return range(0, ref.shape[0], height)


def perceptron(refs, act, down, deep):
    count = act.shape[0]
    tiles = count // LANES

    def matrix(first):
        rows = []
        for ref in refs:
            for base in shards_of(ref, count, deep):
                starts = [base + (first + j) * deep for j in range(tiles)]
                rows.append(jnp.concatenate([ref[at : at + deep] for at in starts], axis=1))
        return jnp.concatenate(rows, axis=0)

    bias = []
    for ref in refs:
        for base in shards_of(ref, count, deep):
            at = base + 2 * tiles * deep
            bias.append(unfold(ref[at : at + EDGE].astype(F32), 0, deep))
    w_in, w_out = matrix(0), matrix(tiles)
    v = dot(w_in, act) + jnp.concatenate(bias, axis=0)
    square = v * v
    half = 0.5 * jnp.tanh(v * (ROOT * 0.044715 * square + ROOT)) + 0.5
    full = v * half
    hidden = full.astype(BF16)
    slope = half + full * (1.0 - half) * (6.0 * ROOT * 0.044715 * square + 2.0 * ROOT)
    low = (dot(w_out, down) * slope).astype(BF16)
    g_bias = jnp.sum(low.astype(F32), axis=1, keepdims=True)
    grads = (dot(low, act, NT).astype(BF16), dot(hidden, down, NT).astype(BF16), g_bias)
    return dot(w_out, hidden, TN), dot(w_in, low, TN), grads


def put(ref, grads, start, deep, edges=None):
    count = grads[0].shape[1]
    tiles = count // LANES
    for base in shards_of(ref, count, deep):
        for index in range(2 * tiles):
            lanes = slice(index % tiles * LANES, (index % tiles + 1) * LANES)
            at = base + index * deep
            ref[at : at + deep] = grads[index // tiles][start : start + deep, lanes]
        edge = fold((grads[2][start : start + deep],), deep)
        if edges is None:
            at = base + 2 * tiles * deep
            ref[at : at + EDGE] = edge.astype(BF16)
        else:
            at = start // deep * EDGE
            edges[at : at + EDGE] = edge
        start += deep
    return start


def spots_of(near, devices, where_ref):
    z, xy = where_ref[0], where_ref[1]
    for d in range(devices):
        spot = ((d % near) ^ xy) * (devices // near) + ((d // near) ^ z)
        yield d, pl.multiple_of(spot * EDGE, EDGE)


def mlp_first(near, pieces, deep, where_ref, given_ref, *refs):
    own_in, refs = refs[:pieces], refs[pieces:]
    other_in, refs = refs[:pieces], refs[pieces:]
    gother_ref, active, downs, normal, inv_ref, gains, sum_ref, grad_ref, ext = refs
    devices, _, channels, _ = given_ref.shape
    count = active.shape[0]

    value = jnp.concatenate([given_ref[d, 0].astype(F32) for d in range(devices)], axis=0)
    mean = jnp.mean(value, axis=0, keepdims=True)
    value = value - mean
    inv = lax.rsqrt(jnp.mean(value * value, axis=0, keepdims=True) + EPS)
    value = value * inv
    normal[...] = value
    inv_ref[...] = inv
    down = jnp.concatenate([given_ref[d, 1].astype(F32) for d in range(devices)], axis=0)
    downs[...] = down.astype(BF16)
    at = 0
    for ref in own_in:
        for base in shards_of(ref, count, deep):
            edge = base + 2 * count // LANES * deep
            ext[at : at + EDGE] = ref[edge : edge + EDGE].astype(F32)
            at += EDGE
    lane = lane_of(channels)
    for d, spot in spots_of(near, devices, where_ref):
        tile = ext[pl.ds(spot, EDGE), :]
        gain, shift = (unfold(tile, index, deep)[:channels] for index in (1, 2))
        pair = jnp.where(lane == 1, gain, jnp.where(lane == 2, shift, 0.0))
        gains[d * channels : (d + 1) * channels] = pair
    active[...] = (value * gains[:, 1:2] + gains[:, 2:3]).astype(BF16)
    sums, total, grads = perceptron(other_in, active[...], downs[...], deep)
    put(gother_ref, grads, 0, deep)
    sum_ref[...] = sums
    grad_ref[...] = total


def mlp_second(
    near, pieces, deep, where_ref, active, downs, normal_ref, inv_ref, gains, sum_ref, grad_ref,
    *refs,
):
    own_in, refs = refs[:pieces], refs[pieces:]
    both_ref, refs = refs[0], refs[1:]
    own_out, (gext,) = refs[:pieces], refs[pieces:]
    count = active.shape[0]
    devices, _, channels, _ = both_ref.shape

    sums, total, grads = perceptron(own_in, active[...], downs[...], deep)
    start = 0
    for ref in own_out:
        start = put(ref, grads, start, deep, gext)
    summed = sum_ref[...] + sums
    agrad = grad_ref[...] + total
    norm = normal_ref[...]
    scaled = agrad * gains[:, 1:2]
    first = jnp.mean(scaled, axis=0, keepdims=True)
    second = jnp.mean(scaled * norm, axis=0, keepdims=True)
    mgrad = (scaled - first - norm * second) * inv_ref[...]
    for d in range(devices):
        both_ref[d, 0] = mgrad[d * channels : (d + 1) * channels].astype(BF16)
        both_ref[d, 1] = summed[d * channels : (d + 1) * channels].astype(BF16)
    by_gain = jnp.sum(agrad * norm, axis=1, keepdims=True)
    by_shift = jnp.sum(agrad, axis=1, keepdims=True)
    for d, spot in spots_of(near, devices, where_ref):
        parts = []
        for value in (by_gain, by_shift):
            value = value[d * channels : (d + 1) * channels]
            if channels < deep:
                value = jnp.concatenate([value, jnp.zeros((deep - channels, 1), F32)], axis=0)
            parts.append(value)
        gext[pl.ds(spot, EDGE), :] += fold((None, *parts), deep)
    at = 0
    for ref in own_out:
        for base in shards_of(ref, count, deep):
            edge = base + 2 * count // LANES * deep
            ref[edge : edge + EDGE] = gext[at : at + EDGE].astype(BF16)
            at += EDGE


def whole(shape):
    return pl.BlockSpec(shape, lambda i: (0,) * len(shape))


def params(mebibytes):
    return pltpu.CompilerParams(vmem_limit_bytes=mebibytes << 20)


def cost(micros):
    return pl.CostEstimate(flops=0, transcendentals=0, bytes_accessed=micros * 3_000_000)


def join(deep, arrays, count):
    full = pl.BlockSpec(memory_space=pltpu.VMEM)
    width = arrays[0].shape[1]
    return pl.pallas_call(
        partial(join_kernel, len(arrays)),
        out_shape=[
            pltpu.VMEM((deep, width), BF16 if i else F32) for i in range(count)
        ],
        in_specs=[full] * len(arrays),
        out_specs=[full] * count,
        compiler_params=params(16),
        cost_estimate=pl.CostEstimate(flops=1 if count > 1 else 1, transcendentals=0, bytes_accessed=1_000_000),
        name="join",
    )(*arrays)


def relay(*arrays):
    full = pl.BlockSpec(memory_space=pltpu.VMEM)
    shape = pltpu.VMEM(arrays[0].shape, BF16)
    return pl.pallas_call(
        relay_kernel,
        out_shape=(shape, shape),
        in_specs=[full] * 5,
        out_specs=(full, full),
        compiler_params=params(16),
        cost_estimate=pl.CostEstimate(flops=100_000_000_000, transcendentals=0, bytes_accessed=1_000_000),
        name="relay",
    )(*arrays)


SMEM = pl.BlockSpec(memory_space=pltpu.SMEM)


def per_device(
    ch, features, cotangent, heights, widths, step_height, rate_height, readout_height,
    step_width, rate_width, readout_width, skip_gain, norm_gain, norm_shift, in_weight,
    in_bias, out_weight, out_bias, layer_scale,
):
    channels, cells = features.shape
    count = in_weight.shape[0]
    pin = lambda v: pltpu.with_memory_space_constraint(v, pltpu.HBM)
    units = in_weight.shape[1]
    states = rate_height.shape[1]
    images = cells // CELLS
    tokens = cells // ch
    parts = CELLS // tokens
    far = 4
    near = ch // far
    deep = -(-(units // 2) // 16) * 16
    tall_one = 2 * count // LANES * deep + EDGE
    width = LANES
    near_groups = [[f * near + i for i in range(near)] for f in range(far)]
    row = lambda v: v.reshape(1, -1)
    exchange = lambda v: lax.ppermute(v, "img", [(0, 1), (1, 0)])
    flip = lambda v, bits: lax.ppermute(v, "ch", [(i, i ^ bits) for i in range(ch)])
    swap = lambda v, groups=None: lax.all_to_all(
        v, "ch", split_axis=0, concat_axis=0, tiled=True, axis_index_groups=groups
    )
    pair = lambda *arrays: lax.optimization_barrier(arrays)
    half = lax.axis_index("img").astype(jnp.int32)
    place = lax.axis_index("ch").astype(jnp.int32)
    full = pl.BlockSpec(memory_space=pltpu.VMEM)

    pack = pl.pallas_call(
        pack_kernel,
        out_shape=jax.ShapeDtypeStruct((tall_one, width), BF16),
        in_specs=[SMEM] + [full] * 5,
        out_specs=full,
        compiler_params=params(16),
        cost_estimate=cost(2),
        name="pack",
    )(
        half.reshape(1), pin(in_weight.T), pin(out_weight), pin(row(in_bias)), pin(row(norm_gain)),
        pin(row(norm_shift)),
    )
    pack, features_after = pair(pack, features)
    shards = [pack] + [flip(pack, bits * near) for bits in range(1, far)]

    groups = -(-channels // SLOT)
    square = (SLOT * SIDE, images // PER * LANES)
    toeplitz = pltpu.VMEM((SLOT * SIDE, SLOT * SIDE), BF16)
    slots = pltpu.VMEM((groups, images * TILES * SLOT, LANES), F32)
    both_shape = (ch, 2, channels, tokens)
    given, taps = pl.pallas_call(
        forward_kernel,
        out_shape=(
            jax.ShapeDtypeStruct(both_shape, BF16),
            jax.ShapeDtypeStruct((groups * SLOT, LANES), F32),
        ),
        in_specs=[SMEM, SMEM] + [full] * 10,
        out_specs=(full, full),
        scratch_shapes=[
            slots, toeplitz, toeplitz, pltpu.VMEM(square, BF16), pltpu.VMEM(square, F32),
        ],
        compiler_params=params(16),
        cost_estimate=cost(6),
        name="mixer_forward",
    )(
        pin(heights), pin(widths), pin(features_after), pin(cotangent), pin(row(layer_scale)),
        pin(row(step_height)), pin(row(step_width)), pin(rate_height), pin(rate_width),
        pin(readout_height), pin(readout_width), pin(row(skip_gain)),
    )
    given, *shards = pair(given, *shards)
    given = swap(given)
    shard = jnp.concatenate(shards, axis=0)
    if near == 4:
        cut = far * tall_one // 2
        beside, above = pair(flip(shard, 1), flip(shard, 2))
        ends = pl.pallas_call(
            cut_kernel,
            out_shape=[jax.ShapeDtypeStruct((cut, width), BF16)] * 2,
            in_specs=[full] * 2,
            out_specs=[full] * 2,
            compiler_params=params(16),
            cost_estimate=pl.CostEstimate(flops=100_000_000_000, transcendentals=0, bytes_accessed=1_000_000),
            name="ends",
        )(beside, above)
        own = [shard, beside, above, flip(ends[0], 2), flip(ends[1], 1)]
        where = jnp.stack([place // near, place % near])
    else:
        own = [swap(jnp.broadcast_to(shard[None], (near,) + shard.shape), near_groups)]
        own = [own[0].reshape(ch * tall_one, width)]
        where = jnp.stack([place // near, place * 0])
    other = [exchange(piece) for piece in own]

    rows = ch * tall_one
    pieces = len(own)
    plane = jax.ShapeDtypeStruct((count, tokens), F32)
    token_low = jax.ShapeDtypeStruct((count, tokens), BF16)
    gother, *state = pl.pallas_call(
        partial(mlp_first, near, pieces, deep),
        out_shape=[
            jax.ShapeDtypeStruct((rows, width), BF16), token_low, token_low, plane,
            jax.ShapeDtypeStruct((1, tokens), F32), jax.ShapeDtypeStruct((count, LANES), F32),
            plane, plane,
        ],
        in_specs=[SMEM] + [full] * (1 + 2 * pieces),
        out_specs=[full] * 8,
        scratch_shapes=[pltpu.VMEM((ch * EDGE, LANES), F32)],
        compiler_params=params(16),
        cost_estimate=cost(5),
        name="mlp_first",
    )(where, given, *own, *other)
    arrived = exchange(gother)
    both, *gown = pl.pallas_call(
        partial(mlp_second, near, pieces, deep),
        out_shape=[jax.ShapeDtypeStruct(both_shape, BF16)]
        + [jax.ShapeDtypeStruct(piece.shape, BF16) for piece in own],
        in_specs=[SMEM] + [full] * (7 + pieces),
        out_specs=[full] * (1 + pieces),
        scratch_shapes=[pltpu.VMEM((ch * EDGE, LANES), F32)],
        compiler_params=params(16),
        cost_estimate=cost(5),
        name="mlp_second",
    )(where, *state, *own)
    both = swap(both)
    tall = far * tall_one
    if near == 4:
        cut = tall // 2
        part = pltpu.VMEM(gown[3].shape, BF16)
        one, two = pl.pallas_call(
            start_kernel,
            out_shape=(part, part),
            in_specs=[full] * 3,
            out_specs=(full, full),
            compiler_params=params(16),
            cost_estimate=cost(1),
            name="start",
        )(gown[3], gown[4], arrived)
        one, two = pair(flip(one, 2), flip(two, 1))
        one, two = relay(gown[1], gown[2], arrived, one, two)
        features_last, one, two = pair(features, one, two)
        first, second, *sent = gown[0], arrived, flip(one, 1), flip(two, 2)
    else:
        features_last = features
        total = (gown[0].astype(F32) + arrived.astype(F32)).astype(BF16)
        sent = list(swap(total.reshape(near, tall, width), near_groups))
        first, second, *sent = sent
    landed = [first, second, *sent]
    table = pltpu.HBM((groups,) + toeplitz.shape, BF16)
    strip = pltpu.HBM((groups, SLOT, images * SLOT, LANES), BF16)
    prepared = pl.pallas_call(
        prepare_kernel,
        out_shape=(
            pltpu.HBM((groups,) + square, BF16), table, table, strip, strip,
        ),
        in_specs=[SMEM, SMEM, full, full],
        out_specs=(full,) * 5,
        scratch_shapes=[slots, pltpu.VMEM(square, F32)],
        compiler_params=params(16),
        cost_estimate=cost(4),
        name="mixer_prepare",
    )(pin(heights), pin(widths), pin(features_last), taps)
    *landed, _ = pair(*landed, prepared[0])
    shards = join(tall_one, landed, far)
    shards = [shards[0]] + [flip(v, (i + 1) * near) for i, v in enumerate(shards[1:])]
    result, grad_features, small = pl.pallas_call(
        backward_kernel,
        out_shape=(
            jax.ShapeDtypeStruct((channels, cells), BF16),
            jax.ShapeDtypeStruct((channels, cells), F32),
            jax.ShapeDtypeStruct((channels, LANES + 4 * states), F32),
        ),
        in_specs=[SMEM, SMEM] + [full] * 17,
        out_specs=(full,) * 3,
        scratch_shapes=[
            slots, slots, pltpu.VMEM(square, BF16),
            pltpu.VMEM((SLOT * SIDE, SLOT * SIDE), F32), pltpu.VMEM(square, BF16),
            pltpu.VMEM(square, BF16), pltpu.VMEM(square, F32),
            pltpu.VMEM((groups * SLOT, LANES), F32),
        ],
        compiler_params=params(16),
        cost_estimate=cost(7),
        name="mixer_backward",
    )(
        pin(heights), pin(widths), pin(features), pin(cotangent), both, taps,
        pin(row(layer_scale)), pin(row(out_bias)), pin(row(step_height)), pin(row(step_width)),
        pin(rate_height), pin(rate_width), pin(readout_height), pin(readout_width),
        *map(pin, prepared),
    )
    *shards, small = pair(*shards, small)
    (mine,) = join(tall_one, shards, 1)
    vector_out = jax.ShapeDtypeStruct((1, channels), F32)
    state_out = jax.ShapeDtypeStruct((channels, states), F32)
    weight_out = jax.ShapeDtypeStruct((units, count), F32)
    outs = pl.pallas_call(
        finish_kernel,
        out_shape=(
            vector_out, state_out, state_out, vector_out, state_out, state_out, vector_out,
            vector_out, vector_out, weight_out, jax.ShapeDtypeStruct((1, units), F32), weight_out,
            vector_out, vector_out,
        ),
        in_specs=[SMEM] + [full] * 4,
        out_specs=(full,) * 14,
        compiler_params=params(16),
        cost_estimate=cost(1),
        name="finish",
    )(half.reshape(1), mine, exchange(mine), small, exchange(small))
    outs = [v.reshape(-1) if v.shape[0] == 1 else v for v in outs]
    outs[9] = outs[9].T
    return (result, grad_features, *outs)


def solution(mesh):
    wide, split, tall = P("ch", "img"), P("ch"), P("ch", None)
    return jax.shard_map(
        partial(per_device, mesh.shape["ch"]),
        mesh=mesh,
        in_specs=(
            wide, wide, P("img"), P("img"), split, tall, tall, split, tall, tall, split, split,
            split, P(None, "ch"), split, tall, split, split,
        ),
        out_specs=(
            wide, wide, split, tall, tall, split, tall, tall, split, split, split,
            P(None, "ch"), split, tall, split, split,
        ),
        check_vma=False,
    )
```

```python
import math
from functools import partial

import jax
import jax.numpy as jnp
from jax import lax
from jax.experimental import pallas as pl
from jax.experimental.pallas import tpu as pltpu
from jax.sharding import PartitionSpec as P

SIDE = 32
CELLS = SIDE * SIDE
LANES = 128
PER = LANES // SIDE
SLOT = 8
EDGE = 16
TILES = CELLS // LANES
EPS = 1e-06
F32 = jnp.float32
BF16 = jnp.bfloat16


def column(row):
    n = row.shape[1]
    eye = lax.broadcasted_iota(jnp.int32, (n, n), 0) == lax.broadcasted_iota(jnp.int32, (n, n), 1)
    return jnp.sum(jnp.where(eye, jnp.broadcast_to(row, (n, n)), 0.0), axis=1, keepdims=True)


def as_row(col):
    n = col.shape[0]
    eye = lax.broadcasted_iota(jnp.int32, (n, n), 0) == lax.broadcasted_iota(jnp.int32, (n, n), 1)
    return jnp.sum(jnp.where(eye, jnp.broadcast_to(col, (n, n)), 0.0), axis=0, keepdims=True)


def image_mask(rows, height, width):
    cell = lax.broadcasted_iota(jnp.int32, (SLOT, CELLS), 1)
    inside = jnp.where((cell // SIDE < height) & (cell % SIDE < width), 1.0, 0.0)
    return jnp.concatenate([inside] * -(-rows // SLOT), axis=0)[:rows]


def lane_of(rows):
    return lax.broadcasted_iota(jnp.int32, (rows, LANES), 1)


def fill_slots(slots, value, image):
    channels = value.shape[0]
    for group in range(slots.shape[0]):
        live = min(SLOT, channels - group * SLOT)
        for k in range(TILES):
            at = (image * TILES + k) * SLOT
            part = value[group * SLOT : group * SLOT + live, k * LANES : (k + 1) * LANES]
            slots[group, pl.ds(at, live), :] = part


def read_slots(slots, image, channels):
    rows = []
    for group in range(slots.shape[0]):
        live = min(SLOT, channels - group * SLOT)
        at = [(image * TILES + k) * SLOT for k in range(TILES)]
        rows.append(jnp.concatenate([slots[group, pl.ds(a, live), :] for a in at], axis=1))
    return jnp.concatenate(rows, axis=0) if len(rows) > 1 else rows[0]


def cross(tiles, lane):
    for bit, far in ((2, 64), (1, 32)):
        low = (lane & far) == 0
        out = list(tiles)
        for k in range(len(tiles)):
            if not k & bit:
                one, two = tiles[k], tiles[k | bit]
                out[k] = jnp.where(low, one, pltpu.roll(two, far, 1))
                out[k | bit] = jnp.where(low, pltpu.roll(one, LANES - far, 1), two)
        tiles = out
    return tiles


def load_channel(slots, group, c, lane):
    count = slots.shape[1] // SLOT
    value = slots[group, pl.ds(c, count, stride=SLOT), :]
    return cross([value[k * SLOT : (k + 1) * SLOT] for k in range(count // SLOT)], lane)


def store_channel(slots, group, c, tiles, lane):
    count = slots.shape[1] // SLOT
    slots[group, pl.ds(c, count, stride=SLOT), :] = jnp.concatenate(cross(tiles, lane), axis=0)


def split(value):
    high = value.astype(BF16)
    return high, (value - high.astype(F32)).astype(BF16)


def pick(row, index):
    spread = jnp.broadcast_to(row, index.shape)
    value = jnp.take_along_axis(spread, jnp.clip(index, 0, LANES - 1), axis=1)
    return value


def build_down(row, c, high_ref, low_ref, lane, sub):
    place = lane % SIDE
    source = (place % TILES) * PER + place // TILES
    here = lane // SIDE == c % PER
    parts = []
    for turn in range(PER):
        index = PER * sub + turn - source
        parts.append(jnp.where(here & (index >= 0), pick(row, index), 0.0))
    high, low = split(jnp.concatenate(parts, axis=0))
    at = (slice(c * SIDE, (c + 1) * SIDE), slice(c // PER * LANES, (c // PER + 1) * LANES))
    high_ref[at] = high
    low_ref[at] = low


def build_across(row, turned, lane, sub):
    place = lane % SIDE
    highs, lows = [], []
    for part in range(PER):
        own = part * SLOT + sub
        index = own - place if turned else place - own
        value = jnp.where(index >= 0, pick(row, index + SIDE), 0.0)
        high = value.astype(BF16).astype(F32)
        highs.append(high)
        lows.append(value - high)
    spread = lambda parts: jnp.concatenate(
        [jnp.where(lane // SIDE == i, p, 0.0) for i in range(PER) for p in parts], axis=0
    ).astype(BF16)
    return spread(highs), spread(lows)


def taps_of(step_h, step_w, rate_h, rate_w, read_h, read_w, skip_ref):
    channels = rate_h.shape[0]
    lane = lane_of(channels)
    kept = jnp.zeros((channels, LANES), F32)
    decay_h = jnp.exp(column(step_h[...])) * rate_h[...]
    decay_w = jnp.exp(column(step_w[...])) * rate_w[...]
    for lag in range(SIDE):
        tap = jnp.sum(read_h[...] * jnp.exp(-decay_h * lag), axis=1, keepdims=True)
        kept = jnp.where(lane == lag, tap, kept)
        tap = jnp.sum(read_w[...] * jnp.exp(-decay_w * lag), axis=1, keepdims=True)
        kept = jnp.where(lane == SIDE + lag, tap, kept)
    return jnp.where(lane == 2 * SIDE, column(skip_ref[...]), kept)


def dot(a, b, dims=(((1,), (0,)), ((), ()))):
    return lax.dot_general(a, b, dims, preferred_element_type=F32)


NT = (((1,), (1,)), ((), ()))
TN = (((0,), (0,)), ((), ()))


def forward_kernel(
    heights, widths, feat_ref, cot_ref, scale_ref, step_h, step_w, rate_h, rate_w, read_h,
    read_w, skip_ref, out_ref, rows_ref, slots, high_a, low_a, field, tall,
):
    channels, cells = feat_ref.shape
    images = cells // CELLS
    rows_ref[0:channels] = taps_of(step_h, step_w, rate_h, rate_w, read_h, read_w, skip_ref)
    for ref in (high_a, low_a, field):
        ref[...] = jnp.zeros_like(ref)
    for image in range(images):
        inside = image_mask(channels, heights[image], widths[image])
        value = feat_ref[:, image * CELLS : (image + 1) * CELLS].astype(F32)
        fill_slots(slots, value * inside, image)
    live = min(SLOT, channels)
    sides = images // PER

    scratch = (high_a, low_a, field, tall)

    def body(group, carry):
        high_a, low_a, field, tall = (ref.at[group] for ref in scratch)
        lane = lane_of(SLOT)
        sub = lax.broadcasted_iota(jnp.int32, (SLOT, LANES), 0)
        for c in range(live):
            row = rows_ref[pl.ds(group * SLOT + c, 1), :]
            build_down(row, c, high_a, low_a, lane, sub)
            tiles = load_channel(slots, group, c, lane)
            for s in range(sides):
                value = jnp.concatenate(tiles[s * PER : (s + 1) * PER], axis=0)
                field[c * SIDE : (c + 1) * SIDE, s * LANES : (s + 1) * LANES] = value.astype(BF16)
        source = field[...]
        tall[...] = dot(high_a[...], source) + dot(low_a[...], source)
        for c in range(live):
            row = rows_ref[pl.ds(group * SLOT + c, 1), :]
            high_b, low_b = build_across(row, False, lane, sub)
            value = jnp.concatenate(
                [tall[c * SIDE : (c + 1) * SIDE, s * LANES : (s + 1) * LANES] for s in range(sides)],
                axis=0,
            )
            high, low = split(value)
            value = dot(
                jnp.concatenate([high, low, high], axis=1),
                jnp.concatenate([high_b, high_b, low_b], axis=0),
            )
            tiles = [value[k * SLOT : (k + 1) * SLOT] for k in range(images)]
            store_channel(slots, group, c, tiles, lane)
        return carry

    for group in range(slots.shape[0]):
        body(group, 0)
    wide = out_ref.shape[3]
    parts = CELLS // wide
    skip = rows_ref[0:channels, 2 * SIDE : 2 * SIDE + 1]
    scale = column(scale_ref[...])
    for image in range(images):
        span = slice(image * CELLS, (image + 1) * CELLS)
        inside = image_mask(channels, heights[image], widths[image])
        value = read_slots(slots, image, channels) + skip * feat_ref[:, span].astype(F32)
        value = (value * inside).astype(BF16)
        down = cot_ref[:, span].astype(F32) * scale
        down = (down * inside).astype(BF16)
        for j in range(parts):
            out_ref[image * parts + j, 0] = value[:, j * wide : (j + 1) * wide]
            out_ref[image * parts + j, 1] = down[:, j * wide : (j + 1) * wide]


def prepare_kernel(
    heights, widths, feat_ref, rows_ref, field_ref, high_a, low_a, high_s, low_s, slots, tall
):
    channels, cells = feat_ref.shape
    images = cells // CELLS
    live = min(SLOT, channels)
    sides = images // PER
    for ref in (field_ref, high_a, low_a):
        ref[...] = jnp.zeros_like(ref)
    for image in range(images):
        inside = image_mask(channels, heights[image], widths[image])
        value = feat_ref[:, image * CELLS : (image + 1) * CELLS].astype(F32)
        fill_slots(slots, value * inside, image)

    def body(group, carry):
        lane = lane_of(SLOT)
        sub = lax.broadcasted_iota(jnp.int32, (SLOT, LANES), 0)
        for c in range(live):
            row = rows_ref[pl.ds(group * SLOT + c, 1), :]
            build_down(row, c, high_a.at[group], low_a.at[group], lane, sub)
            tiles = load_channel(slots, group, c, lane)
            for s in range(sides):
                value = jnp.concatenate(tiles[s * PER : (s + 1) * PER], axis=0)
                at = (group, slice(c * SIDE, (c + 1) * SIDE), slice(s * LANES, (s + 1) * LANES))
                field_ref[at] = value.astype(BF16)
        source = field_ref[group]
        tall[...] = dot(high_a[group], source) + dot(low_a[group], source)
        for c in range(live):
            value = jnp.concatenate(
                [tall[c * SIDE : (c + 1) * SIDE, s * LANES : (s + 1) * LANES] for s in range(sides)],
                axis=0,
            )
            high, low = split(value)
            high_s[group, c] = high
            low_s[group, c] = low
        return carry

    lax.fori_loop(0, slots.shape[0], body, 0)


def backward_kernel(
    heights, widths, feat_ref, cot_ref, both_ref, rows_ref, scale_ref, bias_ref,
    step_h, step_w, rate_h, rate_w, read_h, read_w, field_ref, high_a, low_a, high_s, low_s,
    result_ref, gfeat_ref, small_ref, slots, slots_g, field_g, outer_ref, high_d, low_d, wide_ref, sums,
):
    channels, cells = feat_ref.shape
    images = cells // CELLS
    live = min(SLOT, channels)
    sides = images // PER
    wide = both_ref.shape[3]
    parts = CELLS // wide
    for ref in (sums, field_g, high_d, low_d):
        ref[...] = jnp.zeros_like(ref)
    lane_c = lane_of(channels)
    scale = column(scale_ref[...])
    bias = column(bias_ref[...])
    small = jnp.zeros((channels, LANES), F32)
    for image in range(images):
        span = slice(image * CELLS, (image + 1) * CELLS)
        inside = image_mask(channels, heights[image], widths[image])
        values = feat_ref[:, span].astype(F32)
        grad = jnp.concatenate(
            [both_ref[image * parts + j, 0].astype(F32) for j in range(parts)], axis=1
        )
        grad = grad * inside
        fill_slots(slots_g, grad, image)
        shifted = jnp.concatenate(
            [both_ref[image * parts + j, 1].astype(F32) for j in range(parts)], axis=1
        )
        shifted = shifted + bias
        result = values + inside * (scale * shifted)
        result_ref[:, span] = result.astype(BF16)
        weighted = cot_ref[:, span].astype(F32) * inside
        small = small + jnp.where(
            lane_c == 64,
            jnp.sum(grad * values, axis=1, keepdims=True),
            jnp.where(
                lane_c == 65,
                jnp.sum(weighted * shifted, axis=1, keepdims=True),
                jnp.where(lane_c == 66, scale * jnp.sum(weighted, axis=1, keepdims=True), 0.0),
            ),
        )

    def body(group, carry):
        lane = lane_of(SLOT)
        sub = lax.broadcasted_iota(jnp.int32, (SLOT, LANES), 0)
        place = lane % SIDE
        half = lambda ref, c, s: ref[c * SIDE : (c + 1) * SIDE, s * LANES : (s + 1) * LANES]
        stack = lambda ref, c: jnp.concatenate([half(ref, c, s) for s in range(sides)], axis=0)
        for c in range(live):
            tiles = load_channel(slots_g, group, c, lane)
            for s in range(sides):
                value = jnp.concatenate(tiles[s * PER : (s + 1) * PER], axis=0)
                at = (slice(c * SIDE, (c + 1) * SIDE), slice(s * LANES, (s + 1) * LANES))
                field_g[at] = value.astype(BF16)
        for c in range(live):
            row = rows_ref[pl.ds(group * SLOT + c, 1), :]
            high_b, low_b = build_across(row, True, lane, sub)
            grad = stack(field_g, c)
            flow = dot(
                jnp.concatenate([grad, grad], axis=1), jnp.concatenate([high_b, low_b], axis=0)
            )
            high, low = split(flow)
            for s in range(sides):
                at = (slice(c * SIDE, (c + 1) * SIDE), slice(s * LANES, (s + 1) * LANES))
                high_d[at] = high[s * SIDE : (s + 1) * SIDE]
                low_d[at] = low[s * SIDE : (s + 1) * SIDE]
            outer = dot(
                jnp.concatenate([grad, grad], axis=0),
                jnp.concatenate([high_s[group, c], low_s[group, c]], axis=0),
                TN,
            )
            total = None
            for part in range(PER):
                value = None
                for i in range(PER):
                    at = i * SIDE + part * SLOT
                    term = jnp.where(lane // SIDE == i, outer[at : at + SLOT], 0.0)
                    value = term if value is None else value + term
                index = part * SLOT + sub - place
                value = jnp.take_along_axis(
                    value, jnp.clip(index, 0, SIDE - 1) + lane // SIDE * SIDE, axis=1
                )
                value = jnp.where(index >= 0, value, 0.0)
                total = value if total is None else total + value
            total = jnp.sum(total, axis=0, keepdims=True)
            total = total + pltpu.roll(total, 64, 1)
            total = total + pltpu.roll(total, 32, 1)
            sums[pl.ds(group * SLOT + c, 1), :] = jnp.where(lane[0:1] // SIDE == 1, total, 0.0)
        high, low = high_d[...], low_d[...]
        down = high_a[group]
        back = dot(down, high, TN) + dot(down, low, TN) + dot(low_a[group], high, TN)
        wide_ref[...] = back
        source = field_ref[group]
        outer_ref[...] = dot(high, source, NT) + dot(low, source, NT)
        for c in range(live):
            value = stack(wide_ref, c)
            tiles = [value[k * SLOT : (k + 1) * SLOT] for k in range(images)]
            store_channel(slots, group, c, tiles, lane)
            total = None
            for turn in range(PER):
                at = c * SIDE + turn * SLOT
                value = outer_ref[at : at + SLOT, c // PER * LANES : (c // PER + 1) * LANES]
                index = PER * sub + turn - lane
                safe = jnp.clip(index, 0, SIDE - 1)
                index_at = (safe % PER) * TILES + safe // PER + c % PER * SIDE
                value = jnp.take_along_axis(value, index_at, axis=1)
                value = jnp.where(index >= 0, value, 0.0)
                total = value if total is None else total + value
            total = jnp.sum(total, axis=0, keepdims=True)
            total = jnp.where(lane[0:1] < SIDE, total, 0.0)
            sums[pl.ds(group * SLOT + c, 1), :] += total
        return carry

    lax.fori_loop(0, slots.shape[0], body, 0)
    skip = rows_ref[0:channels, 2 * SIDE : 2 * SIDE + 1]
    for image in range(images):
        span = slice(image * CELLS, (image + 1) * CELLS)
        inside = image_mask(channels, heights[image], widths[image])
        grad = read_slots(slots_g, image, channels)
        value = read_slots(slots, image, channels) + skip * grad
        gfeat_ref[:, span] = cot_ref[:, span].astype(F32) + value * inside
    small = small + sums[0:channels]
    states, small = chain(small, step_h, step_w, rate_h, rate_w, read_h, read_w)
    for index in range(2):
        pair = jnp.concatenate(states[2 * index : 2 * index + 2], axis=1)
        small_ref[:, index * pair.shape[1] : (index + 1) * pair.shape[1]] = pair
    small_ref[:, 2 * pair.shape[1] :] = small


def chain(total, step_h, step_w, rate_h, rate_w, read_h, read_w):
    out, tail = [], total
    lane = lane_of(total.shape[0])
    for place, first, step, rate, read in (
        (67, 0, step_h, rate_h, read_h), (68, SIDE, step_w, rate_w, read_w),
    ):
        pace = jnp.exp(column(step[...]))
        decay = pace * rate[...]
        to_read = jnp.zeros_like(decay)
        to_decay = jnp.zeros_like(decay)
        for lag in range(SIDE):
            term = total[:, first + lag : first + lag + 1] * jnp.exp(-decay * lag)
            to_read = to_read + term
            if lag:
                to_decay = to_decay - float(lag) * term
        to_decay = to_decay * read[...]
        out += [to_read, pace * to_decay]
        tail = jnp.where(lane == place, jnp.sum(to_decay * decay, axis=1, keepdims=True), tail)
    return out, tail


def join_kernel(count, *refs):
    given, outs = refs[:count], refs[count:]
    tall = outs[0].shape[0]
    for index, out in enumerate(outs):
        at = slice(index * tall, (index + 1) * tall)
        total = given[0][at].astype(F32)
        for ref in given[1:]:
            total = total + ref[at].astype(F32)
        out[...] = total.astype(out.dtype)


def cut_kernel(one_ref, two_ref, first_ref, second_ref):
    cut = first_ref.shape[0]
    first_ref[...] = one_ref[:cut]
    second_ref[...] = two_ref[cut:]


def start_kernel(one_ref, two_ref, arrived_ref, out_one, out_two):
    cut = one_ref.shape[0]
    at = arrived_ref.shape[0] - 2 * cut
    for start, ref, out in ((at, one_ref, out_one), (at + cut, two_ref, out_two)):
        total = ref[...].astype(F32) + arrived_ref[start : start + cut].astype(F32)
        out[...] = total.astype(BF16)


def relay_kernel(one_ref, two_ref, arrived_ref, first_ref, second_ref, out_one, out_two):
    tall = one_ref.shape[0]
    cut = tall // 2
    one = one_ref[...].astype(F32) + arrived_ref[tall : 2 * tall].astype(F32)
    two = two_ref[...].astype(F32) + arrived_ref[2 * tall : 3 * tall].astype(F32)
    out_one[:cut] = (one[:cut] + first_ref[...].astype(F32)).astype(BF16)
    out_one[cut:] = one[cut:].astype(BF16)
    out_two[:cut] = two[:cut].astype(BF16)
    out_two[cut:] = (two[cut:] + second_ref[...].astype(F32)).astype(BF16)


def finish_kernel(
    half, mine_ref, other_ref, small_ref, sibling_ref,
    gstep_h, grate_h, gread_h, gstep_w, grate_w, gread_w, gskip, ggain, gshift, gin, ginb, gout,
    gbias, gscale,
):
    units, count = gin.shape
    channels, states = grate_h.shape
    keep = units // 2
    deep = deep_of(mine_ref, count)
    first = half[0] == 0
    mine, other = mine_ref[...], other_ref[...]
    bias = []
    for at, part in ((0, jnp.where(first, mine, other)), (keep, jnp.where(first, other, mine))):
        for index in range(2 * count // LANES):
            out = gin if index < count // LANES else gout
            lanes = pl.ds(index * LANES % count, LANES)
            out[at : at + keep, lanes] = part[index * deep : index * deep + keep]
        bias.append(unfold(part[-EDGE:], 0, deep)[:keep])
    ginb[...] = as_row(jnp.concatenate(bias, axis=0))
    norms = mine[-EDGE:] + other[-EDGE:]
    ggain[...] = as_row(unfold(norms, 1, deep)[:channels])
    gshift[...] = as_row(unfold(norms, 2, deep)[:channels])
    total = small_ref[...] + sibling_ref[...]
    for index, ref in enumerate((gread_h, grate_h, gread_w, grate_w)):
        ref[...] = total[:, index * states : (index + 1) * states]
    total = total[:, 4 * states :]
    gskip[...] = as_row(total[:, 64:65])
    gscale[...] = as_row(total[:, 65:66])
    gbias[...] = as_row(total[:, 66:67])
    gstep_h[...] = as_row(total[:, 67:68])
    gstep_w[...] = as_row(total[:, 68:69])


def deep_of(ref, count, shards=1):
    return (ref.shape[0] // shards - EDGE) * LANES // (2 * count)


def fold(columns, deep):
    lane = lane_of(EDGE)
    pieces = deep // EDGE
    tile = jnp.zeros((EDGE, LANES), F32)
    for index, value in enumerate(columns):
        if value is not None:
            for p in range(pieces):
                part = value[p * EDGE : (p + 1) * EDGE]
                tile = jnp.where(lane == index * pieces + p, part, tile)
    return tile


def unfold(tile, index, deep):
    pieces = deep // EDGE
    first = index * pieces
    return jnp.concatenate([tile[:, first + p : first + p + 1] for p in range(pieces)], axis=0)


def pack_kernel(half, in_ref, out_ref, bias_ref, gain_ref, shift_ref, pack_ref):
    own, count = out_ref.shape
    deep = deep_of(pack_ref, count)
    channels = gain_ref.shape[1]
    keep = own // 2
    row = lax.broadcasted_iota(jnp.int32, (deep, own), 0)
    col = lax.broadcasted_iota(jnp.int32, (deep, own), 1)
    pick = jnp.where((col == row + half[0] * keep) & (row < keep), 1.0, 0.0).astype(BF16)
    first = dot(pick, in_ref[...]).astype(BF16)
    second = dot(pick, out_ref[...]).astype(BF16)
    bias = dot(pick, jnp.broadcast_to(bias_ref[...], (LANES, own)), NT)
    row = lax.broadcasted_iota(jnp.int32, (deep, channels), 0)
    col = lax.broadcasted_iota(jnp.int32, (deep, channels), 1)
    pick = jnp.where(col == row, 1.0, 0.0).astype(BF16)
    gain = dot(pick, jnp.broadcast_to(gain_ref[...], (LANES, channels)), NT)
    shift = dot(pick, jnp.broadcast_to(shift_ref[...], (LANES, channels)), NT)
    half_tiles = count // LANES
    for index in range(2 * half_tiles):
        source = first if index < half_tiles else second
        lanes = slice(index % half_tiles * LANES, (index % half_tiles + 1) * LANES)
        pack_ref[index * deep : (index + 1) * deep] = source[:, lanes]
    pack_ref[2 * half_tiles * deep :] = fold((bias, gain, shift), deep).astype(BF16)


ROOT = math.sqrt(2.0 / math.pi)


def shards_of(ref, count, deep):
    height = 2 * count // LANES * deep + EDGE
    return range(0, ref.shape[0], height)


def perceptron(refs, act, down, deep, sums_first):
    count = act.shape[0]
    tiles = count // LANES

    def matrix(first):
        rows = []
        for ref in refs:
            for base in shards_of(ref, count, deep):
                starts = [base + (first + j) * deep for j in range(tiles)]
                rows.append(jnp.concatenate([ref[at : at + deep] for at in starts], axis=1))
        return jnp.concatenate(rows, axis=0)

    bias = []
    for ref in refs:
        for base in shards_of(ref, count, deep):
            at = base + 2 * tiles * deep
            bias.append(unfold(ref[at : at + EDGE].astype(F32), 0, deep))
    w_in, w_out = matrix(0), matrix(tiles)
    v = dot(w_in, act) + jnp.concatenate(bias, axis=0)
    square = v * v
    half = 0.5 * jnp.tanh(v * (ROOT * 0.044715 * square + ROOT)) + 0.5
    full = v * half
    hidden = full.astype(BF16)
    slope = half + full * (1.0 - half) * (6.0 * ROOT * 0.044715 * square + 2.0 * ROOT)
    low = (dot(w_out, down) * slope).astype(BF16)
    g_bias = jnp.sum(low.astype(F32), axis=1, keepdims=True)
    if sums_first:
        sums, total = dot(w_out, hidden, TN), dot(w_in, low, TN)
    grads = (dot(low, act, NT).astype(BF16), dot(hidden, down, NT).astype(BF16), g_bias)
    if not sums_first:
        sums, total = dot(w_out, hidden, TN), dot(w_in, low, TN)
    return sums, total, grads


def put(ref, grads, start, deep, edges=None):
    count = grads[0].shape[1]
    tiles = count // LANES
    for base in shards_of(ref, count, deep):
        for index in range(2 * tiles):
            lanes = slice(index % tiles * LANES, (index % tiles + 1) * LANES)
            at = base + index * deep
            ref[at : at + deep] = grads[index // tiles][start : start + deep, lanes]
        edge = fold((grads[2][start : start + deep],), deep)
        if edges is None:
            at = base + 2 * tiles * deep
            ref[at : at + EDGE] = edge.astype(BF16)
        else:
            at = start // deep * EDGE
            edges[at : at + EDGE] = edge
        start += deep
    return start


def spots_of(near, devices, where_ref):
    z, xy = where_ref[0], where_ref[1]
    for d in range(devices):
        spot = ((d % near) ^ xy) * (devices // near) + ((d // near) ^ z)
        yield d, pl.multiple_of(spot * EDGE, EDGE)


def piece_of(rows, channels):
    return lax.broadcasted_iota(jnp.int32, (rows, LANES), 0) % channels // EDGE


def spread_of(tiles, index, channels, deep):
    piece = piece_of(tiles.shape[0], channels)[:, 0:1]
    first = index * (deep // EDGE)
    out = tiles[:, first : first + 1]
    for p in range(1, -(-channels // EDGE)):
        out = jnp.where(piece == p, tiles[:, first + p : first + p + 1], out)
    return out


def mlp_first(near, pieces, deep, where_ref, given_ref, *refs):
    own_in, refs = refs[:pieces], refs[pieces:]
    other_in, refs = refs[:pieces], refs[pieces:]
    gother_ref, active, downs, normal, inv_ref, gains, sum_ref, grad_ref, ext = refs
    devices, _, channels, _ = given_ref.shape
    count = active.shape[0]

    value = jnp.concatenate([given_ref[d, 0].astype(F32) for d in range(devices)], axis=0)
    mean = jnp.mean(value, axis=0, keepdims=True)
    value = value - mean
    inv = lax.rsqrt(jnp.mean(value * value, axis=0, keepdims=True) + EPS)
    value = value * inv
    normal[...] = value
    inv_ref[...] = inv
    down = jnp.concatenate([given_ref[d, 1].astype(F32) for d in range(devices)], axis=0)
    downs[...] = down.astype(BF16)
    at = 0
    for ref in own_in:
        for base in shards_of(ref, count, deep):
            edge = base + 2 * count // LANES * deep
            ext[at : at + EDGE] = ref[edge : edge + EDGE].astype(F32)
            at += EDGE
    for d, spot in spots_of(near, devices, where_ref):
        tile = ext[pl.ds(spot, EDGE), :]
        for at in range(0, channels, EDGE):
            rows = min(EDGE, channels - at)
            gains[d * channels + at : d * channels + at + rows] = tile[:rows]
    gain, shift = (spread_of(gains[...], index, channels, deep) for index in (1, 2))
    gains[...] = jnp.broadcast_to(gain, gains.shape)
    active[...] = (value * gain + shift).astype(BF16)
    sums, total, grads = perceptron(other_in, active[...], downs[...], deep, False)
    put(gother_ref, grads, 0, deep)
    sum_ref[...] = sums
    grad_ref[...] = total


def mlp_second(
    near, pieces, deep, where_ref, active, downs, normal_ref, inv_ref, gains, sum_ref, grad_ref,
    *refs,
):
    own_in, refs = refs[:pieces], refs[pieces:]
    both_ref, refs = refs[0], refs[1:]
    own_out, (gext,) = refs[:pieces], refs[pieces:]
    count = active.shape[0]
    devices, _, channels, _ = both_ref.shape

    sums, total, grads = perceptron(own_in, active[...], downs[...], deep, True)
    start = 0
    for ref in own_out:
        start = put(ref, grads, start, deep, gext)
    summed = sum_ref[...] + sums
    agrad = grad_ref[...] + total
    norm = normal_ref[...]
    scaled = agrad * gains[:, 0:1]
    first = jnp.mean(scaled, axis=0, keepdims=True)
    second = jnp.mean(scaled * norm, axis=0, keepdims=True)
    mgrad = (scaled - first - norm * second) * inv_ref[...]
    for d in range(devices):
        both_ref[d, 0] = mgrad[d * channels : (d + 1) * channels].astype(BF16)
        both_ref[d, 1] = summed[d * channels : (d + 1) * channels].astype(BF16)
    by_gain = jnp.sum(agrad * norm, axis=1, keepdims=True)
    by_shift = jnp.sum(agrad, axis=1, keepdims=True)
    lane, piece = lane_of(count), piece_of(count, channels)
    base = deep // EDGE
    tile = jnp.where(lane == base + piece, by_gain, 0.0)
    tile = jnp.where(lane == 2 * base + piece, by_shift, tile)
    for d, spot in spots_of(near, devices, where_ref):
        edge = None
        for at in range(0, channels, EDGE):
            rows = min(EDGE, channels - at)
            part = tile[d * channels + at : d * channels + at + rows]
            if rows < EDGE:
                part = jnp.concatenate([part, jnp.zeros((EDGE - rows, LANES), F32)], axis=0)
            edge = part if edge is None else edge + part
        gext[pl.ds(spot, EDGE), :] += edge
    at = 0
    for ref in own_out:
        for base in shards_of(ref, count, deep):
            edge = base + 2 * count // LANES * deep
            ref[edge : edge + EDGE] = gext[at : at + EDGE].astype(BF16)
            at += EDGE


def whole(shape):
    return pl.BlockSpec(shape, lambda i: (0,) * len(shape))


def params(mebibytes):
    return pltpu.CompilerParams(vmem_limit_bytes=mebibytes << 20)


def cost(micros):
    return pl.CostEstimate(flops=0, transcendentals=0, bytes_accessed=micros * 3_000_000)


def join(deep, arrays, count):
    full = pl.BlockSpec(memory_space=pltpu.VMEM)
    width = arrays[0].shape[1]
    return pl.pallas_call(
        partial(join_kernel, len(arrays)),
        out_shape=[
            pltpu.VMEM((deep, width), BF16 if i else F32) for i in range(count)
        ],
        in_specs=[full] * len(arrays),
        out_specs=[full] * count,
        compiler_params=params(16),
        cost_estimate=pl.CostEstimate(flops=1 if count > 1 else 1, transcendentals=0, bytes_accessed=1_000_000),
        name="join",
    )(*arrays)


def relay(*arrays):
    full = pl.BlockSpec(memory_space=pltpu.VMEM)
    shape = pltpu.VMEM(arrays[0].shape, BF16)
    return pl.pallas_call(
        relay_kernel,
        out_shape=(shape, shape),
        in_specs=[full] * 5,
        out_specs=(full, full),
        compiler_params=params(16),
        cost_estimate=pl.CostEstimate(flops=100_000_000_000, transcendentals=0, bytes_accessed=1_000_000),
        name="relay",
    )(*arrays)


SMEM = pl.BlockSpec(memory_space=pltpu.SMEM)


def per_device(
    ch, features, cotangent, heights, widths, step_height, rate_height, readout_height,
    step_width, rate_width, readout_width, skip_gain, norm_gain, norm_shift, in_weight,
    in_bias, out_weight, out_bias, layer_scale,
):
    channels, cells = features.shape
    count = in_weight.shape[0]
    pin = lambda v: pltpu.with_memory_space_constraint(v, pltpu.HBM)
    units = in_weight.shape[1]
    states = rate_height.shape[1]
    images = cells // CELLS
    tokens = cells // ch
    parts = CELLS // tokens
    far = 4
    near = ch // far
    deep = -(-(units // 2) // 16) * 16
    tall_one = 2 * count // LANES * deep + EDGE
    width = LANES
    near_groups = [[f * near + i for i in range(near)] for f in range(far)]
    row = lambda v: v.reshape(1, -1)
    exchange = lambda v: lax.ppermute(v, "img", [(0, 1), (1, 0)])
    flip = lambda v, bits: lax.ppermute(v, "ch", [(i, i ^ bits) for i in range(ch)])
    swap = lambda v, groups=None: lax.all_to_all(
        v, "ch", split_axis=0, concat_axis=0, tiled=True, axis_index_groups=groups
    )
    pair = lambda *arrays: lax.optimization_barrier(arrays)
    half = lax.axis_index("img").astype(jnp.int32)
    place = lax.axis_index("ch").astype(jnp.int32)
    full = pl.BlockSpec(memory_space=pltpu.VMEM)

    pack = pl.pallas_call(
        pack_kernel,
        out_shape=jax.ShapeDtypeStruct((tall_one, width), BF16),
        in_specs=[SMEM] + [full] * 5,
        out_specs=full,
        compiler_params=params(16),
        cost_estimate=cost(2),
        name="pack",
    )(
        half.reshape(1), pin(in_weight.T), pin(out_weight), pin(row(in_bias)), pin(row(norm_gain)),
        pin(row(norm_shift)),
    )
    pack, features_after = pair(pack, features)
    shards = [pack] + [flip(pack, bits * near) for bits in range(1, far)]

    groups = -(-channels // SLOT)
    square = (SLOT * SIDE, images // PER * LANES)
    toeplitz = pltpu.VMEM((SLOT * SIDE, SLOT * SIDE), BF16)
    slots = pltpu.VMEM((groups, images * TILES * SLOT, LANES), F32)
    both_shape = (ch, 2, channels, tokens)
    given, taps = pl.pallas_call(
        forward_kernel,
        out_shape=(
            jax.ShapeDtypeStruct(both_shape, BF16),
            jax.ShapeDtypeStruct((groups * SLOT, LANES), F32),
        ),
        in_specs=[SMEM, SMEM] + [full] * 10,
        out_specs=(full, full),
        scratch_shapes=[
            slots, pltpu.VMEM((groups,) + toeplitz.shape, BF16),
            pltpu.VMEM((groups,) + toeplitz.shape, BF16), pltpu.VMEM((groups,) + square, BF16),
            pltpu.VMEM((groups,) + square, F32),
        ],
        compiler_params=params(16),
        cost_estimate=cost(6),
        name="mixer_forward",
    )(
        pin(heights), pin(widths), pin(features_after), pin(cotangent), pin(row(layer_scale)),
        pin(row(step_height)), pin(row(step_width)), pin(rate_height), pin(rate_width),
        pin(readout_height), pin(readout_width), pin(row(skip_gain)),
    )
    given, *shards = pair(given, *shards)
    given = swap(given)
    shard = jnp.concatenate(shards, axis=0)
    if near == 4:
        cut = far * tall_one // 2
        beside, above = pair(flip(shard, 1), flip(shard, 2))
        ends = pl.pallas_call(
            cut_kernel,
            out_shape=[jax.ShapeDtypeStruct((cut, width), BF16)] * 2,
            in_specs=[full] * 2,
            out_specs=[full] * 2,
            compiler_params=params(16),
            cost_estimate=pl.CostEstimate(flops=100_000_000_000, transcendentals=0, bytes_accessed=1_000_000),
            name="ends",
        )(beside, above)
        own = [shard, beside, above, flip(ends[0], 2), flip(ends[1], 1)]
        where = jnp.stack([place // near, place % near])
    else:
        own = [swap(jnp.broadcast_to(shard[None], (near,) + shard.shape), near_groups)]
        own = [own[0].reshape(ch * tall_one, width)]
        where = jnp.stack([place // near, place * 0])
    other = [exchange(piece) for piece in own]

    rows = ch * tall_one
    pieces = len(own)
    plane = jax.ShapeDtypeStruct((count, tokens), F32)
    token_low = jax.ShapeDtypeStruct((count, tokens), BF16)
    gother, *state = pl.pallas_call(
        partial(mlp_first, near, pieces, deep),
        out_shape=[
            jax.ShapeDtypeStruct((rows, width), BF16), token_low, token_low, plane,
            jax.ShapeDtypeStruct((1, tokens), F32), jax.ShapeDtypeStruct((count, LANES), F32),
            plane, plane,
        ],
        in_specs=[SMEM] + [full] * (1 + 2 * pieces),
        out_specs=[full] * 8,
        scratch_shapes=[pltpu.VMEM((ch * EDGE, LANES), F32)],
        compiler_params=params(16),
        cost_estimate=cost(5),
        name="mlp_first",
    )(where, given, *own, *other)
    arrived = exchange(gother)
    both, *gown = pl.pallas_call(
        partial(mlp_second, near, pieces, deep),
        out_shape=[jax.ShapeDtypeStruct(both_shape, BF16)]
        + [jax.ShapeDtypeStruct(piece.shape, BF16) for piece in own],
        in_specs=[SMEM] + [full] * (7 + pieces),
        out_specs=[full] * (1 + pieces),
        scratch_shapes=[pltpu.VMEM((ch * EDGE, LANES), F32)],
        compiler_params=params(16),
        cost_estimate=cost(5),
        name="mlp_second",
    )(where, *state, *own)
    both = swap(both)
    tall = far * tall_one
    if near == 4:
        cut = tall // 2
        part = pltpu.VMEM(gown[3].shape, BF16)
        one, two = pl.pallas_call(
            start_kernel,
            out_shape=(part, part),
            in_specs=[full] * 3,
            out_specs=(full, full),
            compiler_params=params(16),
            cost_estimate=cost(1),
            name="start",
        )(gown[3], gown[4], arrived)
        one, two = pair(flip(one, 2), flip(two, 1))
        one, two = relay(gown[1], gown[2], arrived, one, two)
        features_last, one, two = pair(features, one, two)
        first, second, *sent = gown[0], arrived, flip(one, 1), flip(two, 2)
    else:
        features_last = features
        total = (gown[0].astype(F32) + arrived.astype(F32)).astype(BF16)
        sent = list(swap(total.reshape(near, tall, width), near_groups))
        first, second, *sent = sent
    landed = [first, second, *sent]
    table = pltpu.HBM((groups,) + toeplitz.shape, BF16)
    strip = pltpu.HBM((groups, SLOT, images * SLOT, LANES), BF16)
    prepared = pl.pallas_call(
        prepare_kernel,
        out_shape=(
            pltpu.HBM((groups,) + square, BF16), table, table, strip, strip,
        ),
        in_specs=[SMEM, SMEM, full, full],
        out_specs=(full,) * 5,
        scratch_shapes=[slots, pltpu.VMEM(square, F32)],
        compiler_params=params(16),
        cost_estimate=cost(4),
        name="mixer_prepare",
    )(pin(heights), pin(widths), pin(features_last), taps)
    *landed, _ = pair(*landed, prepared[0])
    shards = join(tall_one, landed, far)
    shards = [shards[0]] + [flip(v, (i + 1) * near) for i, v in enumerate(shards[1:])]
    result, grad_features, small = pl.pallas_call(
        backward_kernel,
        out_shape=(
            jax.ShapeDtypeStruct((channels, cells), BF16),
            jax.ShapeDtypeStruct((channels, cells), F32),
            jax.ShapeDtypeStruct((channels, LANES + 4 * states), F32),
        ),
        in_specs=[SMEM, SMEM] + [full] * 17,
        out_specs=(full,) * 3,
        scratch_shapes=[
            slots, slots, pltpu.VMEM(square, BF16),
            pltpu.VMEM((SLOT * SIDE, SLOT * SIDE), F32), pltpu.VMEM(square, BF16),
            pltpu.VMEM(square, BF16), pltpu.VMEM(square, F32),
            pltpu.VMEM((groups * SLOT, LANES), F32),
        ],
        compiler_params=params(16),
        cost_estimate=cost(7),
        name="mixer_backward",
    )(
        pin(heights), pin(widths), pin(features), pin(cotangent), both, taps,
        pin(row(layer_scale)), pin(row(out_bias)), pin(row(step_height)), pin(row(step_width)),
        pin(rate_height), pin(rate_width), pin(readout_height), pin(readout_width),
        *map(pin, prepared),
    )
    *shards, small = pair(*shards, small)
    (mine,) = join(tall_one, shards, 1)
    vector_out = jax.ShapeDtypeStruct((1, channels), F32)
    state_out = jax.ShapeDtypeStruct((channels, states), F32)
    weight_out = jax.ShapeDtypeStruct((units, count), F32)
    outs = pl.pallas_call(
        finish_kernel,
        out_shape=(
            vector_out, state_out, state_out, vector_out, state_out, state_out, vector_out,
            vector_out, vector_out, weight_out, jax.ShapeDtypeStruct((1, units), F32), weight_out,
            vector_out, vector_out,
        ),
        in_specs=[SMEM] + [full] * 4,
        out_specs=(full,) * 14,
        compiler_params=params(16),
        cost_estimate=cost(1),
        name="finish",
    )(half.reshape(1), mine, exchange(mine), small, exchange(small))
    outs = [v.reshape(-1) if v.shape[0] == 1 else v for v in outs]
    outs[9] = outs[9].T
    return (result, grad_features, *outs)


def solution(mesh):
    wide, split, tall = P("ch", "img"), P("ch"), P("ch", None)
    return jax.shard_map(
        partial(per_device, mesh.shape["ch"]),
        mesh=mesh,
        in_specs=(
            wide, wide, P("img"), P("img"), split, tall, tall, split, tall, tall, split, split,
            split, P(None, "ch"), split, tall, split, split,
        ),
        out_specs=(
            wide, wide, split, tall, tall, split, tall, tall, split, split, split,
            P(None, "ch"), split, tall, split, split,
        ),
        check_vma=False,
    )
```

```python
import math
from functools import partial

import jax
import jax.numpy as jnp
from jax import lax
from jax.experimental import pallas as pl
from jax.experimental.pallas import tpu as pltpu
from jax.sharding import PartitionSpec as P

SIDE = 32
CELLS = SIDE * SIDE
LANES = 128
PER = LANES // SIDE
SLOT = 8
EDGE = 16
TILES = CELLS // LANES
EPS = 1e-06
F32 = jnp.float32
BF16 = jnp.bfloat16


def column(row):
    n = row.shape[1]
    eye = lax.broadcasted_iota(jnp.int32, (n, n), 0) == lax.broadcasted_iota(jnp.int32, (n, n), 1)
    return jnp.sum(jnp.where(eye, jnp.broadcast_to(row, (n, n)), 0.0), axis=1, keepdims=True)


def as_row(col):
    n = col.shape[0]
    eye = lax.broadcasted_iota(jnp.int32, (n, n), 0) == lax.broadcasted_iota(jnp.int32, (n, n), 1)
    return jnp.sum(jnp.where(eye, jnp.broadcast_to(col, (n, n)), 0.0), axis=0, keepdims=True)


def image_mask(rows, height, width):
    cell = lax.broadcasted_iota(jnp.int32, (SLOT, CELLS), 1)
    inside = jnp.where((cell // SIDE < height) & (cell % SIDE < width), 1.0, 0.0)
    return jnp.concatenate([inside] * -(-rows // SLOT), axis=0)[:rows]


def lane_of(rows):
    return lax.broadcasted_iota(jnp.int32, (rows, LANES), 1)


def fill_slots(slots, value, image):
    channels = value.shape[0]
    for group in range(slots.shape[0]):
        live = min(SLOT, channels - group * SLOT)
        for k in range(TILES):
            at = (image * TILES + k) * SLOT
            part = value[group * SLOT : group * SLOT + live, k * LANES : (k + 1) * LANES]
            slots[group, pl.ds(at, live), :] = part


def read_slots(slots, image, channels):
    rows = []
    for group in range(slots.shape[0]):
        live = min(SLOT, channels - group * SLOT)
        at = [(image * TILES + k) * SLOT for k in range(TILES)]
        rows.append(jnp.concatenate([slots[group, pl.ds(a, live), :] for a in at], axis=1))
    return jnp.concatenate(rows, axis=0) if len(rows) > 1 else rows[0]


def cross(tiles, lane):
    for bit, far in ((2, 64), (1, 32)):
        low = (lane & far) == 0
        out = list(tiles)
        for k in range(len(tiles)):
            if not k & bit:
                one, two = tiles[k], tiles[k | bit]
                out[k] = jnp.where(low, one, pltpu.roll(two, far, 1))
                out[k | bit] = jnp.where(low, pltpu.roll(one, LANES - far, 1), two)
        tiles = out
    return tiles


def load_channel(slots, group, c, lane):
    count = slots.shape[1] // SLOT
    value = slots[group, pl.ds(c, count, stride=SLOT), :]
    return cross([value[k * SLOT : (k + 1) * SLOT] for k in range(count // SLOT)], lane)


def store_channel(slots, group, c, tiles, lane):
    count = slots.shape[1] // SLOT
    slots[group, pl.ds(c, count, stride=SLOT), :] = jnp.concatenate(cross(tiles, lane), axis=0)


def split(value):
    high = value.astype(BF16)
    return high, (value - high.astype(F32)).astype(BF16)


def pick(row, index):
    spread = jnp.broadcast_to(row, index.shape)
    value = jnp.take_along_axis(spread, jnp.clip(index, 0, LANES - 1), axis=1)
    return value


def build_down(row, c, high_ref, low_ref, lane, sub):
    place = lane % SIDE
    source = (place % TILES) * PER + place // TILES
    here = lane // SIDE == c % PER
    parts = []
    for turn in range(PER):
        index = PER * sub + turn - source
        parts.append(jnp.where(here & (index >= 0), pick(row, index), 0.0))
    high, low = split(jnp.concatenate(parts, axis=0))
    at = (slice(c * SIDE, (c + 1) * SIDE), slice(c // PER * LANES, (c // PER + 1) * LANES))
    high_ref[at] = high
    low_ref[at] = low


def build_across(row, turned, lane, sub):
    place = lane % SIDE
    highs, lows = [], []
    for part in range(PER):
        own = part * SLOT + sub
        index = own - place if turned else place - own
        value = jnp.where(index >= 0, pick(row, index + SIDE), 0.0)
        high = value.astype(BF16).astype(F32)
        highs.append(high)
        lows.append(value - high)
    spread = lambda parts: jnp.concatenate(
        [jnp.where(lane // SIDE == i, p, 0.0) for i in range(PER) for p in parts], axis=0
    ).astype(BF16)
    return spread(highs), spread(lows)


def taps_of(step_h, step_w, rate_h, rate_w, read_h, read_w, skip_ref):
    channels = rate_h.shape[0]
    lane = lane_of(channels)
    kept = jnp.zeros((channels, LANES), F32)
    decay_h = jnp.exp(column(step_h[...])) * rate_h[...]
    decay_w = jnp.exp(column(step_w[...])) * rate_w[...]
    for lag in range(SIDE):
        tap = jnp.sum(read_h[...] * jnp.exp(-decay_h * lag), axis=1, keepdims=True)
        kept = jnp.where(lane == lag, tap, kept)
        tap = jnp.sum(read_w[...] * jnp.exp(-decay_w * lag), axis=1, keepdims=True)
        kept = jnp.where(lane == SIDE + lag, tap, kept)
    return jnp.where(lane == 2 * SIDE, column(skip_ref[...]), kept)


def dot(a, b, dims=(((1,), (0,)), ((), ()))):
    return lax.dot_general(a, b, dims, preferred_element_type=F32)


NT = (((1,), (1,)), ((), ()))
TN = (((0,), (0,)), ((), ()))


def forward_kernel(
    heights, widths, feat_ref, cot_ref, scale_ref, step_h, step_w, rate_h, rate_w, read_h,
    read_w, skip_ref, out_ref, rows_ref, slots, high_a, low_a, field, tall,
):
    channels, cells = feat_ref.shape
    images = cells // CELLS
    rows_ref[0:channels] = taps_of(step_h, step_w, rate_h, rate_w, read_h, read_w, skip_ref)
    for ref in (high_a, low_a, field):
        ref[...] = jnp.zeros_like(ref)
    for image in range(images):
        inside = image_mask(channels, heights[image], widths[image])
        value = feat_ref[:, image * CELLS : (image + 1) * CELLS].astype(F32)
        fill_slots(slots, value * inside, image)
    live = min(SLOT, channels)
    sides = images // PER

    scratch = (high_a, low_a, field, tall)

    def body(group, carry):
        high_a, low_a, field, tall = (ref.at[group] for ref in scratch)
        lane = lane_of(SLOT)
        sub = lax.broadcasted_iota(jnp.int32, (SLOT, LANES), 0)
        for c in range(live):
            row = rows_ref[pl.ds(group * SLOT + c, 1), :]
            build_down(row, c, high_a, low_a, lane, sub)
            tiles = load_channel(slots, group, c, lane)
            for s in range(sides):
                value = jnp.concatenate(tiles[s * PER : (s + 1) * PER], axis=0)
                field[c * SIDE : (c + 1) * SIDE, s * LANES : (s + 1) * LANES] = value.astype(BF16)
        source = field[...]
        tall[...] = dot(high_a[...], source) + dot(low_a[...], source)
        for c in range(live):
            row = rows_ref[pl.ds(group * SLOT + c, 1), :]
            high_b, low_b = build_across(row, False, lane, sub)
            value = jnp.concatenate(
                [tall[c * SIDE : (c + 1) * SIDE, s * LANES : (s + 1) * LANES] for s in range(sides)],
                axis=0,
            )
            high, low = split(value)
            value = dot(
                jnp.concatenate([high, low, high], axis=1),
                jnp.concatenate([high_b, high_b, low_b], axis=0),
            )
            tiles = [value[k * SLOT : (k + 1) * SLOT] for k in range(images)]
            store_channel(slots, group, c, tiles, lane)
        return carry

    for group in range(slots.shape[0]):
        body(group, 0)
    wide = out_ref.shape[3]
    parts = CELLS // wide
    skip = rows_ref[0:channels, 2 * SIDE : 2 * SIDE + 1]
    scale = column(scale_ref[...])
    for image in range(images):
        span = slice(image * CELLS, (image + 1) * CELLS)
        inside = image_mask(channels, heights[image], widths[image])
        value = read_slots(slots, image, channels) + skip * feat_ref[:, span].astype(F32)
        value = (value * inside).astype(BF16)
        down = cot_ref[:, span].astype(F32) * scale
        down = (down * inside).astype(BF16)
        for j in range(parts):
            out_ref[image * parts + j, 0] = value[:, j * wide : (j + 1) * wide]
            out_ref[image * parts + j, 1] = down[:, j * wide : (j + 1) * wide]


def prepare_kernel(
    heights, widths, feat_ref, rows_ref, field_ref, high_a, low_a, high_s, low_s, slots, tall
):
    channels, cells = feat_ref.shape
    images = cells // CELLS
    live = min(SLOT, channels)
    sides = images // PER
    for ref in (field_ref, high_a, low_a):
        ref[...] = jnp.zeros_like(ref)
    for image in range(images):
        inside = image_mask(channels, heights[image], widths[image])
        value = feat_ref[:, image * CELLS : (image + 1) * CELLS].astype(F32)
        fill_slots(slots, value * inside, image)

    def body(group, carry):
        lane = lane_of(SLOT)
        sub = lax.broadcasted_iota(jnp.int32, (SLOT, LANES), 0)
        for c in range(live):
            row = rows_ref[pl.ds(group * SLOT + c, 1), :]
            build_down(row, c, high_a.at[group], low_a.at[group], lane, sub)
            tiles = load_channel(slots, group, c, lane)
            for s in range(sides):
                value = jnp.concatenate(tiles[s * PER : (s + 1) * PER], axis=0)
                at = (group, slice(c * SIDE, (c + 1) * SIDE), slice(s * LANES, (s + 1) * LANES))
                field_ref[at] = value.astype(BF16)
        source = field_ref[group]
        tall[...] = dot(high_a[group], source) + dot(low_a[group], source)
        for c in range(live):
            value = jnp.concatenate(
                [tall[c * SIDE : (c + 1) * SIDE, s * LANES : (s + 1) * LANES] for s in range(sides)],
                axis=0,
            )
            high, low = split(value)
            high_s[group, c] = high
            low_s[group, c] = low
        return carry

    lax.fori_loop(0, slots.shape[0], body, 0)


def backward_kernel(
    heights, widths, feat_ref, cot_ref, both_ref, rows_ref, scale_ref, bias_ref,
    step_h, step_w, rate_h, rate_w, read_h, read_w, field_ref, high_a, low_a, high_s, low_s,
    result_ref, gfeat_ref, small_ref, slots, slots_g, field_g, outer_ref, high_d, low_d, wide_ref, sums,
):
    channels, cells = feat_ref.shape
    images = cells // CELLS
    live = min(SLOT, channels)
    sides = images // PER
    wide = both_ref.shape[3]
    parts = CELLS // wide
    for ref in (sums, field_g, high_d, low_d):
        ref[...] = jnp.zeros_like(ref)
    lane_c = lane_of(channels)
    scale = column(scale_ref[...])
    bias = column(bias_ref[...])
    small = jnp.zeros((channels, LANES), F32)
    for image in range(images):
        span = slice(image * CELLS, (image + 1) * CELLS)
        inside = image_mask(channels, heights[image], widths[image])
        values = feat_ref[:, span].astype(F32)
        grad = jnp.concatenate(
            [both_ref[image * parts + j, 0].astype(F32) for j in range(parts)], axis=1
        )
        grad = grad * inside
        fill_slots(slots_g, grad, image)
        shifted = jnp.concatenate(
            [both_ref[image * parts + j, 1].astype(F32) for j in range(parts)], axis=1
        )
        shifted = shifted + bias
        result = values + inside * (scale * shifted)
        result_ref[:, span] = result.astype(BF16)
        weighted = cot_ref[:, span].astype(F32) * inside
        small = small + jnp.where(
            lane_c == 64,
            jnp.sum(grad * values, axis=1, keepdims=True),
            jnp.where(
                lane_c == 65,
                jnp.sum(weighted * shifted, axis=1, keepdims=True),
                jnp.where(lane_c == 66, scale * jnp.sum(weighted, axis=1, keepdims=True), 0.0),
            ),
        )

    def body(group, carry):
        lane = lane_of(SLOT)
        sub = lax.broadcasted_iota(jnp.int32, (SLOT, LANES), 0)
        place = lane % SIDE
        half = lambda ref, c, s: ref[c * SIDE : (c + 1) * SIDE, s * LANES : (s + 1) * LANES]
        stack = lambda ref, c: jnp.concatenate([half(ref, c, s) for s in range(sides)], axis=0)
        for c in range(live):
            tiles = load_channel(slots_g, group, c, lane)
            for s in range(sides):
                value = jnp.concatenate(tiles[s * PER : (s + 1) * PER], axis=0)
                at = (slice(c * SIDE, (c + 1) * SIDE), slice(s * LANES, (s + 1) * LANES))
                field_g[at] = value.astype(BF16)
        for c in range(live):
            row = rows_ref[pl.ds(group * SLOT + c, 1), :]
            high_b, low_b = build_across(row, True, lane, sub)
            grad = stack(field_g, c)
            flow = dot(
                jnp.concatenate([grad, grad], axis=1), jnp.concatenate([high_b, low_b], axis=0)
            )
            high, low = split(flow)
            for s in range(sides):
                at = (slice(c * SIDE, (c + 1) * SIDE), slice(s * LANES, (s + 1) * LANES))
                high_d[at] = high[s * SIDE : (s + 1) * SIDE]
                low_d[at] = low[s * SIDE : (s + 1) * SIDE]
            outer = dot(
                jnp.concatenate([grad, grad], axis=0),
                jnp.concatenate([high_s[group, c], low_s[group, c]], axis=0),
                TN,
            )
            total = None
            for part in range(PER):
                value = None
                for i in range(PER):
                    at = i * SIDE + part * SLOT
                    term = jnp.where(lane // SIDE == i, outer[at : at + SLOT], 0.0)
                    value = term if value is None else value + term
                index = part * SLOT + sub - place
                value = jnp.take_along_axis(
                    value, jnp.clip(index, 0, SIDE - 1) + lane // SIDE * SIDE, axis=1
                )
                value = jnp.where(index >= 0, value, 0.0)
                total = value if total is None else total + value
            total = jnp.sum(total, axis=0, keepdims=True)
            total = total + pltpu.roll(total, 64, 1)
            total = total + pltpu.roll(total, 32, 1)
            sums[pl.ds(group * SLOT + c, 1), :] = jnp.where(lane[0:1] // SIDE == 1, total, 0.0)
        high, low = high_d[...], low_d[...]
        down = high_a[group]
        back = dot(down, high, TN) + dot(down, low, TN) + dot(low_a[group], high, TN)
        wide_ref[...] = back
        source = field_ref[group]
        outer_ref[...] = dot(high, source, NT) + dot(low, source, NT)
        for c in range(live):
            value = stack(wide_ref, c)
            tiles = [value[k * SLOT : (k + 1) * SLOT] for k in range(images)]
            store_channel(slots, group, c, tiles, lane)
            total = None
            for turn in range(PER):
                at = c * SIDE + turn * SLOT
                value = outer_ref[at : at + SLOT, c // PER * LANES : (c // PER + 1) * LANES]
                index = PER * sub + turn - lane
                safe = jnp.clip(index, 0, SIDE - 1)
                index_at = (safe % PER) * TILES + safe // PER + c % PER * SIDE
                value = jnp.take_along_axis(value, index_at, axis=1)
                value = jnp.where(index >= 0, value, 0.0)
                total = value if total is None else total + value
            total = jnp.sum(total, axis=0, keepdims=True)
            total = jnp.where(lane[0:1] < SIDE, total, 0.0)
            sums[pl.ds(group * SLOT + c, 1), :] += total
        return carry

    lax.fori_loop(0, slots.shape[0], body, 0)
    skip = rows_ref[0:channels, 2 * SIDE : 2 * SIDE + 1]
    for image in range(images):
        span = slice(image * CELLS, (image + 1) * CELLS)
        inside = image_mask(channels, heights[image], widths[image])
        grad = read_slots(slots_g, image, channels)
        value = read_slots(slots, image, channels) + skip * grad
        gfeat_ref[:, span] = cot_ref[:, span].astype(F32) + value * inside
    small = small + sums[0:channels]
    states, small = chain(small, step_h, step_w, rate_h, rate_w, read_h, read_w)
    for index in range(2):
        pair = jnp.concatenate(states[2 * index : 2 * index + 2], axis=1)
        small_ref[:, index * pair.shape[1] : (index + 1) * pair.shape[1]] = pair
    small_ref[:, 2 * pair.shape[1] :] = small


def chain(total, step_h, step_w, rate_h, rate_w, read_h, read_w):
    out, tail = [], total
    lane = lane_of(total.shape[0])
    for place, first, step, rate, read in (
        (67, 0, step_h, rate_h, read_h), (68, SIDE, step_w, rate_w, read_w),
    ):
        pace = jnp.exp(column(step[...]))
        decay = pace * rate[...]
        to_read = jnp.zeros_like(decay)
        to_decay = jnp.zeros_like(decay)
        for lag in range(SIDE):
            term = total[:, first + lag : first + lag + 1] * jnp.exp(-decay * lag)
            to_read = to_read + term
            if lag:
                to_decay = to_decay - float(lag) * term
        to_decay = to_decay * read[...]
        out += [to_read, pace * to_decay]
        tail = jnp.where(lane == place, jnp.sum(to_decay * decay, axis=1, keepdims=True), tail)
    return out, tail


def join_kernel(count, *refs):
    given, outs = refs[:count], refs[count:]
    tall = outs[0].shape[0]
    for index, out in enumerate(outs):
        at = slice(index * tall, (index + 1) * tall)
        total = given[0][at].astype(F32)
        for ref in given[1:]:
            total = total + ref[at].astype(F32)
        out[...] = total.astype(out.dtype)


def cut_kernel(one_ref, two_ref, first_ref, second_ref):
    cut = first_ref.shape[0]
    first_ref[...] = one_ref[:cut]
    second_ref[...] = two_ref[cut:]


def start_kernel(one_ref, two_ref, arrived_ref, out_one, out_two):
    cut = one_ref.shape[0]
    at = arrived_ref.shape[0] - 2 * cut
    for start, ref, out in ((at, one_ref, out_one), (at + cut, two_ref, out_two)):
        total = ref[...].astype(F32) + arrived_ref[start : start + cut].astype(F32)
        out[...] = total.astype(BF16)


def relay_kernel(one_ref, two_ref, arrived_ref, first_ref, second_ref, out_one, out_two):
    tall = one_ref.shape[0]
    cut = tall // 2
    one = one_ref[...].astype(F32) + arrived_ref[tall : 2 * tall].astype(F32)
    two = two_ref[...].astype(F32) + arrived_ref[2 * tall : 3 * tall].astype(F32)
    out_one[:cut] = (one[:cut] + first_ref[...].astype(F32)).astype(BF16)
    out_one[cut:] = one[cut:].astype(BF16)
    out_two[:cut] = two[:cut].astype(BF16)
    out_two[cut:] = (two[cut:] + second_ref[...].astype(F32)).astype(BF16)


def finish_kernel(
    half, mine_ref, other_ref, small_ref, sibling_ref,
    gstep_h, grate_h, gread_h, gstep_w, grate_w, gread_w, gskip, ggain, gshift, gin, ginb, gout,
    gbias, gscale,
):
    units, count = gin.shape
    channels, states = grate_h.shape
    keep = units // 2
    deep = deep_of(mine_ref, count)
    first = half[0] == 0
    mine, other = mine_ref[...], other_ref[...]
    bias = []
    for at, part in ((0, jnp.where(first, mine, other)), (keep, jnp.where(first, other, mine))):
        for index in range(2 * count // LANES):
            out = gin if index < count // LANES else gout
            lanes = pl.ds(index * LANES % count, LANES)
            out[at : at + keep, lanes] = part[index * deep : index * deep + keep]
        bias.append(unfold(part[-EDGE:], 0, deep)[:keep])
    ginb[...] = as_row(jnp.concatenate(bias, axis=0))
    norms = mine[-EDGE:] + other[-EDGE:]
    ggain[...] = as_row(unfold(norms, 1, deep)[:channels])
    gshift[...] = as_row(unfold(norms, 2, deep)[:channels])
    total = small_ref[...] + sibling_ref[...]
    for index, ref in enumerate((gread_h, grate_h, gread_w, grate_w)):
        ref[...] = total[:, index * states : (index + 1) * states]
    total = total[:, 4 * states :]
    gskip[...] = as_row(total[:, 64:65])
    gscale[...] = as_row(total[:, 65:66])
    gbias[...] = as_row(total[:, 66:67])
    gstep_h[...] = as_row(total[:, 67:68])
    gstep_w[...] = as_row(total[:, 68:69])


def deep_of(ref, count, shards=1):
    return (ref.shape[0] // shards - EDGE) * LANES // (2 * count)


def fold(columns, deep):
    lane = lane_of(EDGE)
    pieces = deep // EDGE
    tile = jnp.zeros((EDGE, LANES), F32)
    for index, value in enumerate(columns):
        if value is not None:
            for p in range(pieces):
                part = value[p * EDGE : (p + 1) * EDGE]
                tile = jnp.where(lane == index * pieces + p, part, tile)
    return tile


def unfold(tile, index, deep):
    pieces = deep // EDGE
    first = index * pieces
    return jnp.concatenate([tile[:, first + p : first + p + 1] for p in range(pieces)], axis=0)


def pack_kernel(half, in_ref, out_ref, bias_ref, gain_ref, shift_ref, pack_ref):
    own, count = out_ref.shape
    deep = deep_of(pack_ref, count)
    channels = gain_ref.shape[1]
    keep = own // 2
    row = lax.broadcasted_iota(jnp.int32, (deep, own), 0)
    col = lax.broadcasted_iota(jnp.int32, (deep, own), 1)
    pick = jnp.where((col == row + half[0] * keep) & (row < keep), 1.0, 0.0).astype(BF16)
    first = dot(pick, in_ref[...]).astype(BF16)
    second = dot(pick, out_ref[...]).astype(BF16)
    bias = dot(pick, jnp.broadcast_to(bias_ref[...], (LANES, own)), NT)
    row = lax.broadcasted_iota(jnp.int32, (deep, channels), 0)
    col = lax.broadcasted_iota(jnp.int32, (deep, channels), 1)
    pick = jnp.where(col == row, 1.0, 0.0).astype(BF16)
    gain = dot(pick, jnp.broadcast_to(gain_ref[...], (LANES, channels)), NT)
    shift = dot(pick, jnp.broadcast_to(shift_ref[...], (LANES, channels)), NT)
    half_tiles = count // LANES
    for index in range(2 * half_tiles):
        source = first if index < half_tiles else second
        lanes = slice(index % half_tiles * LANES, (index % half_tiles + 1) * LANES)
        pack_ref[index * deep : (index + 1) * deep] = source[:, lanes]
    pack_ref[2 * half_tiles * deep :] = fold((bias, gain, shift), deep).astype(BF16)


ROOT = math.sqrt(2.0 / math.pi)


def shards_of(ref, count, deep):
    height = 2 * count // LANES * deep + EDGE
    return range(0, ref.shape[0], height)


def perceptron(refs, act, down, deep, sums_first):
    count = act.shape[0]
    tiles = count // LANES

    def matrix(first):
        rows = []
        for ref in refs:
            for base in shards_of(ref, count, deep):
                starts = [base + (first + j) * deep for j in range(tiles)]
                rows.append(jnp.concatenate([ref[at : at + deep] for at in starts], axis=1))
        return jnp.concatenate(rows, axis=0)

    bias = []
    for ref in refs:
        for base in shards_of(ref, count, deep):
            at = base + 2 * tiles * deep
            bias.append(unfold(ref[at : at + EDGE].astype(F32), 0, deep))
    w_in, w_out = matrix(0), matrix(tiles)
    v = dot(w_in, act) + jnp.concatenate(bias, axis=0)
    square = v * v
    half = 0.5 * jnp.tanh(v * (ROOT * 0.044715 * square + ROOT)) + 0.5
    full = v * half
    hidden = full.astype(BF16)
    slope = half + full * (1.0 - half) * (6.0 * ROOT * 0.044715 * square + 2.0 * ROOT)
    low = (dot(w_out, down) * slope).astype(BF16)
    g_bias = jnp.sum(low.astype(F32), axis=1, keepdims=True)
    if sums_first:
        sums, total = dot(w_out, hidden, TN), dot(w_in, low, TN)
    grads = (dot(low, act, NT).astype(BF16), dot(hidden, down, NT).astype(BF16), g_bias)
    if not sums_first:
        sums, total = dot(w_out, hidden, TN), dot(w_in, low, TN)
    return sums, total, grads


def put(ref, grads, start, deep, edges=None):
    count = grads[0].shape[1]
    tiles = count // LANES
    for base in shards_of(ref, count, deep):
        for index in range(2 * tiles):
            lanes = slice(index % tiles * LANES, (index % tiles + 1) * LANES)
            at = base + index * deep
            ref[at : at + deep] = grads[index // tiles][start : start + deep, lanes]
        edge = fold((grads[2][start : start + deep],), deep)
        if edges is None:
            at = base + 2 * tiles * deep
            ref[at : at + EDGE] = edge.astype(BF16)
        else:
            at = start // deep * EDGE
            edges[at : at + EDGE] = edge
        start += deep
    return start


def spots_of(near, devices, where_ref):
    z, xy = where_ref[0], where_ref[1]
    for d in range(devices):
        spot = ((d % near) ^ xy) * (devices // near) + ((d // near) ^ z)
        yield d, pl.multiple_of(spot * EDGE, EDGE)


def piece_of(rows, channels):
    return lax.broadcasted_iota(jnp.int32, (rows, LANES), 0) % channels // EDGE


def spread_of(tiles, index, channels, deep):
    piece = piece_of(tiles.shape[0], channels)[:, 0:1]
    first = index * (deep // EDGE)
    out = tiles[:, first : first + 1]
    for p in range(1, -(-channels // EDGE)):
        out = jnp.where(piece == p, tiles[:, first + p : first + p + 1], out)
    return out


def mlp_first(near, pieces, deep, where_ref, given_ref, *refs):
    own_in, refs = refs[:pieces], refs[pieces:]
    other_in, refs = refs[:pieces], refs[pieces:]
    gother_ref, active, downs, normal, inv_ref, gains, sum_ref, grad_ref, ext = refs
    devices, _, channels, _ = given_ref.shape
    count = active.shape[0]

    value = jnp.concatenate([given_ref[d, 0].astype(F32) for d in range(devices)], axis=0)
    mean = jnp.mean(value, axis=0, keepdims=True)
    value = value - mean
    inv = lax.rsqrt(jnp.mean(value * value, axis=0, keepdims=True) + EPS)
    value = value * inv
    normal[...] = value
    inv_ref[...] = inv
    down = jnp.concatenate([given_ref[d, 1].astype(F32) for d in range(devices)], axis=0)
    downs[...] = down.astype(BF16)
    at = 0
    for ref in own_in:
        for base in shards_of(ref, count, deep):
            edge = base + 2 * count // LANES * deep
            ext[at : at + EDGE] = ref[edge : edge + EDGE].astype(F32)
            at += EDGE
    for d, spot in spots_of(near, devices, where_ref):
        tile = ext[pl.ds(spot, EDGE), :]
        for at in range(0, channels, EDGE):
            rows = min(EDGE, channels - at)
            gains[d * channels + at : d * channels + at + rows] = tile[:rows]
    gain, shift = (spread_of(gains[...], index, channels, deep) for index in (1, 2))
    gains[...] = jnp.broadcast_to(gain, gains.shape)
    active[...] = (value * gain + shift).astype(BF16)
    sums, total, grads = perceptron(other_in, active[...], downs[...], deep, False)
    put(gother_ref, grads, 0, deep)
    sum_ref[...] = sums
    grad_ref[...] = total


def mlp_second(
    near, pieces, deep, where_ref, active, downs, normal_ref, inv_ref, gains, sum_ref, grad_ref,
    *refs,
):
    own_in, refs = refs[:pieces], refs[pieces:]
    both_ref, refs = refs[0], refs[1:]
    own_out, (gext,) = refs[:pieces], refs[pieces:]
    count = active.shape[0]
    devices, _, channels, _ = both_ref.shape

    sums, total, grads = perceptron(own_in, active[...], downs[...], deep, True)
    start = 0
    for ref in own_out:
        start = put(ref, grads, start, deep, gext)
    summed = sum_ref[...] + sums
    agrad = grad_ref[...] + total
    norm = normal_ref[...]
    scaled = agrad * gains[:, 0:1]
    first = jnp.mean(scaled, axis=0, keepdims=True)
    second = jnp.mean(scaled * norm, axis=0, keepdims=True)
    mgrad = (scaled - first - norm * second) * inv_ref[...]
    for d in range(devices):
        both_ref[d, 0] = mgrad[d * channels : (d + 1) * channels].astype(BF16)
        both_ref[d, 1] = summed[d * channels : (d + 1) * channels].astype(BF16)
    by_gain = jnp.sum(agrad * norm, axis=1, keepdims=True)
    by_shift = jnp.sum(agrad, axis=1, keepdims=True)
    lane, piece = lane_of(count), piece_of(count, channels)
    base = deep // EDGE
    tile = jnp.where(lane == base + piece, by_gain, 0.0)
    tile = jnp.where(lane == 2 * base + piece, by_shift, tile)
    for d, spot in spots_of(near, devices, where_ref):
        edge = None
        for at in range(0, channels, EDGE):
            rows = min(EDGE, channels - at)
            part = tile[d * channels + at : d * channels + at + rows]
            if rows < EDGE:
                part = jnp.concatenate([part, jnp.zeros((EDGE - rows, LANES), F32)], axis=0)
            edge = part if edge is None else edge + part
        gext[pl.ds(spot, EDGE), :] += edge
    at = 0
    for ref in own_out:
        for base in shards_of(ref, count, deep):
            edge = base + 2 * count // LANES * deep
            ref[edge : edge + EDGE] = gext[at : at + EDGE].astype(BF16)
            at += EDGE


def whole(shape):
    return pl.BlockSpec(shape, lambda i: (0,) * len(shape))


def params(mebibytes):
    return pltpu.CompilerParams(vmem_limit_bytes=mebibytes << 20)


def cost(micros):
    return pl.CostEstimate(flops=0, transcendentals=0, bytes_accessed=micros * 3_000_000)


def join(deep, arrays, count):
    full = pl.BlockSpec(memory_space=pltpu.VMEM)
    width = arrays[0].shape[1]
    return pl.pallas_call(
        partial(join_kernel, len(arrays)),
        out_shape=[
            pltpu.VMEM((deep, width), BF16 if i else F32) for i in range(count)
        ],
        in_specs=[full] * len(arrays),
        out_specs=[full] * count,
        compiler_params=params(16),
        cost_estimate=pl.CostEstimate(flops=1 if count > 1 else 1, transcendentals=0, bytes_accessed=1_000_000),
        name="join",
    )(*arrays)


def relay(*arrays):
    full = pl.BlockSpec(memory_space=pltpu.VMEM)
    shape = pltpu.VMEM(arrays[0].shape, BF16)
    return pl.pallas_call(
        relay_kernel,
        out_shape=(shape, shape),
        in_specs=[full] * 5,
        out_specs=(full, full),
        compiler_params=params(16),
        cost_estimate=pl.CostEstimate(flops=100_000_000_000, transcendentals=0, bytes_accessed=1_000_000),
        name="relay",
    )(*arrays)


SMEM = pl.BlockSpec(memory_space=pltpu.SMEM)


def per_device(
    ch, features, cotangent, heights, widths, step_height, rate_height, readout_height,
    step_width, rate_width, readout_width, skip_gain, norm_gain, norm_shift, in_weight,
    in_bias, out_weight, out_bias, layer_scale,
):
    channels, cells = features.shape
    count = in_weight.shape[0]
    pin = lambda v: pltpu.with_memory_space_constraint(v, pltpu.HBM)
    units = in_weight.shape[1]
    states = rate_height.shape[1]
    images = cells // CELLS
    tokens = cells // ch
    parts = CELLS // tokens
    far = 4
    near = ch // far
    deep = -(-(units // 2) // 16) * 16
    tall_one = 2 * count // LANES * deep + EDGE
    width = LANES
    near_groups = [[f * near + i for i in range(near)] for f in range(far)]
    row = lambda v: v.reshape(1, -1)
    exchange = lambda v: lax.ppermute(v, "img", [(0, 1), (1, 0)])
    flip = lambda v, bits: lax.ppermute(v, "ch", [(i, i ^ bits) for i in range(ch)])
    swap = lambda v, groups=None: lax.all_to_all(
        v, "ch", split_axis=0, concat_axis=0, tiled=True, axis_index_groups=groups
    )
    pair = lambda *arrays: lax.optimization_barrier(arrays)
    half = lax.axis_index("img").astype(jnp.int32)
    place = lax.axis_index("ch").astype(jnp.int32)
    full = pl.BlockSpec(memory_space=pltpu.VMEM)

    pack = pl.pallas_call(
        pack_kernel,
        out_shape=jax.ShapeDtypeStruct((tall_one, width), BF16),
        in_specs=[SMEM] + [full] * 5,
        out_specs=full,
        compiler_params=params(16),
        cost_estimate=cost(2),
        name="pack",
    )(
        half.reshape(1), pin(in_weight.T), pin(out_weight), pin(row(in_bias)), pin(row(norm_gain)),
        pin(row(norm_shift)),
    )
    pack, features_after = pair(pack, features)
    shards = [pack] + [flip(pack, bits * near) for bits in range(1, far)]

    groups = -(-channels // SLOT)
    square = (SLOT * SIDE, images // PER * LANES)
    toeplitz = pltpu.VMEM((SLOT * SIDE, SLOT * SIDE), BF16)
    slots = pltpu.VMEM((groups, images * TILES * SLOT, LANES), F32)
    both_shape = (ch, 2, channels, tokens)
    given, taps = pl.pallas_call(
        forward_kernel,
        out_shape=(
            jax.ShapeDtypeStruct(both_shape, BF16),
            jax.ShapeDtypeStruct((groups * SLOT, LANES), F32),
        ),
        in_specs=[SMEM, SMEM] + [full] * 10,
        out_specs=(full, full),
        scratch_shapes=[
            slots, pltpu.VMEM((groups,) + toeplitz.shape, BF16),
            pltpu.VMEM((groups,) + toeplitz.shape, BF16), pltpu.VMEM((groups,) + square, BF16),
            pltpu.VMEM((groups,) + square, F32),
        ],
        compiler_params=params(16),
        cost_estimate=cost(6),
        name="mixer_forward",
    )(
        pin(heights), pin(widths), pin(features_after), pin(cotangent), pin(row(layer_scale)),
        pin(row(step_height)), pin(row(step_width)), pin(rate_height), pin(rate_width),
        pin(readout_height), pin(readout_width), pin(row(skip_gain)),
    )
    given, *shards = pair(given, *shards)
    given = swap(given)
    shard = jnp.concatenate(shards, axis=0)
    if near == 4:
        cut = far * tall_one // 2
        beside, above = pair(flip(shard, 1), flip(shard, 2))
        ends = pl.pallas_call(
            cut_kernel,
            out_shape=[jax.ShapeDtypeStruct((cut, width), BF16)] * 2,
            in_specs=[full] * 2,
            out_specs=[full] * 2,
            compiler_params=params(16),
            cost_estimate=pl.CostEstimate(flops=100_000_000_000, transcendentals=0, bytes_accessed=1_000_000),
            name="ends",
        )(beside, above)
        own = [shard, beside, above, flip(ends[0], 2), flip(ends[1], 1)]
        where = jnp.stack([place // near, place % near])
    else:
        own = [swap(jnp.broadcast_to(shard[None], (near,) + shard.shape), near_groups)]
        own = [own[0].reshape(ch * tall_one, width)]
        where = jnp.stack([place // near, place * 0])
    other = [exchange(piece) for piece in own]

    rows = ch * tall_one
    pieces = len(own)
    plane = jax.ShapeDtypeStruct((count, tokens), F32)
    token_low = jax.ShapeDtypeStruct((count, tokens), BF16)
    gother, *state = pl.pallas_call(
        partial(mlp_first, near, pieces, deep),
        out_shape=[
            jax.ShapeDtypeStruct((rows, width), BF16), token_low, token_low, plane,
            jax.ShapeDtypeStruct((1, tokens), F32), jax.ShapeDtypeStruct((count, LANES), F32),
            plane, plane,
        ],
        in_specs=[SMEM] + [full] * (1 + 2 * pieces),
        out_specs=[full] * 8,
        scratch_shapes=[pltpu.VMEM((ch * EDGE, LANES), F32)],
        compiler_params=params(16),
        cost_estimate=cost(5),
        name="mlp_first",
    )(where, given, *own, *other)
    arrived = exchange(gother)
    both, *gown = pl.pallas_call(
        partial(mlp_second, near, pieces, deep),
        out_shape=[jax.ShapeDtypeStruct(both_shape, BF16)]
        + [pltpu.HBM(own[0].shape, BF16)]
        + [jax.ShapeDtypeStruct(piece.shape, BF16) for piece in own[1:]],
        in_specs=[SMEM] + [full] * (7 + pieces),
        out_specs=[full] * (1 + pieces),
        scratch_shapes=[pltpu.VMEM((ch * EDGE, LANES), F32)],
        compiler_params=params(16),
        cost_estimate=cost(5),
        name="mlp_second",
    )(where, *state, *own)
    both = swap(both)
    tall = far * tall_one
    if near == 4:
        cut = tall // 2
        add = lambda v, at: (v.astype(F32) + arrived[at : at + v.shape[0]].astype(F32)).astype(BF16)
        one, two = pair(add(gown[3], 3 * tall), add(gown[4], 3 * tall + cut))
        one, two = pair(flip(one, 2), flip(two, 1))
        one, two = relay(gown[1], gown[2], arrived, one, two)
        features_last, first, one, two = pair(features, gown[0], one, two)
        landed = [*join(tall, [pin(first), arrived], 1), flip(one, 1), flip(two, 2)]
    else:
        features_last = features
        total = (gown[0].astype(F32) + arrived.astype(F32)).astype(BF16)
        sent = list(swap(total.reshape(near, tall, width), near_groups))
        landed = sent
    table = jax.ShapeDtypeStruct((groups,) + toeplitz.shape, BF16)
    strip = jax.ShapeDtypeStruct((groups, SLOT, images * SLOT, LANES), BF16)
    prepared = pl.pallas_call(
        prepare_kernel,
        out_shape=(
            jax.ShapeDtypeStruct((groups,) + square, BF16), table, table, strip, strip,
        ),
        in_specs=[SMEM, SMEM, full, full],
        out_specs=(full,) * 5,
        scratch_shapes=[slots, pltpu.VMEM(square, F32)],
        compiler_params=params(16),
        cost_estimate=cost(4),
        name="mixer_prepare",
    )(pin(heights), pin(widths), pin(features_last), taps)
    *landed, _ = pair(*landed, prepared[0])
    shards = join(tall_one, landed, far)
    shards = [shards[0]] + [flip(v, (i + 1) * near) for i, v in enumerate(shards[1:])]
    result, grad_features, small = pl.pallas_call(
        backward_kernel,
        out_shape=(
            jax.ShapeDtypeStruct((channels, cells), BF16),
            jax.ShapeDtypeStruct((channels, cells), F32),
            jax.ShapeDtypeStruct((channels, LANES + 4 * states), F32),
        ),
        in_specs=[SMEM, SMEM] + [full] * 17,
        out_specs=(full,) * 3,
        scratch_shapes=[
            slots, slots, pltpu.VMEM(square, BF16),
            pltpu.VMEM((SLOT * SIDE, SLOT * SIDE), F32), pltpu.VMEM(square, BF16),
            pltpu.VMEM(square, BF16), pltpu.VMEM(square, F32),
            pltpu.VMEM((groups * SLOT, LANES), F32),
        ],
        compiler_params=params(16),
        cost_estimate=cost(7),
        name="mixer_backward",
    )(
        pin(heights), pin(widths), pin(features), pin(cotangent), both, taps,
        pin(row(layer_scale)), pin(row(out_bias)), pin(row(step_height)), pin(row(step_width)),
        pin(rate_height), pin(rate_width), pin(readout_height), pin(readout_width),
        *prepared,
    )
    *shards, small = pair(*shards, small)
    (mine,) = join(tall_one, shards, 1)
    vector_out = jax.ShapeDtypeStruct((1, channels), F32)
    state_out = jax.ShapeDtypeStruct((channels, states), F32)
    weight_out = jax.ShapeDtypeStruct((units, count), F32)
    outs = pl.pallas_call(
        finish_kernel,
        out_shape=(
            vector_out, state_out, state_out, vector_out, state_out, state_out, vector_out,
            vector_out, vector_out, weight_out, jax.ShapeDtypeStruct((1, units), F32), weight_out,
            vector_out, vector_out,
        ),
        in_specs=[SMEM] + [full] * 4,
        out_specs=(full,) * 14,
        compiler_params=params(16),
        cost_estimate=cost(1),
        name="finish",
    )(half.reshape(1), mine, exchange(mine), small, exchange(small))
    outs = [v.reshape(-1) if v.shape[0] == 1 else v for v in outs]
    outs[9] = outs[9].T
    return (result, grad_features, *outs)


def solution(mesh):
    wide, split, tall = P("ch", "img"), P("ch"), P("ch", None)
    return jax.shard_map(
        partial(per_device, mesh.shape["ch"]),
        mesh=mesh,
        in_specs=(
            wide, wide, P("img"), P("img"), split, tall, tall, split, tall, tall, split, split,
            split, P(None, "ch"), split, tall, split, split,
        ),
        out_specs=(
            wide, wide, split, tall, tall, split, tall, tall, split, split, split,
            P(None, "ch"), split, tall, split, split,
        ),
        check_vma=False,
    )
```

```python
import math
from functools import partial

import jax
import jax.numpy as jnp
from jax import lax
from jax.experimental import pallas as pl
from jax.experimental.pallas import tpu as pltpu
from jax.sharding import PartitionSpec as P

SIDE = 32
CELLS = SIDE * SIDE
LANES = 128
PER = LANES // SIDE
SLOT = 8
EDGE = 16
TILES = CELLS // LANES
EPS = 1e-06
F32 = jnp.float32
BF16 = jnp.bfloat16


def column(row):
    n = row.shape[1]
    eye = lax.broadcasted_iota(jnp.int32, (n, n), 0) == lax.broadcasted_iota(jnp.int32, (n, n), 1)
    return jnp.sum(jnp.where(eye, jnp.broadcast_to(row, (n, n)), 0.0), axis=1, keepdims=True)


def as_row(col):
    n = col.shape[0]
    eye = lax.broadcasted_iota(jnp.int32, (n, n), 0) == lax.broadcasted_iota(jnp.int32, (n, n), 1)
    return jnp.sum(jnp.where(eye, jnp.broadcast_to(col, (n, n)), 0.0), axis=0, keepdims=True)


def image_mask(rows, height, width):
    cell = lax.broadcasted_iota(jnp.int32, (SLOT, CELLS), 1)
    inside = jnp.where((cell // SIDE < height) & (cell % SIDE < width), 1.0, 0.0)
    return jnp.concatenate([inside] * -(-rows // SLOT), axis=0)[:rows]


def lane_of(rows):
    return lax.broadcasted_iota(jnp.int32, (rows, LANES), 1)


def fill_slots(slots, value, image):
    channels = value.shape[0]
    for group in range(slots.shape[0]):
        live = min(SLOT, channels - group * SLOT)
        for k in range(TILES):
            at = (image * TILES + k) * SLOT
            part = value[group * SLOT : group * SLOT + live, k * LANES : (k + 1) * LANES]
            slots[group, pl.ds(at, live), :] = part


def read_slots(slots, image, channels):
    rows = []
    for group in range(slots.shape[0]):
        live = min(SLOT, channels - group * SLOT)
        at = [(image * TILES + k) * SLOT for k in range(TILES)]
        rows.append(jnp.concatenate([slots[group, pl.ds(a, live), :] for a in at], axis=1))
    return jnp.concatenate(rows, axis=0) if len(rows) > 1 else rows[0]


def cross(tiles, lane):
    for bit, far in ((2, 64), (1, 32)):
        low = (lane & far) == 0
        out = list(tiles)
        for k in range(len(tiles)):
            if not k & bit:
                one, two = tiles[k], tiles[k | bit]
                out[k] = jnp.where(low, one, pltpu.roll(two, far, 1))
                out[k | bit] = jnp.where(low, pltpu.roll(one, LANES - far, 1), two)
        tiles = out
    return tiles


def load_channel(slots, group, c, lane):
    count = slots.shape[1] // SLOT
    value = slots[group, pl.ds(c, count, stride=SLOT), :]
    return cross([value[k * SLOT : (k + 1) * SLOT] for k in range(count // SLOT)], lane)


def store_channel(slots, group, c, tiles, lane):
    count = slots.shape[1] // SLOT
    slots[group, pl.ds(c, count, stride=SLOT), :] = jnp.concatenate(cross(tiles, lane), axis=0)


def split(value):
    high = value.astype(BF16)
    return high, (value - high.astype(F32)).astype(BF16)


def pick(row, index):
    spread = jnp.broadcast_to(row, index.shape)
    value = jnp.take_along_axis(spread, jnp.clip(index, 0, LANES - 1), axis=1)
    return value


def build_down(row, c, high_ref, low_ref, lane, sub):
    place = lane % SIDE
    source = (place % TILES) * PER + place // TILES
    here = lane // SIDE == c % PER
    parts = []
    for turn in range(PER):
        index = PER * sub + turn - source
        parts.append(jnp.where(here & (index >= 0), pick(row, index), 0.0))
    high, low = split(jnp.concatenate(parts, axis=0))
    at = (slice(c * SIDE, (c + 1) * SIDE), slice(c // PER * LANES, (c // PER + 1) * LANES))
    high_ref[at] = high
    low_ref[at] = low


def build_across(row, turned, lane, sub):
    place = lane % SIDE
    highs, lows = [], []
    for part in range(PER):
        own = part * SLOT + sub
        index = own - place if turned else place - own
        value = jnp.where(index >= 0, pick(row, index + SIDE), 0.0)
        high = value.astype(BF16).astype(F32)
        highs.append(high)
        lows.append(value - high)
    spread = lambda parts: jnp.concatenate(
        [jnp.where(lane // SIDE == i, p, 0.0) for i in range(PER) for p in parts], axis=0
    ).astype(BF16)
    return spread(highs), spread(lows)


def taps_of(step_h, step_w, rate_h, rate_w, read_h, read_w, skip_ref):
    channels = rate_h.shape[0]
    lane = lane_of(channels)
    kept = jnp.zeros((channels, LANES), F32)
    decay_h = jnp.exp(column(step_h[...])) * rate_h[...]
    decay_w = jnp.exp(column(step_w[...])) * rate_w[...]
    for lag in range(SIDE):
        tap = jnp.sum(read_h[...] * jnp.exp(-decay_h * lag), axis=1, keepdims=True)
        kept = jnp.where(lane == lag, tap, kept)
        tap = jnp.sum(read_w[...] * jnp.exp(-decay_w * lag), axis=1, keepdims=True)
        kept = jnp.where(lane == SIDE + lag, tap, kept)
    return jnp.where(lane == 2 * SIDE, column(skip_ref[...]), kept)


def dot(a, b, dims=(((1,), (0,)), ((), ()))):
    return lax.dot_general(a, b, dims, preferred_element_type=F32)


NT = (((1,), (1,)), ((), ()))
TN = (((0,), (0,)), ((), ()))


def forward_kernel(
    heights, widths, feat_ref, cot_ref, scale_ref, step_h, step_w, rate_h, rate_w, read_h,
    read_w, skip_ref, out_ref, rows_ref, slots, high_a, low_a, field, tall,
):
    channels, cells = feat_ref.shape
    images = cells // CELLS
    rows_ref[0:channels] = taps_of(step_h, step_w, rate_h, rate_w, read_h, read_w, skip_ref)
    for ref in (high_a, low_a, field):
        ref[...] = jnp.zeros_like(ref)
    for image in range(images):
        inside = image_mask(channels, heights[image], widths[image])
        value = feat_ref[:, image * CELLS : (image + 1) * CELLS].astype(F32)
        fill_slots(slots, value * inside, image)
    live = min(SLOT, channels)
    sides = images // PER

    scratch = (high_a, low_a, field, tall)

    def body(group, carry):
        high_a, low_a, field, tall = (ref.at[group] for ref in scratch)
        lane = lane_of(SLOT)
        sub = lax.broadcasted_iota(jnp.int32, (SLOT, LANES), 0)
        for c in range(live):
            row = rows_ref[pl.ds(group * SLOT + c, 1), :]
            build_down(row, c, high_a, low_a, lane, sub)
            tiles = load_channel(slots, group, c, lane)
            for s in range(sides):
                value = jnp.concatenate(tiles[s * PER : (s + 1) * PER], axis=0)
                field[c * SIDE : (c + 1) * SIDE, s * LANES : (s + 1) * LANES] = value.astype(BF16)
        source = field[...]
        tall[...] = dot(high_a[...], source) + dot(low_a[...], source)
        for c in range(live):
            row = rows_ref[pl.ds(group * SLOT + c, 1), :]
            high_b, low_b = build_across(row, False, lane, sub)
            value = jnp.concatenate(
                [tall[c * SIDE : (c + 1) * SIDE, s * LANES : (s + 1) * LANES] for s in range(sides)],
                axis=0,
            )
            high, low = split(value)
            value = dot(
                jnp.concatenate([high, low, high], axis=1),
                jnp.concatenate([high_b, high_b, low_b], axis=0),
            )
            tiles = [value[k * SLOT : (k + 1) * SLOT] for k in range(images)]
            store_channel(slots, group, c, tiles, lane)
        return carry

    for group in range(slots.shape[0]):
        body(group, 0)
    wide = out_ref.shape[3]
    parts = CELLS // wide
    skip = rows_ref[0:channels, 2 * SIDE : 2 * SIDE + 1]
    scale = column(scale_ref[...])
    for image in range(images):
        span = slice(image * CELLS, (image + 1) * CELLS)
        inside = image_mask(channels, heights[image], widths[image])
        value = read_slots(slots, image, channels) + skip * feat_ref[:, span].astype(F32)
        value = (value * inside).astype(BF16)
        down = cot_ref[:, span].astype(F32) * scale
        down = (down * inside).astype(BF16)
        for j in range(parts):
            out_ref[image * parts + j, 0] = value[:, j * wide : (j + 1) * wide]
            out_ref[image * parts + j, 1] = down[:, j * wide : (j + 1) * wide]


def prepare_kernel(
    heights, widths, feat_ref, rows_ref, field_ref, high_a, low_a, high_s, low_s, slots, tall
):
    channels, cells = feat_ref.shape
    images = cells // CELLS
    live = min(SLOT, channels)
    sides = images // PER
    for ref in (field_ref, high_a, low_a):
        ref[...] = jnp.zeros_like(ref)
    for image in range(images):
        inside = image_mask(channels, heights[image], widths[image])
        value = feat_ref[:, image * CELLS : (image + 1) * CELLS].astype(F32)
        fill_slots(slots, value * inside, image)

    def body(group, carry):
        lane = lane_of(SLOT)
        sub = lax.broadcasted_iota(jnp.int32, (SLOT, LANES), 0)
        for c in range(live):
            row = rows_ref[pl.ds(group * SLOT + c, 1), :]
            build_down(row, c, high_a.at[group], low_a.at[group], lane, sub)
            tiles = load_channel(slots, group, c, lane)
            for s in range(sides):
                value = jnp.concatenate(tiles[s * PER : (s + 1) * PER], axis=0)
                at = (group, slice(c * SIDE, (c + 1) * SIDE), slice(s * LANES, (s + 1) * LANES))
                field_ref[at] = value.astype(BF16)
        source = field_ref[group]
        tall[...] = dot(high_a[group], source) + dot(low_a[group], source)
        for c in range(live):
            value = jnp.concatenate(
                [tall[c * SIDE : (c + 1) * SIDE, s * LANES : (s + 1) * LANES] for s in range(sides)],
                axis=0,
            )
            high, low = split(value)
            high_s[group, c] = high
            low_s[group, c] = low
        return carry

    lax.fori_loop(0, slots.shape[0], body, 0)


def backward_kernel(
    heights, widths, feat_ref, cot_ref, both_ref, rows_ref, scale_ref, bias_ref,
    step_h, step_w, rate_h, rate_w, read_h, read_w, field_ref, high_a, low_a, high_s, low_s,
    result_ref, gfeat_ref, small_ref, slots, slots_g, field_g, outer_ref, high_d, low_d, wide_ref, sums,
):
    channels, cells = feat_ref.shape
    images = cells // CELLS
    live = min(SLOT, channels)
    sides = images // PER
    wide = both_ref.shape[3]
    parts = CELLS // wide
    for ref in (sums, field_g, high_d, low_d):
        ref[...] = jnp.zeros_like(ref)
    lane_c = lane_of(channels)
    scale = column(scale_ref[...])
    bias = column(bias_ref[...])
    small = jnp.zeros((channels, LANES), F32)
    for image in range(images):
        span = slice(image * CELLS, (image + 1) * CELLS)
        inside = image_mask(channels, heights[image], widths[image])
        values = feat_ref[:, span].astype(F32)
        grad = jnp.concatenate(
            [both_ref[image * parts + j, 0].astype(F32) for j in range(parts)], axis=1
        )
        grad = grad * inside
        fill_slots(slots_g, grad, image)
        shifted = jnp.concatenate(
            [both_ref[image * parts + j, 1].astype(F32) for j in range(parts)], axis=1
        )
        shifted = shifted + bias
        result = values + inside * (scale * shifted)
        result_ref[:, span] = result.astype(BF16)
        weighted = cot_ref[:, span].astype(F32) * inside
        small = small + jnp.where(
            lane_c == 64,
            jnp.sum(grad * values, axis=1, keepdims=True),
            jnp.where(
                lane_c == 65,
                jnp.sum(weighted * shifted, axis=1, keepdims=True),
                jnp.where(lane_c == 66, scale * jnp.sum(weighted, axis=1, keepdims=True), 0.0),
            ),
        )

    def body(group, carry):
        lane = lane_of(SLOT)
        sub = lax.broadcasted_iota(jnp.int32, (SLOT, LANES), 0)
        place = lane % SIDE
        half = lambda ref, c, s: ref[c * SIDE : (c + 1) * SIDE, s * LANES : (s + 1) * LANES]
        stack = lambda ref, c: jnp.concatenate([half(ref, c, s) for s in range(sides)], axis=0)
        for c in range(live):
            tiles = load_channel(slots_g, group, c, lane)
            for s in range(sides):
                value = jnp.concatenate(tiles[s * PER : (s + 1) * PER], axis=0)
                at = (slice(c * SIDE, (c + 1) * SIDE), slice(s * LANES, (s + 1) * LANES))
                field_g[at] = value.astype(BF16)
        for c in range(live):
            row = rows_ref[pl.ds(group * SLOT + c, 1), :]
            high_b, low_b = build_across(row, True, lane, sub)
            grad = stack(field_g, c)
            flow = dot(
                jnp.concatenate([grad, grad], axis=1), jnp.concatenate([high_b, low_b], axis=0)
            )
            high, low = split(flow)
            for s in range(sides):
                at = (slice(c * SIDE, (c + 1) * SIDE), slice(s * LANES, (s + 1) * LANES))
                high_d[at] = high[s * SIDE : (s + 1) * SIDE]
                low_d[at] = low[s * SIDE : (s + 1) * SIDE]
            outer = dot(
                jnp.concatenate([grad, grad], axis=0),
                jnp.concatenate([high_s[group, c], low_s[group, c]], axis=0),
                TN,
            )
            total = None
            for part in range(PER):
                value = None
                for i in range(PER):
                    at = i * SIDE + part * SLOT
                    term = jnp.where(lane // SIDE == i, outer[at : at + SLOT], 0.0)
                    value = term if value is None else value + term
                index = part * SLOT + sub - place
                value = jnp.take_along_axis(
                    value, jnp.clip(index, 0, SIDE - 1) + lane // SIDE * SIDE, axis=1
                )
                value = jnp.where(index >= 0, value, 0.0)
                total = value if total is None else total + value
            total = jnp.sum(total, axis=0, keepdims=True)
            total = total + pltpu.roll(total, 64, 1)
            total = total + pltpu.roll(total, 32, 1)
            sums[pl.ds(group * SLOT + c, 1), :] = jnp.where(lane[0:1] // SIDE == 1, total, 0.0)
        high, low = high_d[...], low_d[...]
        down = high_a[group]
        back = dot(down, high, TN) + dot(down, low, TN) + dot(low_a[group], high, TN)
        wide_ref[...] = back
        source = field_ref[group]
        outer_ref[...] = dot(high, source, NT) + dot(low, source, NT)
        for c in range(live):
            value = stack(wide_ref, c)
            tiles = [value[k * SLOT : (k + 1) * SLOT] for k in range(images)]
            store_channel(slots, group, c, tiles, lane)
            total = None
            for turn in range(PER):
                at = c * SIDE + turn * SLOT
                value = outer_ref[at : at + SLOT, c // PER * LANES : (c // PER + 1) * LANES]
                index = PER * sub + turn - lane
                safe = jnp.clip(index, 0, SIDE - 1)
                index_at = (safe % PER) * TILES + safe // PER + c % PER * SIDE
                value = jnp.take_along_axis(value, index_at, axis=1)
                value = jnp.where(index >= 0, value, 0.0)
                total = value if total is None else total + value
            total = jnp.sum(total, axis=0, keepdims=True)
            total = jnp.where(lane[0:1] < SIDE, total, 0.0)
            sums[pl.ds(group * SLOT + c, 1), :] += total
        return carry

    lax.fori_loop(0, slots.shape[0], body, 0)
    skip = rows_ref[0:channels, 2 * SIDE : 2 * SIDE + 1]
    for image in range(images):
        span = slice(image * CELLS, (image + 1) * CELLS)
        inside = image_mask(channels, heights[image], widths[image])
        grad = read_slots(slots_g, image, channels)
        value = read_slots(slots, image, channels) + skip * grad
        gfeat_ref[:, span] = cot_ref[:, span].astype(F32) + value * inside
    small = small + sums[0:channels]
    states, small = chain(small, step_h, step_w, rate_h, rate_w, read_h, read_w)
    for index in range(2):
        pair = jnp.concatenate(states[2 * index : 2 * index + 2], axis=1)
        small_ref[:, index * pair.shape[1] : (index + 1) * pair.shape[1]] = pair
    small_ref[:, 2 * pair.shape[1] :] = small


def chain(total, step_h, step_w, rate_h, rate_w, read_h, read_w):
    out, tail = [], total
    lane = lane_of(total.shape[0])
    for place, first, step, rate, read in (
        (67, 0, step_h, rate_h, read_h), (68, SIDE, step_w, rate_w, read_w),
    ):
        pace = jnp.exp(column(step[...]))
        decay = pace * rate[...]
        to_read = jnp.zeros_like(decay)
        to_decay = jnp.zeros_like(decay)
        for lag in range(SIDE):
            term = total[:, first + lag : first + lag + 1] * jnp.exp(-decay * lag)
            to_read = to_read + term
            if lag:
                to_decay = to_decay - float(lag) * term
        to_decay = to_decay * read[...]
        out += [to_read, pace * to_decay]
        tail = jnp.where(lane == place, jnp.sum(to_decay * decay, axis=1, keepdims=True), tail)
    return out, tail


def stack_kernel(*refs):
    out = refs[-1]
    tall = refs[0].shape[0]
    for index, ref in enumerate(refs[:-1]):
        out[index * tall : (index + 1) * tall] = ref[...]


def join_kernel(count, *refs):
    given, outs = refs[:count], refs[count:]
    tall = outs[0].shape[0]
    for index, out in enumerate(outs):
        at = slice(index * tall, (index + 1) * tall)
        total = given[0][at].astype(F32)
        for ref in given[1:]:
            total = total + ref[at].astype(F32)
        out[...] = total.astype(out.dtype)


def cut_kernel(one_ref, two_ref, first_ref, second_ref):
    cut = first_ref.shape[0]
    first_ref[...] = one_ref[:cut]
    second_ref[...] = two_ref[cut:]


def start_kernel(one_ref, two_ref, arrived_ref, out_one, out_two):
    cut = one_ref.shape[0]
    at = arrived_ref.shape[0] - 2 * cut
    for start, ref, out in ((at, one_ref, out_one), (at + cut, two_ref, out_two)):
        total = ref[...].astype(F32) + arrived_ref[start : start + cut].astype(F32)
        out[...] = total.astype(BF16)


def relay_kernel(one_ref, two_ref, arrived_ref, first_ref, second_ref, out_one, out_two):
    tall = one_ref.shape[0]
    cut = tall // 2
    one = one_ref[...].astype(F32) + arrived_ref[tall : 2 * tall].astype(F32)
    two = two_ref[...].astype(F32) + arrived_ref[2 * tall : 3 * tall].astype(F32)
    out_one[:cut] = (one[:cut] + first_ref[...].astype(F32)).astype(BF16)
    out_one[cut:] = one[cut:].astype(BF16)
    out_two[:cut] = two[:cut].astype(BF16)
    out_two[cut:] = (two[cut:] + second_ref[...].astype(F32)).astype(BF16)


def finish_kernel(
    half, mine_ref, other_ref, small_ref, sibling_ref,
    gstep_h, grate_h, gread_h, gstep_w, grate_w, gread_w, gskip, ggain, gshift, gin, ginb, gout,
    gbias, gscale,
):
    units, count = gin.shape
    channels, states = grate_h.shape
    keep = units // 2
    deep = deep_of(mine_ref, count)
    first = half[0] == 0
    mine, other = mine_ref[...], other_ref[...]
    bias = []
    for at, part in ((0, jnp.where(first, mine, other)), (keep, jnp.where(first, other, mine))):
        for index in range(2 * count // LANES):
            out = gin if index < count // LANES else gout
            lanes = pl.ds(index * LANES % count, LANES)
            out[at : at + keep, lanes] = part[index * deep : index * deep + keep]
        bias.append(unfold(part[-EDGE:], 0, deep)[:keep])
    ginb[...] = as_row(jnp.concatenate(bias, axis=0))
    norms = mine[-EDGE:] + other[-EDGE:]
    ggain[...] = as_row(unfold(norms, 1, deep)[:channels])
    gshift[...] = as_row(unfold(norms, 2, deep)[:channels])
    total = small_ref[...] + sibling_ref[...]
    for index, ref in enumerate((gread_h, grate_h, gread_w, grate_w)):
        ref[...] = total[:, index * states : (index + 1) * states]
    total = total[:, 4 * states :]
    gskip[...] = as_row(total[:, 64:65])
    gscale[...] = as_row(total[:, 65:66])
    gbias[...] = as_row(total[:, 66:67])
    gstep_h[...] = as_row(total[:, 67:68])
    gstep_w[...] = as_row(total[:, 68:69])


def deep_of(ref, count, shards=1):
    return (ref.shape[0] // shards - EDGE) * LANES // (2 * count)


def fold(columns, deep):
    lane = lane_of(EDGE)
    pieces = deep // EDGE
    tile = jnp.zeros((EDGE, LANES), F32)
    for index, value in enumerate(columns):
        if value is not None:
            for p in range(pieces):
                part = value[p * EDGE : (p + 1) * EDGE]
                tile = jnp.where(lane == index * pieces + p, part, tile)
    return tile


def unfold(tile, index, deep):
    pieces = deep // EDGE
    first = index * pieces
    return jnp.concatenate([tile[:, first + p : first + p + 1] for p in range(pieces)], axis=0)


def pack_kernel(half, in_ref, out_ref, bias_ref, gain_ref, shift_ref, pack_ref):
    own, count = out_ref.shape
    deep = deep_of(pack_ref, count)
    channels = gain_ref.shape[1]
    keep = own // 2
    row = lax.broadcasted_iota(jnp.int32, (deep, own), 0)
    col = lax.broadcasted_iota(jnp.int32, (deep, own), 1)
    pick = jnp.where((col == row + half[0] * keep) & (row < keep), 1.0, 0.0).astype(BF16)
    first = dot(pick, in_ref[...]).astype(BF16)
    second = dot(pick, out_ref[...]).astype(BF16)
    bias = dot(pick, jnp.broadcast_to(bias_ref[...], (LANES, own)), NT)
    row = lax.broadcasted_iota(jnp.int32, (deep, channels), 0)
    col = lax.broadcasted_iota(jnp.int32, (deep, channels), 1)
    pick = jnp.where(col == row, 1.0, 0.0).astype(BF16)
    gain = dot(pick, jnp.broadcast_to(gain_ref[...], (LANES, channels)), NT)
    shift = dot(pick, jnp.broadcast_to(shift_ref[...], (LANES, channels)), NT)
    half_tiles = count // LANES
    for index in range(2 * half_tiles):
        source = first if index < half_tiles else second
        lanes = slice(index % half_tiles * LANES, (index % half_tiles + 1) * LANES)
        pack_ref[index * deep : (index + 1) * deep] = source[:, lanes]
    pack_ref[2 * half_tiles * deep :] = fold((bias, gain, shift), deep).astype(BF16)


ROOT = math.sqrt(2.0 / math.pi)


def shards_of(ref, count, deep):
    height = 2 * count // LANES * deep + EDGE
    return range(0, ref.shape[0], height)


def perceptron(refs, act, down, deep, sums_first):
    count = act.shape[0]
    tiles = count // LANES

    def matrix(first):
        rows = []
        for ref in refs:
            for base in shards_of(ref, count, deep):
                starts = [base + (first + j) * deep for j in range(tiles)]
                rows.append(jnp.concatenate([ref[at : at + deep] for at in starts], axis=1))
        return jnp.concatenate(rows, axis=0)

    bias = []
    for ref in refs:
        for base in shards_of(ref, count, deep):
            at = base + 2 * tiles * deep
            bias.append(unfold(ref[at : at + EDGE].astype(F32), 0, deep))
    w_in, w_out = matrix(0), matrix(tiles)
    v = dot(w_in, act) + jnp.concatenate(bias, axis=0)
    square = v * v
    half = 0.5 * jnp.tanh(v * (ROOT * 0.044715 * square + ROOT)) + 0.5
    full = v * half
    hidden = full.astype(BF16)
    slope = half + full * (1.0 - half) * (6.0 * ROOT * 0.044715 * square + 2.0 * ROOT)
    low = (dot(w_out, down) * slope).astype(BF16)
    g_bias = jnp.sum(low.astype(F32), axis=1, keepdims=True)
    if sums_first:
        sums, total = dot(w_out, hidden, TN), dot(w_in, low, TN)
    grads = (dot(low, act, NT).astype(BF16), dot(hidden, down, NT).astype(BF16), g_bias)
    if not sums_first:
        sums, total = dot(w_out, hidden, TN), dot(w_in, low, TN)
    return sums, total, grads


def put(ref, grads, start, deep, edges=None):
    count = grads[0].shape[1]
    tiles = count // LANES
    for base in shards_of(ref, count, deep):
        for index in range(2 * tiles):
            lanes = slice(index % tiles * LANES, (index % tiles + 1) * LANES)
            at = base + index * deep
            ref[at : at + deep] = grads[index // tiles][start : start + deep, lanes]
        edge = fold((grads[2][start : start + deep],), deep)
        if edges is None:
            at = base + 2 * tiles * deep
            ref[at : at + EDGE] = edge.astype(BF16)
        else:
            at = start // deep * EDGE
            edges[at : at + EDGE] = edge
        start += deep
    return start


def spots_of(near, devices, where_ref):
    z, xy = where_ref[0], where_ref[1]
    for d in range(devices):
        spot = ((d % near) ^ xy) * (devices // near) + ((d // near) ^ z)
        yield d, pl.multiple_of(spot * EDGE, EDGE)


def piece_of(rows, channels):
    return lax.broadcasted_iota(jnp.int32, (rows, LANES), 0) % channels // EDGE


def spread_of(tiles, index, channels, deep):
    piece = piece_of(tiles.shape[0], channels)[:, 0:1]
    first = index * (deep // EDGE)
    out = tiles[:, first : first + 1]
    for p in range(1, -(-channels // EDGE)):
        out = jnp.where(piece == p, tiles[:, first + p : first + p + 1], out)
    return out


def mlp_first(near, pieces, deep, where_ref, given_ref, *refs):
    own_in, refs = refs[:pieces], refs[pieces:]
    other_in, refs = refs[:pieces], refs[pieces:]
    gother_ref, active, downs, normal, inv_ref, gains, sum_ref, grad_ref, ext = refs
    devices, _, channels, _ = given_ref.shape
    count = active.shape[0]

    value = jnp.concatenate([given_ref[d, 0].astype(F32) for d in range(devices)], axis=0)
    mean = jnp.mean(value, axis=0, keepdims=True)
    value = value - mean
    inv = lax.rsqrt(jnp.mean(value * value, axis=0, keepdims=True) + EPS)
    value = value * inv
    normal[...] = value
    inv_ref[...] = inv
    down = jnp.concatenate([given_ref[d, 1].astype(F32) for d in range(devices)], axis=0)
    downs[...] = down.astype(BF16)
    at = 0
    for ref in own_in:
        for base in shards_of(ref, count, deep):
            edge = base + 2 * count // LANES * deep
            ext[at : at + EDGE] = ref[edge : edge + EDGE].astype(F32)
            at += EDGE
    for d, spot in spots_of(near, devices, where_ref):
        tile = ext[pl.ds(spot, EDGE), :]
        for at in range(0, channels, EDGE):
            rows = min(EDGE, channels - at)
            gains[d * channels + at : d * channels + at + rows] = tile[:rows]
    gain, shift = (spread_of(gains[...], index, channels, deep) for index in (1, 2))
    gains[...] = jnp.broadcast_to(gain, gains.shape)
    active[...] = (value * gain + shift).astype(BF16)
    sums, total, grads = perceptron(other_in, active[...], downs[...], deep, False)
    put(gother_ref, grads, 0, deep)
    sum_ref[...] = sums
    grad_ref[...] = total


def mlp_second(
    near, pieces, deep, where_ref, active, downs, normal_ref, inv_ref, gains, sum_ref, grad_ref,
    *refs,
):
    own_in, refs = refs[:pieces], refs[pieces:]
    both_ref, refs = refs[0], refs[1:]
    own_out, (gext,) = refs[:pieces], refs[pieces:]
    count = active.shape[0]
    devices, _, channels, _ = both_ref.shape

    sums, total, grads = perceptron(own_in, active[...], downs[...], deep, True)
    start = 0
    for ref in own_out:
        start = put(ref, grads, start, deep, gext)
    summed = sum_ref[...] + sums
    agrad = grad_ref[...] + total
    norm = normal_ref[...]
    scaled = agrad * gains[:, 0:1]
    first = jnp.mean(scaled, axis=0, keepdims=True)
    second = jnp.mean(scaled * norm, axis=0, keepdims=True)
    mgrad = (scaled - first - norm * second) * inv_ref[...]
    for d in range(devices):
        both_ref[d, 0] = mgrad[d * channels : (d + 1) * channels].astype(BF16)
        both_ref[d, 1] = summed[d * channels : (d + 1) * channels].astype(BF16)
    by_gain = jnp.sum(agrad * norm, axis=1, keepdims=True)
    by_shift = jnp.sum(agrad, axis=1, keepdims=True)
    lane, piece = lane_of(count), piece_of(count, channels)
    base = deep // EDGE
    tile = jnp.where(lane == base + piece, by_gain, 0.0)
    tile = jnp.where(lane == 2 * base + piece, by_shift, tile)
    for d, spot in spots_of(near, devices, where_ref):
        edge = None
        for at in range(0, channels, EDGE):
            rows = min(EDGE, channels - at)
            part = tile[d * channels + at : d * channels + at + rows]
            if rows < EDGE:
                part = jnp.concatenate([part, jnp.zeros((EDGE - rows, LANES), F32)], axis=0)
            edge = part if edge is None else edge + part
        gext[pl.ds(spot, EDGE), :] += edge
    at = 0
    for ref in own_out:
        for base in shards_of(ref, count, deep):
            edge = base + 2 * count // LANES * deep
            ref[edge : edge + EDGE] = gext[at : at + EDGE].astype(BF16)
            at += EDGE


def whole(shape):
    return pl.BlockSpec(shape, lambda i: (0,) * len(shape))


def params(mebibytes):
    return pltpu.CompilerParams(vmem_limit_bytes=mebibytes << 20)


def cost(micros):
    return pl.CostEstimate(flops=0, transcendentals=0, bytes_accessed=micros * 3_000_000)


def join(deep, arrays, count):
    full = pl.BlockSpec(memory_space=pltpu.VMEM)
    width = arrays[0].shape[1]
    return pl.pallas_call(
        partial(join_kernel, len(arrays)),
        out_shape=[
            pltpu.VMEM((deep, width), BF16 if i else F32) for i in range(count)
        ],
        in_specs=[full] * len(arrays),
        out_specs=[full] * count,
        compiler_params=params(16),
        cost_estimate=pl.CostEstimate(flops=1 if count > 1 else 1, transcendentals=0, bytes_accessed=1_000_000),
        name="join",
    )(*arrays)


def relay(*arrays):
    full = pl.BlockSpec(memory_space=pltpu.VMEM)
    shape = pltpu.VMEM(arrays[0].shape, BF16)
    return pl.pallas_call(
        relay_kernel,
        out_shape=(shape, shape),
        in_specs=[full] * 5,
        out_specs=(full, full),
        compiler_params=params(16),
        cost_estimate=pl.CostEstimate(flops=100_000_000_000, transcendentals=0, bytes_accessed=1_000_000),
        name="relay",
    )(*arrays)


SMEM = pl.BlockSpec(memory_space=pltpu.SMEM)


def per_device(
    ch, features, cotangent, heights, widths, step_height, rate_height, readout_height,
    step_width, rate_width, readout_width, skip_gain, norm_gain, norm_shift, in_weight,
    in_bias, out_weight, out_bias, layer_scale,
):
    channels, cells = features.shape
    count = in_weight.shape[0]
    pin = lambda v: pltpu.with_memory_space_constraint(v, pltpu.HBM)
    units = in_weight.shape[1]
    states = rate_height.shape[1]
    images = cells // CELLS
    tokens = cells // ch
    parts = CELLS // tokens
    far = 4
    near = ch // far
    deep = -(-(units // 2) // 16) * 16
    tall_one = 2 * count // LANES * deep + EDGE
    width = LANES
    near_groups = [[f * near + i for i in range(near)] for f in range(far)]
    row = lambda v: v.reshape(1, -1)
    exchange = lambda v: lax.ppermute(v, "img", [(0, 1), (1, 0)])
    flip = lambda v, bits: lax.ppermute(v, "ch", [(i, i ^ bits) for i in range(ch)])
    swap = lambda v, groups=None: lax.all_to_all(
        v, "ch", split_axis=0, concat_axis=0, tiled=True, axis_index_groups=groups
    )
    pair = lambda *arrays: lax.optimization_barrier(arrays)
    half = lax.axis_index("img").astype(jnp.int32)
    place = lax.axis_index("ch").astype(jnp.int32)
    full = pl.BlockSpec(memory_space=pltpu.VMEM)

    pack = pl.pallas_call(
        pack_kernel,
        out_shape=jax.ShapeDtypeStruct((tall_one, width), BF16),
        in_specs=[SMEM] + [full] * 5,
        out_specs=full,
        compiler_params=params(16),
        cost_estimate=cost(2),
        name="pack",
    )(
        half.reshape(1), pin(in_weight.T), pin(out_weight), pin(row(in_bias)), pin(row(norm_gain)),
        pin(row(norm_shift)),
    )
    pack, features_after = pair(pack, features)
    shards = [flip(pack, bits * near) for bits in range(far - 1, 0, -1)]
    shards = [pack] + shards[::-1]

    groups = -(-channels // SLOT)
    square = (SLOT * SIDE, images // PER * LANES)
    toeplitz = pltpu.VMEM((SLOT * SIDE, SLOT * SIDE), BF16)
    slots = pltpu.VMEM((groups, images * TILES * SLOT, LANES), F32)
    both_shape = (ch, 2, channels, tokens)
    given, taps = pl.pallas_call(
        forward_kernel,
        out_shape=(
            jax.ShapeDtypeStruct(both_shape, BF16),
            jax.ShapeDtypeStruct((groups * SLOT, LANES), F32),
        ),
        in_specs=[SMEM, SMEM] + [full] * 10,
        out_specs=(full, full),
        scratch_shapes=[
            slots, pltpu.VMEM((groups,) + toeplitz.shape, BF16),
            pltpu.VMEM((groups,) + toeplitz.shape, BF16), pltpu.VMEM((groups,) + square, BF16),
            pltpu.VMEM((groups,) + square, F32),
        ],
        compiler_params=params(16),
        cost_estimate=cost(6),
        name="mixer_forward",
    )(
        pin(heights), pin(widths), pin(features_after), pin(cotangent), pin(row(layer_scale)),
        pin(row(step_height)), pin(row(step_width)), pin(rate_height), pin(rate_width),
        pin(readout_height), pin(readout_width), pin(row(skip_gain)),
    )
    given, *shards = pair(given, *shards)
    given = swap(given)
    shard = pl.pallas_call(
        stack_kernel,
        out_shape=pltpu.VMEM((far * tall_one, width), BF16),
        in_specs=[full] * far,
        out_specs=full,
        compiler_params=params(16),
        cost_estimate=cost(1),
        name="stack",
    )(*shards)
    if near == 4:
        cut = far * tall_one // 2
        beside, above = pair(flip(shard, 1), flip(shard, 2))
        ends = pl.pallas_call(
            cut_kernel,
            out_shape=[jax.ShapeDtypeStruct((cut, width), BF16)] * 2,
            in_specs=[full] * 2,
            out_specs=[full] * 2,
            compiler_params=params(16),
            cost_estimate=pl.CostEstimate(flops=100_000_000_000, transcendentals=0, bytes_accessed=1_000_000),
            name="ends",
        )(beside, above)
        own = [shard, beside, above, flip(ends[0], 2), flip(ends[1], 1)]
        where = jnp.stack([place // near, place % near])
    else:
        own = [swap(jnp.broadcast_to(shard[None], (near,) + shard.shape), near_groups)]
        own = [own[0].reshape(ch * tall_one, width)]
        where = jnp.stack([place // near, place * 0])
    other = [exchange(piece) for piece in own]

    rows = ch * tall_one
    pieces = len(own)
    plane = jax.ShapeDtypeStruct((count, tokens), F32)
    token_low = jax.ShapeDtypeStruct((count, tokens), BF16)
    gother, *state = pl.pallas_call(
        partial(mlp_first, near, pieces, deep),
        out_shape=[
            jax.ShapeDtypeStruct((rows, width), BF16), token_low, token_low, plane,
            jax.ShapeDtypeStruct((1, tokens), F32), jax.ShapeDtypeStruct((count, LANES), F32),
            plane, plane,
        ],
        in_specs=[SMEM] + [full] * (1 + 2 * pieces),
        out_specs=[full] * 8,
        scratch_shapes=[pltpu.VMEM((ch * EDGE, LANES), F32)],
        compiler_params=params(16),
        cost_estimate=cost(5),
        name="mlp_first",
    )(where, given, *own, *other)
    arrived = exchange(gother)
    both, *gown = pl.pallas_call(
        partial(mlp_second, near, pieces, deep),
        out_shape=[jax.ShapeDtypeStruct(both_shape, BF16)]
        + [pltpu.HBM(own[0].shape, BF16)]
        + [jax.ShapeDtypeStruct(piece.shape, BF16) for piece in own[1:]],
        in_specs=[SMEM] + [full] * (7 + pieces),
        out_specs=[full] * (1 + pieces),
        scratch_shapes=[pltpu.VMEM((ch * EDGE, LANES), F32)],
        compiler_params=params(16),
        cost_estimate=cost(5),
        name="mlp_second",
    )(where, *state, *own)
    both = swap(both)
    tall = far * tall_one
    if near == 4:
        cut = tall // 2
        add = lambda v, at: (v.astype(F32) + arrived[at : at + v.shape[0]].astype(F32)).astype(BF16)
        one, two = pair(add(gown[3], 3 * tall), add(gown[4], 3 * tall + cut))
        one, two = pair(flip(one, 2), flip(two, 1))
        one, two = relay(gown[1], gown[2], arrived, one, two)
        features_last, first, one, two = pair(features, gown[0], one, two)
        landed = [*join(tall, [pin(first), arrived], 1), flip(one, 1), flip(two, 2)]
    else:
        features_last = features
        total = (gown[0].astype(F32) + arrived.astype(F32)).astype(BF16)
        sent = list(swap(total.reshape(near, tall, width), near_groups))
        landed = sent
    table = jax.ShapeDtypeStruct((groups,) + toeplitz.shape, BF16)
    strip = jax.ShapeDtypeStruct((groups, SLOT, images * SLOT, LANES), BF16)
    prepared = pl.pallas_call(
        prepare_kernel,
        out_shape=(
            jax.ShapeDtypeStruct((groups,) + square, BF16), table, table, strip, strip,
        ),
        in_specs=[SMEM, SMEM, full, full],
        out_specs=(full,) * 5,
        scratch_shapes=[slots, pltpu.VMEM(square, F32)],
        compiler_params=params(16),
        cost_estimate=cost(4),
        name="mixer_prepare",
    )(pin(heights), pin(widths), pin(features_last), taps)
    *landed, _ = pair(*landed, prepared[0])
    shards = join(tall_one, landed, far)
    shards = [shards[0]] + [flip(v, (i + 1) * near) for i, v in enumerate(shards[1:])]
    result, grad_features, small = pl.pallas_call(
        backward_kernel,
        out_shape=(
            jax.ShapeDtypeStruct((channels, cells), BF16),
            jax.ShapeDtypeStruct((channels, cells), F32),
            jax.ShapeDtypeStruct((channels, LANES + 4 * states), F32),
        ),
        in_specs=[SMEM, SMEM] + [full] * 17,
        out_specs=(full,) * 3,
        scratch_shapes=[
            slots, slots, pltpu.VMEM(square, BF16),
            pltpu.VMEM((SLOT * SIDE, SLOT * SIDE), F32), pltpu.VMEM(square, BF16),
            pltpu.VMEM(square, BF16), pltpu.VMEM(square, F32),
            pltpu.VMEM((groups * SLOT, LANES), F32),
        ],
        compiler_params=params(16),
        cost_estimate=cost(7),
        name="mixer_backward",
    )(
        pin(heights), pin(widths), pin(features), pin(cotangent), both, taps,
        pin(row(layer_scale)), pin(row(out_bias)), pin(row(step_height)), pin(row(step_width)),
        pin(rate_height), pin(rate_width), pin(readout_height), pin(readout_width),
        *prepared,
    )
    *shards, small = pair(*shards, small)
    (mine,) = join(tall_one, shards, 1)
    vector_out = jax.ShapeDtypeStruct((1, channels), F32)
    state_out = jax.ShapeDtypeStruct((channels, states), F32)
    weight_out = jax.ShapeDtypeStruct((units, count), F32)
    outs = pl.pallas_call(
        finish_kernel,
        out_shape=(
            vector_out, state_out, state_out, vector_out, state_out, state_out, vector_out,
            vector_out, vector_out, weight_out, jax.ShapeDtypeStruct((1, units), F32), weight_out,
            vector_out, vector_out,
        ),
        in_specs=[SMEM] + [full] * 4,
        out_specs=(full,) * 14,
        compiler_params=params(16),
        cost_estimate=cost(1),
        name="finish",
    )(half.reshape(1), mine, exchange(mine), small, exchange(small))
    outs = [v.reshape(-1) if v.shape[0] == 1 else v for v in outs]
    outs[9] = outs[9].T
    return (result, grad_features, *outs)


def solution(mesh):
    wide, split, tall = P("ch", "img"), P("ch"), P("ch", None)
    return jax.shard_map(
        partial(per_device, mesh.shape["ch"]),
        mesh=mesh,
        in_specs=(
            wide, wide, P("img"), P("img"), split, tall, tall, split, tall, tall, split, split,
            split, P(None, "ch"), split, tall, split, split,
        ),
        out_specs=(
            wide, wide, split, tall, tall, split, tall, tall, split, split, split,
            P(None, "ch"), split, tall, split, split,
        ),
        check_vma=False,
    )
```
